256 devices in a mesh: cells: 64 (over z, x, core), views: 4 (over y).
Axes of the slice: x: 4, y: 4, z: 8, core: 2. Of those that a mesh axis runs over, the one named last changes fastest.
Arguments:
- params: float32 [59, 131072], P(None, 'cells'), may hold values from -5 to 4, as said below
- first_moment: float32 [59, 131072], P(None, 'cells'), may hold values from -0.6 to 0.6
- second_moment: float32 [59, 131072], P(None, 'cells'), may hold values from 1e-12 to 0.05
- cameras: float32 [4, 6], P('views'), may hold values from -0.004 to 0.004
- visible: int32 [4, 131072], P('views', 'cells'), may hold values from 0 to 1, as said below
- send_plan: int32 [4, 64, 64, 32], P('views', 'cells'), may hold values from -1 to 2047, as said below
- tile_lists: int32 [4, 256, 512], P('views', 'cells'), may hold values from -1 to 2047, as said below
- target: float32 [4, 3, 65536], P('views', None, 'cells'), may hold values from 0 to 1
Outputs:
- updated_params: float32 [59, 131072], P(None, 'cells')
- updated_first: float32 [59, 131072], P(None, 'cells')
- updated_second: float32 [59, 131072], P(None, 'cells')
The draws below stay inside these ranges and needn't reach their ends.
Inputs may be any that keep to these rules, and one draw needn't show every extreme that they name: `params`: rows 0 to 2 hold a Gaussian's mean, 3 to 5 the logarithms of its scales, 6 to 9 a rotation quaternion whose first component is at least 0.6, 10 its opacity logit, 11 to 58 its spherical-harmonic coefficients; every Gaussian lies at depth 2 or more before every camera. In each view, between a quarter and three quarters of each owner's block of 2048 Gaussians are visible. Every row of an owner's block of 2048 Gaussians belongs to exactly one rendering device, 32 rows to each device; send_plan[v, s, d, :] lists exactly the rows of owner s that belong to device d and are visible in view v, live entries first, then -1; in every view some device receives 32 rows from every owner. `tile_lists`: tile t is rendered on device t // 4; an entry e stands for send_plan[v, e // 32, t // 4, e % 32], which is live; live entries come first, ordered by increasing params[2] of their Gaussians, then -1; some tile of each view has 512 live entries.
All inputs are finite; a program needn't handle non-finite values.
Results may differ from the reference program's by a relative error of at most 0.0003.
Values sent between devices are 32-bit elements; how exact they have to be, the bound alone decides.
No kernel may reach another device: no remote copies, remote signals or barrier semaphores. Data moves between devices by JAX's collectives and lax.ppermute only.
A program may use at most 64 MiB of HBM per device.

```python
import jax
import jax.numpy as jnp
from jax import lax

G_DEV = 2048
TILES_DEV = 4
L = 512
TILE_COLS = 32
ADAM_STEP = 1000
CAP = 32
VIEWS = 4
OWNERS = 64
GAUSSIANS = 131072
TILES = 256
N_CELLS = 64
N_VIEWS = 4


def draw_scene(key):
    block_cols = TILE_COLS // 4
    block_high = 4 * TILES_DEV
    hot_rows = (L + OWNERS - 1) // OWNERS
    widest = min(27, (block_high - 1) // 2)
    reach_span = widest - 5
    shape_rows = (OWNERS, G_DEV)
    local_ids = jnp.arange(G_DEV, dtype=jnp.int32)
    placement = jnp.argsort(jax.random.randint(jax.random.fold_in(key, 301), shape_rows, 0, 4096) * G_DEV + local_ids[None, :], axis=-1).astype(jnp.int32)
    home_owner = placement // CAP
    within = placement % CAP
    edge_splat = (within == CAP - 1) & (within >= hot_rows) & (home_owner < block_cols)
    hot_tile = jax.random.randint(jax.random.fold_in(key, 302), (OWNERS,), 0, TILES_DEV)
    random_tile = jax.random.randint(jax.random.fold_in(key, 303), shape_rows, 0, TILES_DEV)
    aim_tile = jnp.where(within < hot_rows, hot_tile[home_owner], random_tile)
    aim_across = 16 * (aim_tile % 4) + jax.random.randint(jax.random.fold_in(key, 304), shape_rows, 0, 16)
    aim_down = 16 * (aim_tile // 4) + jax.random.randint(jax.random.fold_in(key, 305), shape_rows, 0, 16)
    reach = 6 + jnp.minimum(jax.random.randint(jax.random.fold_in(key, 306), shape_rows, 0, reach_span), jax.random.randint(jax.random.fold_in(key, 307), shape_rows, 0, reach_span))
    centre_across = jnp.clip(aim_across, reach, 63 - reach)
    centre_down = jnp.clip(aim_down, reach, block_high - 1 - reach)
    first_col = jnp.where(edge_splat, (aim_across - 28) // 16, (centre_across - reach) // 16)
    last_col = jnp.where(edge_splat, (aim_across + 28) // 16, (centre_across + reach) // 16)
    first_row = jnp.where(edge_splat, 0, (centre_down - reach) // 16)
    last_row = jnp.where(edge_splat, 0, (centre_down + reach) // 16)
    pixel_across = 64 * (home_owner % block_cols) + jnp.where(edge_splat, aim_across, centre_across)
    pixel_down = jnp.where(edge_splat, -48, block_high * (home_owner // block_cols) + centre_down)
    depth_keys = jax.random.randint(jax.random.fold_in(key, 308), (GAUSSIANS,), 0, 1024) * GAUSSIANS + jnp.arange(GAUSSIANS, dtype=jnp.int32)
    depth_rank = jnp.argsort(depth_keys).astype(jnp.int32).reshape(OWNERS, G_DEV)
    front_owner = jax.random.randint(jax.random.fold_in(key, 309), (VIEWS, 1, 1), 0, OWNERS)
    drawn = jax.random.randint(jax.random.fold_in(key, 310), (VIEWS, OWNERS, 1), G_DEV // 4, 3 * G_DEV // 4 + 1)
    noise = jax.random.randint(jax.random.fold_in(key, 311), (VIEWS, OWNERS, G_DEV), 0, 1024)
    scores = jnp.where(home_owner[None] == front_owner, 0, 1024 * G_DEV) + noise * G_DEV + local_ids[None, None, :]
    ranks = jnp.argsort(jnp.argsort(scores, axis=-1), axis=-1)
    seen = ranks < drawn
    visible = seen.astype(jnp.int32).reshape(VIEWS, GAUSSIANS)
    home_rows = jnp.argsort(placement, axis=-1).astype(jnp.int32)
    seen_home = jnp.take_along_axis(seen, jnp.broadcast_to(home_rows[None], (VIEWS, OWNERS, G_DEV)), axis=2).reshape(VIEWS, OWNERS, OWNERS, CAP)
    rows_home = jnp.broadcast_to(home_rows.reshape(1, OWNERS, OWNERS, CAP), (VIEWS, OWNERS, OWNERS, CAP))
    slot_ids = jnp.arange(CAP, dtype=jnp.int32)
    compact = jnp.argsort(jnp.where(seen_home, slot_ids, CAP + slot_ids), axis=-1)
    plan = jnp.where(jnp.take_along_axis(seen_home, compact, axis=3), jnp.take_along_axis(rows_home, compact, axis=3), -1).astype(jnp.int32)
    safe_rows = jnp.maximum(plan, 0)
    sources = jnp.arange(OWNERS, dtype=jnp.int32)[None, :, None, None]

    def per_slot(table):
        return jnp.transpose(table[sources, safe_rows], (0, 2, 1, 3)).reshape(VIEWS, OWNERS, 1, OWNERS * CAP)
    live = jnp.transpose(plan >= 0, (0, 2, 1, 3)).reshape(VIEWS, OWNERS, 1, OWNERS * CAP)
    tile_local = jnp.arange(TILES_DEV, dtype=jnp.int32)[None, None, :, None]
    tile_across = tile_local % 4
    tile_down = tile_local // 4
    meets = live & (per_slot(first_col) <= tile_across) & (per_slot(last_col) >= tile_across) & (per_slot(first_row) <= tile_down) & (per_slot(last_row) >= tile_down)
    slot_all = jnp.arange(OWNERS * CAP, dtype=jnp.int32)
    edge_ints = edge_splat.astype(jnp.int32)
    sort_key = jnp.where(meets, per_slot(depth_rank) + GAUSSIANS * (1 - per_slot(edge_ints)), 2 * GAUSSIANS + slot_all)
    order = jnp.argsort(sort_key, axis=-1)[..., :L].astype(jnp.int32)
    best = jnp.take_along_axis(sort_key, order, axis=-1)
    lists = jnp.where(best < 2 * GAUSSIANS, order, -1).astype(jnp.int32).reshape(VIEWS, OWNERS * TILES_DEV, L)
    return (visible, plan, lists, pixel_across, pixel_down, reach, depth_rank, edge_ints)


def draw_visible(key, part):
    return draw_scene(key)[0]


def draw_send_plan(key, part):
    return draw_scene(key)[1]


def draw_tile_lists(key, part):
    return draw_scene(key)[2]


def draw_params(key, part):
    scene = draw_scene(key)
    half_width = TILE_COLS * 8.0
    rows_pix = TILES // TILE_COLS * 16
    edge_splat = scene[7].reshape(GAUSSIANS) > 0
    rank_part = (scene[6].reshape(GAUSSIANS).astype(jnp.float32) + 0.5) / GAUSSIANS
    across = (scene[3].reshape(GAUSSIANS).astype(jnp.float32) + 0.5 - half_width) / half_width
    down = (scene[4].reshape(GAUSSIANS).astype(jnp.float32) + 0.5 - rows_pix * 0.5) / half_width
    depth = jnp.where(edge_splat, 2.05 + 0.4 * rank_part, 2.5 + 1.5 * rank_part)
    sigma_pix = (scene[5].reshape(GAUSSIANS).astype(jnp.float32) - 3.0) / 3.0
    jitter = jax.random.uniform(jax.random.fold_in(key, 201), (3, GAUSSIANS), jnp.float32, -0.15, 0.15)
    drawn_scale = jnp.log(sigma_pix * depth / half_width)[None, :] + jitter
    edge_scale = jnp.log(48.0 / half_width * depth / (5.4 * jnp.sqrt(1.0 + down * down)))
    log_scale = jnp.where(edge_splat[None, :], jnp.broadcast_to(edge_scale[None, :], (3, GAUSSIANS)), drawn_scale)
    quat_first = jax.random.uniform(jax.random.fold_in(key, 204), (1, GAUSSIANS), jnp.float32, 0.6, 1.2)
    quat_rest = jax.random.uniform(jax.random.fold_in(key, 205), (3, GAUSSIANS), jnp.float32, -1.0, 1.0)
    logit = jax.random.uniform(jax.random.fold_in(key, 206), (1, GAUSSIANS), jnp.float32, -3.5, -1.0)
    constant_part = jax.random.uniform(jax.random.fold_in(key, 207), (3, GAUSSIANS), jnp.float32, -1.5, 1.5)
    higher = jnp.clip(0.3 * jax.random.normal(jax.random.fold_in(key, 208), (45, GAUSSIANS), jnp.float32), -1.5, 1.5)
    edge_logit = jax.random.uniform(jax.random.fold_in(key, 211), (1, GAUSSIANS), jnp.float32, -1.5, -1.0)
    logit = jnp.where(edge_splat[None, :], edge_logit, logit)
    means = jnp.stack([across * depth, down * depth, depth])
    return jnp.concatenate([means, log_scale, quat_first, quat_rest, logit, constant_part, higher], axis=0)


def draw_moments(key):
    edge_splat = draw_scene(key)[7].reshape(GAUSSIANS) > 0
    faint_second = jnp.exp(jax.random.uniform(jax.random.fold_in(key, 402), (59, GAUSSIANS), jnp.float32, -27.631021, -25.328436))
    drawn_second = jnp.exp(jax.random.uniform(jax.random.fold_in(key, 403), (59, GAUSSIANS), jnp.float32, -6.9077553, -2.9957323))
    second = jnp.where(edge_splat[None, :], faint_second, drawn_second)
    drawn_first = jnp.clip(0.1 * jax.random.normal(jax.random.fold_in(key, 404), (59, GAUSSIANS), jnp.float32), -0.6, 0.6)
    faint_first = 0.3 * jnp.sqrt(faint_second) * jnp.clip(jax.random.normal(jax.random.fold_in(key, 405), (59, GAUSSIANS), jnp.float32), -2.0, 2.0)
    first = jnp.where(edge_splat[None, :], faint_first, drawn_first)
    return (first, second)


def draw_first_moment(key, part):
    return draw_moments(key)[0]


def draw_second_moment(key, part):
    return draw_moments(key)[1]


def levels(stream_key, extent, cuts, least, largest):
    level = 1.0
    for position, blocks in cuts:
        draws = jax.random.uniform(jax.random.fold_in(jax.random.fold_in(stream_key, 6), position), (blocks,), jnp.float32, least / len(cuts), largest / len(cuts))
        level = level * jnp.repeat(jnp.exp(draws), extent[position] // blocks).reshape((-1,) + (1,) * (len(extent) - 1 - position))
    return level


def setup_inputs(seed: int = 0) -> dict:
    keys = jax.random.split(jax.random.key(seed), 9)
    params = draw_params(jax.random.fold_in(keys[8], 71), 0)
    first_moment = draw_first_moment(jax.random.fold_in(keys[8], 71), 0)
    second_moment = draw_second_moment(jax.random.fold_in(keys[8], 71), 0)
    cameras = jnp.clip(jax.random.uniform(keys[3], (VIEWS, 6), jnp.float32, -0.004, 0.004) * levels(keys[3], (VIEWS, 6), ((0, 4),), -0.4, 0.0), -0.004, 0.004)
    visible = draw_visible(jax.random.fold_in(keys[8], 71), 0)
    send_plan = draw_send_plan(jax.random.fold_in(keys[8], 71), 0)
    tile_lists = draw_tile_lists(jax.random.fold_in(keys[8], 71), 0)
    target = jnp.clip(1.0 * jax.random.uniform(keys[7], (VIEWS, 3, TILES * 256), jnp.float32) ** levels(keys[7], (VIEWS, 3, TILES * 256), ((0, 4), (2, 64)), -0.2, 0.2), 0.0, 1.0)
    return {"params": params, "first_moment": first_moment, "second_moment": second_moment, "cameras": cameras, "visible": visible, "send_plan": send_plan, "tile_lists": tile_lists, "target": target}


harmonic_zero = 0.28209479177387814
harmonic_one = 0.4886025119029199
harmonic_two = (1.0925484305920792, -1.0925484305920792, 0.31539156525252005, -1.0925484305920792, 0.5462742152960396)
harmonic_three = (-0.5900435899266435, 2.890611442640554, -0.4570457994644658, 0.3731763325901154, -0.4570457994644658, 1.445305721320277, -0.5900435899266435)

def harmonics(across, upward, onward):
    across_sq = across * across
    upward_sq = upward * upward
    onward_sq = onward * onward
    return jnp.stack([harmonic_zero * jnp.ones_like(across), -harmonic_one * upward, harmonic_one * onward, -harmonic_one * across, harmonic_two[0] * across * upward, harmonic_two[1] * upward * onward, harmonic_two[2] * (2.0 * onward_sq - across_sq - upward_sq), harmonic_two[3] * across * onward, harmonic_two[4] * (across_sq - upward_sq), harmonic_three[0] * upward * (3.0 * across_sq - upward_sq), harmonic_three[1] * across * upward * onward, harmonic_three[2] * upward * (4.0 * onward_sq - across_sq - upward_sq), harmonic_three[3] * onward * (2.0 * onward_sq - 3.0 * across_sq - 3.0 * upward_sq), harmonic_three[4] * across * (4.0 * onward_sq - across_sq - upward_sq), harmonic_three[5] * onward * (across_sq - upward_sq), harmonic_three[6] * across * (across_sq - 3.0 * upward_sq)])

def camera_rotation(angles):
    cos_roll, sin_roll = (jnp.cos(angles[0]), jnp.sin(angles[0]))
    cos_pitch, sin_pitch = (jnp.cos(angles[1]), jnp.sin(angles[1]))
    cos_yaw, sin_yaw = (jnp.cos(angles[2]), jnp.sin(angles[2]))
    naught = jnp.zeros_like(cos_roll)
    unit_one = jnp.ones_like(cos_roll)
    roll = jnp.stack([jnp.stack([unit_one, naught, naught]), jnp.stack([naught, cos_roll, -sin_roll]), jnp.stack([naught, sin_roll, cos_roll])])
    pitch = jnp.stack([jnp.stack([cos_pitch, naught, sin_pitch]), jnp.stack([naught, unit_one, naught]), jnp.stack([-sin_pitch, naught, cos_pitch])])
    yawing = jnp.stack([jnp.stack([cos_yaw, -sin_yaw, naught]), jnp.stack([sin_yaw, cos_yaw, naught]), jnp.stack([naught, naught, unit_one])])
    inner_turn = jnp.dot(pitch, roll, precision=lax.Precision.HIGHEST)
    return jnp.dot(yawing, inner_turn, precision=lax.Precision.HIGHEST)

def project(values, camera):
    turn = camera_rotation(camera[0:3])
    offset = values[0:3] - camera[3:6][:, None]
    in_view = jnp.dot(turn, offset, precision=lax.Precision.HIGHEST)
    inv_depth = 1.0 / in_view[2]
    screen_col = in_view[0] * inv_depth
    screen_row = in_view[1] * inv_depth
    scales = jnp.exp(values[3:6])
    quat = values[6:10] / jnp.sqrt(lax.optimization_barrier(jnp.sum(values[6:10] * values[6:10], axis=0, keepdims=True)))
    quat_w, quat_x, quat_y, quat_z = (quat[0], quat[1], quat[2], quat[3])
    spin = [[1.0 - 2.0 * (quat_y * quat_y + quat_z * quat_z), 2.0 * (quat_x * quat_y - quat_w * quat_z), 2.0 * (quat_x * quat_z + quat_w * quat_y)], [2.0 * (quat_x * quat_y + quat_w * quat_z), 1.0 - 2.0 * (quat_x * quat_x + quat_z * quat_z), 2.0 * (quat_y * quat_z - quat_w * quat_x)], [2.0 * (quat_x * quat_z - quat_w * quat_y), 2.0 * (quat_y * quat_z + quat_w * quat_x), 1.0 - 2.0 * (quat_x * quat_x + quat_y * quat_y)]]
    basis_cam = []
    for outer_index in range(3):
        row_terms = []
        for col_index in range(3):
            entry = turn[outer_index, 0] * spin[0][col_index]
            for mid_index in range(1, 3):
                entry = entry + turn[outer_index, mid_index] * spin[mid_index][col_index]
            row_terms.append(entry * scales[col_index])
        basis_cam.append(row_terms)
    jac_top = [(basis_cam[0][col_index] - screen_col * basis_cam[2][col_index]) * inv_depth for col_index in range(3)]
    jac_low = [(basis_cam[1][col_index] - screen_row * basis_cam[2][col_index]) * inv_depth for col_index in range(3)]
    sigma_a = jac_top[0] * jac_top[0] + jac_top[1] * jac_top[1] + jac_top[2] * jac_top[2]
    sigma_b = jac_top[0] * jac_low[0] + jac_top[1] * jac_low[1] + jac_top[2] * jac_low[2]
    sigma_c = jac_low[0] * jac_low[0] + jac_low[1] * jac_low[1] + jac_low[2] * jac_low[2]
    determinant = sigma_a * sigma_c - sigma_b * sigma_b
    opacity = jax.nn.sigmoid(values[10])
    distance = jnp.sqrt(lax.optimization_barrier(jnp.sum(offset * offset, axis=0)))
    unit_dir = offset / distance
    basis = harmonics(unit_dir[0], unit_dir[1], unit_dir[2])
    coeffs = values[11:59].reshape(16, 3, values.shape[1])
    colors = 0.5 + lax.optimization_barrier(jnp.sum(basis[:, None, :] * coeffs, axis=0))
    screen = jnp.stack([screen_col, screen_row, sigma_c / determinant, -sigma_b / determinant, sigma_a / determinant, opacity])
    return jnp.concatenate([screen, colors], axis=0)

def group_loss(pieces):
    features, live_mask, pixel_column, pixel_row, target_tile = pieces
    entries = live_mask.shape[1]
    delta_col = pixel_column[:, :, None] - features[0][:, None, :]
    delta_row = pixel_row[:, :, None] - features[1][:, None, :]
    power = -0.5 * (features[2][:, None, :] * delta_col * delta_col + 2.0 * features[3][:, None, :] * delta_col * delta_row + features[4][:, None, :] * delta_row * delta_row)
    alphas = features[5][:, None, :] * jnp.exp(power) * live_mask[:, None, :]
    log_keep = jnp.log(1.0 - alphas)
    earlier = (lax.broadcasted_iota(jnp.int32, (entries, entries), 0) < lax.broadcasted_iota(jnp.int32, (entries, entries), 1)).astype(jnp.float32)
    transmit = jnp.exp(jnp.einsum('bpl,lm->bpm', log_keep, earlier, precision=lax.Precision.HIGHEST))
    weights = alphas * transmit
    image = jnp.einsum('bpl,kbl->kbp', weights, features[6:9], precision=lax.Precision.HIGHEST)
    error = image - target_tile
    return jnp.sum(error * error)

def render_tiles(picked, live_mask, pixel_column, pixel_row, target_tile):
    groups = live_mask.shape[0] // 4
    entries = live_mask.shape[1]
    pixels = pixel_column.shape[1]
    stacked = (jnp.transpose(picked.reshape(picked.shape[0], groups, 4, entries), (1, 0, 2, 3)), live_mask.reshape(groups, 4, entries), pixel_column.reshape(groups, 4, pixels), pixel_row.reshape(groups, 4, pixels), jnp.transpose(target_tile.reshape(3, groups, 4, pixels), (1, 0, 2, 3)))
    return jnp.sum(lax.map(jax.checkpoint(group_loss), stacked))

def pixel_grid(first_tile, count, tiles_dev, rows_pix):
    tile_ids = first_tile + jnp.arange(count, dtype=jnp.int32)
    pixel_ids = jnp.arange(256, dtype=jnp.int32)
    block_cols = TILE_COLS // 4
    owner_ids = tile_ids // tiles_dev
    local_ids = tile_ids % tiles_dev
    tile_col = 4 * (owner_ids % block_cols) + local_ids % 4
    tile_row = tiles_dev // 4 * (owner_ids // block_cols) + local_ids // 4
    half_width = TILE_COLS * 8.0
    column = (tile_col[:, None] * 16 + pixel_ids[None, :] % 16).astype(jnp.float32)
    row_pos = (tile_row[:, None] * 16 + pixel_ids[None, :] // 16).astype(jnp.float32)
    return ((column + 0.5 - half_width) / half_width, (row_pos + 0.5 - rows_pix * 0.5) / half_width)

def adam_update(params, first_moment, second_moment, gradient, counts):
    row_ids = lax.broadcasted_iota(jnp.int32, params.shape, 0)
    rates = jnp.where(row_ids < 6, 0.01, jnp.where(row_ids < 10, 0.005, jnp.where(row_ids < 11, 0.05, jnp.where(row_ids < 14, 0.0025, 0.000125))))
    first_new = 0.9 * first_moment + 0.1 * gradient
    second = 0.999 * second_moment + 0.001 * gradient * gradient
    bias_one = 1.0 - 0.9 ** ADAM_STEP
    bias_two = 1.0 - 0.999 ** ADAM_STEP
    stride = rates * (first_new / bias_one) / (jnp.sqrt(second / bias_two) + 1e-08)
    seen_mask = counts > 0.0
    return (jnp.where(seen_mask, params - stride, params), jnp.where(seen_mask, first_new, first_moment), jnp.where(seen_mask, second, second_moment))

def reference(params, first_moment, second_moment, cameras, visible, send_plan, tile_lists, target):
    tiles_all = tile_lists.shape[1]
    tiles_dev = tiles_all // N_CELLS
    capacity = send_plan.shape[3]
    block = params.shape[1] // N_CELLS
    rows_pix = tiles_all // TILE_COLS * 16
    pixel_column, pixel_row = pixel_grid(0, tiles_all, tiles_dev, rows_pix)
    device_of = (jnp.arange(tiles_all, dtype=jnp.int32) // tiles_dev)[:, None]

    def view_loss(values, view_index):
        features = project(values, cameras[view_index])
        lists = tile_lists[view_index]
        live_mask = (lists >= 0).astype(jnp.float32)
        slot_ids = jnp.maximum(lists, 0)
        source = slot_ids // capacity
        column = slot_ids % capacity
        local_row = send_plan[view_index][source, device_of, column]
        global_row = (source * block + jnp.maximum(local_row, 0)).astype(jnp.int32)
        picked = jnp.take(features, global_row, axis=1)
        target_tile = target[view_index].reshape(3, tiles_all, 256)
        return render_tiles(picked, live_mask, pixel_column, pixel_row, target_tile)

    def total_loss(values):
        total = jnp.zeros((), jnp.float32)
        for view_index in range(N_VIEWS):
            total = total + view_loss(values, view_index)
        return total
    gradient = jax.grad(total_loss)(params)
    counts = lax.optimization_barrier(jnp.sum(visible.astype(jnp.float32), axis=0, keepdims=True))
    new_params, new_first, new_second = adam_update(params, first_moment, second_moment, gradient, counts)
    return (new_params, new_first, new_second)
```

```python
import functools

import jax
import jax.numpy as jnp
import numpy as np
from jax import lax
from jax.experimental import pallas as pl
from jax.experimental.pallas import tpu as pltpu
from jax.sharding import PartitionSpec as P

TILE_COLS = 32
ADAM_STEP = 1000
ROWS = 59
FEATS = 9
LANES = 128
LOG2E = 1.4426950408889634
ABSENT = -10000.0

harmonic_zero = 0.28209479177387814
harmonic_one = 0.4886025119029199
harmonic_two = (
    1.0925484305920792,
    -1.0925484305920792,
    0.31539156525252005,
    -1.0925484305920792,
    0.5462742152960396,
)
harmonic_three = (
    -0.5900435899266435,
    2.890611442640554,
    -0.4570457994644658,
    0.3731763325901154,
    -0.4570457994644658,
    1.445305721320277,
    -0.5900435899266435,
)

F32 = jnp.float32
BF16 = jnp.bfloat16
I32 = jnp.int32


def harmonics(across, upward, onward):
    across_sq = across * across
    upward_sq = upward * upward
    onward_sq = onward * onward
    return [
        None,
        -harmonic_one * upward,
        harmonic_one * onward,
        -harmonic_one * across,
        harmonic_two[0] * across * upward,
        harmonic_two[1] * upward * onward,
        harmonic_two[2] * (2.0 * onward_sq - across_sq - upward_sq),
        harmonic_two[3] * across * onward,
        harmonic_two[4] * (across_sq - upward_sq),
        harmonic_three[0] * upward * (3.0 * across_sq - upward_sq),
        harmonic_three[1] * across * upward * onward,
        harmonic_three[2] * upward * (4.0 * onward_sq - across_sq - upward_sq),
        harmonic_three[3] * onward * (2.0 * onward_sq - 3.0 * across_sq - 3.0 * upward_sq),
        harmonic_three[4] * across * (4.0 * onward_sq - across_sq - upward_sq),
        harmonic_three[5] * onward * (across_sq - upward_sq),
        harmonic_three[6] * across * (across_sq - 3.0 * upward_sq),
    ]


def rotation(roll, pitch, yaw):
    cr, sr = jnp.cos(roll), jnp.sin(roll)
    cp, sp = jnp.cos(pitch), jnp.sin(pitch)
    cy, sy = jnp.cos(yaw), jnp.sin(yaw)
    return [
        cy * cp,
        cy * sp * sr - sy * cr,
        cy * sp * cr + sy * sr,
        sy * cp,
        sy * sp * sr + cy * cr,
        sy * sp * cr - cy * sr,
        -sp,
        cp * sr,
        cp * cr,
    ]


def shape_basis(rows):
    scales = [jnp.exp(rows[3 + k]) for k in range(3)]
    qw, qx, qy, qz = rows[6], rows[7], rows[8], rows[9]
    norm = 1.0 / jnp.sqrt(qw * qw + qx * qx + qy * qy + qz * qz)
    qw, qx, qy, qz = qw * norm, qx * norm, qy * norm, qz * norm
    spin = [
        [1.0 - 2.0 * (qy * qy + qz * qz), 2.0 * (qx * qy - qw * qz), 2.0 * (qx * qz + qw * qy)],
        [2.0 * (qx * qy + qw * qz), 1.0 - 2.0 * (qx * qx + qz * qz), 2.0 * (qy * qz - qw * qx)],
        [2.0 * (qx * qz - qw * qy), 2.0 * (qy * qz + qw * qx), 1.0 - 2.0 * (qx * qx + qy * qy)],
    ]
    return [[spin[m][k] * scales[k] for k in range(3)] for m in range(3)]


def project_view(rows, basis, opacity, turn, centre):
    offset = [rows[k] - centre[k] for k in range(3)]
    seen = [
        turn[3 * m] * offset[0] + turn[3 * m + 1] * offset[1] + turn[3 * m + 2] * offset[2]
        for m in range(3)
    ]
    inv_depth = 1.0 / seen[2]
    col = seen[0] * inv_depth
    row = seen[1] * inv_depth
    cam = [
        [
            turn[3 * m] * basis[0][k] + turn[3 * m + 1] * basis[1][k] + turn[3 * m + 2] * basis[2][k]
            for k in range(3)
        ]
        for m in range(3)
    ]
    top = [(cam[0][k] - col * cam[2][k]) * inv_depth for k in range(3)]
    low = [(cam[1][k] - row * cam[2][k]) * inv_depth for k in range(3)]
    sa = top[0] * top[0] + top[1] * top[1] + top[2] * top[2]
    sb = top[0] * low[0] + top[1] * low[1] + top[2] * low[2]
    sc = low[0] * low[0] + low[1] * low[1] + low[2] * low[2]
    inv_det = 1.0 / (sa * sc - sb * sb)
    inv_dist = 1.0 / jnp.sqrt(
        offset[0] * offset[0] + offset[1] * offset[1] + offset[2] * offset[2]
    )
    harm = harmonics(offset[0] * inv_dist, offset[1] * inv_dist, offset[2] * inv_dist)
    colors = []
    for k in range(3):
        total = 0.5 + harmonic_zero * rows[11 + k]
        for j in range(1, 16):
            total = total + harm[j] * rows[11 + 3 * j + k]
        colors.append(total)
    return [col, row, sc * inv_det, -sb * inv_det, sa * inv_det, opacity, *colors]


def logistic(x):
    return 1.0 / (1.0 + jnp.exp(-x))


def block_transpose(four):
    lane = lax.broadcasted_iota(I32, (8, LANES), 1)
    low = lane < 64
    even = (lane & 32) == 0
    a, b, c, d = four
    a, c = jnp.where(low, a, pltpu.roll(c, 64, 1)), jnp.where(low, pltpu.roll(a, 64, 1), c)
    b, d = jnp.where(low, b, pltpu.roll(d, 64, 1)), jnp.where(low, pltpu.roll(b, 64, 1), d)
    a, b = jnp.where(even, a, pltpu.roll(b, 32, 1)), jnp.where(even, pltpu.roll(a, 96, 1), b)
    c, d = jnp.where(even, c, pltpu.roll(d, 32, 1)), jnp.where(even, pltpu.roll(c, 96, 1), d)
    return [a, b, c, d]


def wire_to_table(wire_ref, at, table_ref):
    for j in range(3):
        for h in range(2):
            four = [
                wire_ref[pl.ds(at + 3 * (32 * h + 8 * q) + j, 8, stride=3), :] for q in range(4)
            ]
            parts = block_transpose(four)
            for i in range(4):
                f = 4 * j + i
                if f < FEATS:
                    table_ref[16 * f + 8 * h : 16 * f + 8 * h + 8, :] = parts[i]


def table_to_wire(table, wire_ref):
    zero = jnp.zeros((8, LANES), F32)
    for j in range(3):
        for h in range(2):
            four = [table[4 * j + i][h] if 4 * j + i < FEATS else zero for i in range(4)]
            parts = block_transpose(four)
            for q in range(4):
                wire_ref[pl.ds(3 * (32 * h + 8 * q) + j, 8, stride=3), :] = parts[q]


def lookup(table_ref, feats, row, lane):
    found = [jnp.zeros((8, LANES), F32) for _ in range(feats)]
    for k in range(16):
        here = row == k
        for f in range(feats):
            source = jnp.broadcast_to(table_ref[16 * f + k : 16 * f + k + 1, :], (8, LANES))
            found[f] = jnp.where(here, jnp.take_along_axis(source, lane, axis=1, mode="promise_in_bounds"), found[f])
    return found


def to_dense(natural_ref, scratch_ref):
    for k in range(16):
        for a in range(8):
            high = min(8, ROWS - 8 * a)
            scratch_ref[64 * k + 8 * a : 64 * k + 8 * a + high, :] = natural_ref[
                8 * a : 8 * a + high, LANES * k : LANES * k + LANES
            ]


def dense_rows(scratch_ref):
    return [
        jnp.concatenate(
            [scratch_ref[pl.ds(512 * h + f, 8, stride=64), :] for h in range(2)], axis=0
        )
        for f in range(ROWS)
    ]


def project_kernel(camera_ref, params_ref, plan_ref, wire_ref, scratch_ref, table_ref, idx_ref):
    to_dense(params_ref, scratch_ref)
    rows = dense_rows(scratch_ref)
    angle = [jnp.full((8, LANES), camera_ref[0, k], F32) for k in range(3)]
    turn = [jnp.concatenate([t, t], axis=0) for t in rotation(*angle)]
    centre = [camera_ref[0, 3 + k] for k in range(3)]
    feats = project_view(rows, shape_basis(rows), logistic(rows[10]), turn, centre)
    for f in range(FEATS):
        table_ref[16 * f : 16 * f + 16, :] = feats[f]
    for h in range(2):
        for q in range(4):
            idx_ref[8 * h : 8 * h + 8, 32 * q : 32 * q + 32] = jnp.maximum(
                plan_ref[32 * h + 8 * q : 32 * h + 8 * q + 8, :], 0
            )
    out = [[None, None] for _ in range(FEATS)]
    for h in range(2):
        idx = idx_ref[8 * h : 8 * h + 8, :]
        found = lookup(table_ref, FEATS, idx >> 7, idx & 127)
        for f in range(FEATS):
            out[f][h] = found[f]
    table_to_wire(out, wire_ref)


def prep_kernel(camera_ref, plan_ref, lists_ref, inverse_ref, owner_ref):
    row = lax.broadcasted_iota(I32, (16, LANES), 0)
    lane = lax.broadcasted_iota(I32, (16, LANES), 1)
    device = 32 * (row >> 3) + 8 * (lane >> 5) + (row & 7)
    slot = 32 * device + (lane & 31)
    none = jnp.full((16, LANES), -1, I32)

    def tile_step(i, kept):
        s = i >> 2
        u = i & 3
        kept = list(kept)
        for jj in range(16):
            for t in range(4):
                e = lists_ref[t, 64 * s + 16 * u + jj]
                kept[t] = jnp.where(slot == e, LANES * u + 8 * jj + s, kept[t])
        return tuple(kept)

    kept = lax.fori_loop(0, 32, tile_step, (none,) * 4)
    for t in range(4):
        inverse_ref[16 * t : 16 * t + 16, :] = kept[t]

    gauss = row * LANES + lane

    def plan_step(d, kept):
        code = (8 * (d >> 5) + (d & 7)) * LANES + 32 * ((d >> 3) & 3)
        for c in range(32):
            kept = jnp.where(gauss == plan_ref[d, c], code + c, kept)
        return kept

    kept = lax.fori_loop(0, 64, plan_step, none)
    owner_ref[0:16, :] = kept.astype(F32)
    angle = [jnp.full((8, LANES), camera_ref[0, k], F32) for k in range(3)]
    turn = rotation(*angle)
    for k in range(9):
        owner_ref[16 + k : 17 + k, :] = turn[k][0:1, :]
    for k in range(3):
        owner_ref[25 + k : 26 + k, :] = jnp.full((1, LANES), camera_ref[0, 3 + k], F32)
    owner_ref[28:32, :] = jnp.zeros((4, LANES), F32)


def split(x, parts):
    done = []
    for _ in range(parts - 1):
        high = x.astype(BF16).astype(F32)
        done.append(high)
        x = x - high
    done.append(x)
    return done


def sublane_shift(x, by, fill):
    s = lax.broadcasted_iota(I32, x.shape, 0)
    moved = pltpu.roll(x, by % 8, 0)
    return jnp.where((s >= by) if by > 0 else (s < 8 + by), moved, fill)


def render_kernel(
    place_ref,
    wire_ref,
    entry_ref,
    inverse_ref,
    target_ref,
    basis_ref,
    moment_ref,
    out_ref,
    table_ref,
    lhs_ref,
    power_ref,
    color_ref,
    alpha_ref,
    trans_ref,
    split_ref,
    sums_ref,
    grads_ref,
):
    device = place_ref[0]
    rows_pix = place_ref[1]
    wire_to_table(wire_ref, 0, table_ref)

    entry = [entry_ref[8 * h : 8 * h + 8, :] for h in range(2)]
    feats = [[None, None] for _ in range(FEATS)]
    for h in range(2):
        e = jnp.maximum(entry[h], 0)
        row = 8 * ((e >> 10) & 1) + ((e >> 5) & 7)
        lane = 32 * ((e >> 8) & 3) + (e & 31)
        found = lookup(table_ref, FEATS, row, lane)
        for f in range(FEATS):
            feats[f][h] = found[f]
    feats = [jnp.concatenate(two, axis=0) for two in feats]
    live = jnp.concatenate(entry, axis=0) >= 0
    col, scr, c0, c1, c2, opacity = feats[:6]

    block_cols = TILE_COLS // 4
    tile_col = (
        4 * (device % block_cols) + lax.broadcasted_iota(I32, (16, LANES), 0) // 4
    ).astype(F32)
    tile_row = (device // block_cols).astype(F32)
    half = TILE_COLS * 8.0
    ex = (16.0 * tile_col + 8.0 - half) - half * col
    ey = (16.0 * tile_row + 8.0 - rows_pix.astype(F32) * 0.5) - half * scr
    factor = -0.5 * LOG2E / (half * half)
    a = factor * c0
    b = (2.0 * factor) * c1
    c = factor * c2
    bx = b * ex
    by = b * ey
    coeffs = [
        a,
        b,
        c,
        2.0 * a * ex + by,
        bx + 2.0 * c * ey,
        (a * ex + by) * ex + c * ey * ey + LOG2E * jnp.log(opacity),
    ]
    rest = [0.0, 0.0, 0.0, 0.0, 0.0, ABSENT]
    lines = []
    pieces = [split(jnp.where(live, x, r), 3) for x, r in zip(coeffs, rest)]
    for part in range(3):
        lines += [pieces[k][part] for k in range(6)]
    tints = [split(feats[6 + k], 3) for k in range(3)]
    for part in range(3):
        lines += [tints[k][part] for k in range(3)]
    lines += [jnp.zeros((16, LANES), F32)] * 5
    for k in range(32):
        for h in range(2):
            lhs_ref[pl.ds(256 * h + k, 8, stride=32), :] = lines[k][8 * h : 8 * h + 8, :]

    for t in range(4):
        for u in range(4):
            lhs = lhs_ref[32 * (4 * t + u) : 32 * (4 * t + u) + 32, :].T.astype(BF16)
            both = jnp.dot(lhs, basis_ref[...], preferred_element_type=F32)
            power_ref[128 * u : 128 * u + 128, :] = both[:, 0:256]
            color_ref[128 * u : 128 * u + 128, :] = both[:, 256:640]

        one = jnp.ones((8, LANES), F32)
        zero = jnp.zeros((8, LANES), F32)

        def forward(j, carry, t=t):
            at = pl.ds(pl.multiple_of(8 * j, 8), 8)
            tint = [color_ref[at, 128 * k : 128 * k + 128] for k in range(3)]
            new = []
            for p in range(2):
                trans, *image = carry[4 * p : 4 * p + 4]
                alpha = jnp.exp2(power_ref[at, 128 * p : 128 * p + 128])
                alpha_ref[at, 128 * p : 128 * p + 128] = alpha
                trans_ref[at, 128 * p : 128 * p + 128] = trans
                weight = alpha * trans
                new += [trans * (1.0 - alpha)]
                new += [image[k] + weight * tint[k] for k in range(3)]
            return tuple(new)

        carry = lax.fori_loop(0, 64, forward, (one, zero, zero, zero) * 2, unroll=8)

        before, behind, slopes = [], [], []
        for p in range(2):
            kept, *image = carry[4 * p : 4 * p + 4]
            lead = sublane_shift(kept, 1, 1.0)
            for by_ in (1, 2, 4):
                lead = lead * sublane_shift(lead, by_, 1.0)
            before.append(lead)
            slope = []
            for k in range(3):
                shown = jnp.sum(lead * image[k], axis=0, keepdims=True)
                goal = target_ref[k : k + 1, 256 * t + 128 * p : 256 * t + 128 * p + 128]
                slope.append(2.0 * (shown - goal))
            slopes.append(slope)
            add = slope[0] * image[0] + slope[1] * image[1] + slope[2] * image[2]
            mul = kept
            for by_ in (1, 2, 4):
                add = add + mul * sublane_shift(add, -by_, 0.0)
                mul = mul * sublane_shift(mul, -by_, 1.0)
            behind.append(sublane_shift(add, -1, 0.0))

        slope = [jnp.concatenate([slopes[0][k], slopes[1][k]], axis=1) for k in range(3)]
        sliced = [split(slope[k], 3) for k in range(3)]
        pad = jnp.zeros((1, 256), F32)
        rhs = []
        for part in range(3):
            rhs += [pad] * 18 + [sliced[k][part] for _ in range(3) for k in range(3)] + [pad] * 5
        rhs = jnp.concatenate(rhs, axis=0).astype(BF16)
        for u in range(4):
            lhs = lhs_ref[32 * (4 * t + u) : 32 * (4 * t + u) + 32, :].T.astype(BF16)
            lhs = jnp.concatenate([lhs, lhs, lhs], axis=1)
            power_ref[128 * u : 128 * u + 128, :] = jnp.dot(lhs, rhs, preferred_element_type=F32)

        def backward(i, carry):
            carry = list(carry)
            at = pl.multiple_of(16 * (31 - i), 16)
            for p in range(2):
                rest = carry[p]
                pair = [None, None]
                for o in (1, 0):
                    here = pl.ds(at + 8 * o, 8)
                    alpha = alpha_ref[here, 128 * p : 128 * p + 128]
                    trans = trans_ref[here, 128 * p : 128 * p + 128] * before[p]
                    gap = power_ref[here, 128 * p : 128 * p + 128] - rest
                    step = alpha * gap
                    rest = rest + step
                    pair[o] = (trans * step, trans * alpha)
                carry[p] = rest
                for n in range(2):
                    value = jnp.concatenate([pair[0][n], pair[1][n]], axis=0)
                    high = value.astype(BF16)
                    split_ref[2 * n, pl.ds(at, 16), 128 * p : 128 * p + 128] = high
                    split_ref[2 * n + 1, pl.ds(at, 16), 128 * p : 128 * p + 128] = (
                        value - high.astype(F32)
                    ).astype(BF16)
            return tuple(carry)

        lax.fori_loop(0, 32, backward, tuple(behind), unroll=4)

        across = (((1,), (1,)), ((), ()))
        nine = jnp.concatenate(
            [sliced[k][part] for part in range(3) for k in range(3)] + [pad] * 7, axis=0
        ).astype(BF16)
        moments = lax.dot_general(
            moment_ref[...], split_ref[0], across, preferred_element_type=F32
        ) + lax.dot_general(moment_ref[...], split_ref[1], across, preferred_element_type=F32)
        shades = lax.dot_general(
            nine, split_ref[2], across, preferred_element_type=F32
        ) + lax.dot_general(nine, split_ref[3], across, preferred_element_type=F32)
        for u in range(4):
            sums_ref[32 * (4 * t + u) : 32 * (4 * t + u) + 16, :] = moments[
                :, 128 * u : 128 * u + 128
            ]
            sums_ref[32 * (4 * t + u) + 16 : 32 * (4 * t + u) + 32, :] = shades[
                :, 128 * u : 128 * u + 128
            ]

    def summed(k):
        return jnp.concatenate(
            [sums_ref[pl.ds(256 * h + k, 8, stride=32), :] for h in range(2)], axis=0
        )

    mxx, mxy, myy, mx, my, m0 = [summed(k) for k in range(6)]
    sx = ex * m0 + mx
    sy = ey * m0 + my
    sxx = ex * (ex * m0 + 2.0 * mx) + mxx
    sxy = ex * (ey * m0 + my) + ey * mx + mxy
    syy = ey * (ey * m0 + 2.0 * my) + myy
    unit = 1.0 / half
    grads = [
        (c0 * sx + c1 * sy) * unit,
        (c1 * sx + c2 * sy) * unit,
        (-0.5 * unit * unit) * sxx,
        (-unit * unit) * sxy,
        (-0.5 * unit * unit) * syy,
        m0 / opacity,
    ]
    for k in range(3):
        grads.append(summed(16 + k) + summed(19 + k) + summed(22 + k))
    for f in range(FEATS):
        grads_ref[16 * f : 16 * f + 16, :] = grads[f]

    out = [[None, None] for _ in range(FEATS)]
    for h in range(2):
        total = [jnp.zeros((8, LANES), F32) for _ in range(FEATS)]
        for t in range(4):
            code = inverse_ref[16 * t + 8 * h : 16 * t + 8 * h + 8, :]
            row = code >> 7
            lane = code & 127
            found = [jnp.zeros((8, LANES), F32) for _ in range(FEATS)]
            for u in range(4):
                here = row == u
                for f in range(FEATS):
                    at = 16 * f + 4 * t + u
                    source = jnp.broadcast_to(grads_ref[at : at + 1, :], (8, LANES))
                    found[f] = jnp.where(
                        here, jnp.take_along_axis(source, lane, axis=1, mode="promise_in_bounds"), found[f]
                    )
            total = [x + y for x, y in zip(total, found)]
        for f in range(FEATS):
            out[f][h] = total[f]
    table_to_wire(out, out_ref)


def adam_kernel(
    wire_ref,
    owner_ref,
    params_ref,
    first_ref,
    second_ref,
    new_params_ref,
    new_first_ref,
    new_second_ref,
    scratch_ref,
    table_ref,
    pulled_ref,
):
    to_dense(params_ref, scratch_ref)
    rows = dense_rows(scratch_ref)
    seen = jnp.zeros((16, LANES), jnp.bool_)
    cotangents = []
    cams = []
    for v in range(4):
        wire_to_table(wire_ref, 192 * v, table_ref)
        halves = []
        for h in range(2):
            code = owner_ref[32 * v + 8 * h : 32 * v + 8 * h + 8, :].astype(I32)
            found = lookup(table_ref, FEATS, code >> 7, code & 127)
            halves.append(found)
        for f in range(FEATS):
            for h in range(2):
                at = 16 * (FEATS * v + f) + 8 * h
                pulled_ref[at : at + 8, :] = halves[h][f]
        seen = seen | (owner_ref[32 * v : 32 * v + 16, :] >= 0.0)
        cams.append(
            [
                jnp.broadcast_to(owner_ref[32 * v + 16 + k : 32 * v + 17 + k, :], (16, LANES))
                for k in range(12)
            ]
        )
    for v in range(4):
        cotangents.append(
            [
                pulled_ref[16 * (FEATS * v + f) : 16 * (FEATS * v + f) + 16, :]
                for f in range(FEATS)
            ]
        )

    def all_views(values):
        basis = shape_basis(values)
        opacity = logistic(values[10])
        return [project_view(values, basis, opacity, cam[:9], cam[9:]) for cam in cams]

    _, pull = jax.vjp(all_views, rows)
    gradient = pull(cotangents)[0]
    for f in range(ROWS):
        for h in range(2):
            scratch_ref[pl.ds(512 * h + f, 8, stride=64), :] = gradient[f][8 * h : 8 * h + 8, :]
    seen = seen.astype(F32)
    bias_one = 1.0 - 0.9**ADAM_STEP
    bias_two = 1.0 - 0.999**ADAM_STEP
    for a in range(8):
        high = min(8, ROWS - 8 * a)
        row = lax.broadcasted_iota(I32, (high, LANES), 0) + 8 * a
        rate = jnp.where(
            row < 6,
            0.01,
            jnp.where(row < 10, 0.005, jnp.where(row < 11, 0.05, jnp.where(row < 14, 0.0025, 0.000125))),
        ).astype(F32) * (1.0 / bias_one)
        for k in range(16):
            at = (slice(8 * a, 8 * a + high), slice(LANES * k, LANES * k + LANES))
            grad = scratch_ref[64 * k + 8 * a : 64 * k + 8 * a + high, :]
            here = jnp.broadcast_to(seen[k : k + 1, :], (high, LANES)) > 0.0
            p, m, s = params_ref[at], first_ref[at], second_ref[at]
            m_new = 0.9 * m + 0.1 * grad
            s_new = 0.999 * s + 0.001 * grad * grad
            stride = rate * m_new / (jnp.sqrt(s_new * (1.0 / bias_two)) + 1e-08)
            new_params_ref[at] = jnp.where(here, p - stride, p)
            new_first_ref[at] = jnp.where(here, m_new, m)
            new_second_ref[at] = jnp.where(here, s_new, s)


def pixel_constants():
    pixel = np.arange(256)
    x = pixel % 16 - 7.5
    y = pixel // 16 - 7.5
    six = np.stack([x * x, x * y, y * y, x, y, np.ones(256)])
    basis = np.zeros((32, 640), np.float32)
    for part in range(3):
        basis[6 * part : 6 * part + 6, :256] = six
        for k in range(3):
            basis[18 + 3 * part + k, 256 + 128 * k : 384 + 128 * k] = 1.0
    moment = np.zeros((16, 256), np.float32)
    moment[:6] = six
    return jnp.asarray(basis, BF16), jnp.asarray(moment, BF16)


VMEM = pl.BlockSpec(memory_space=pltpu.VMEM)
SMEM = pl.BlockSpec(memory_space=pltpu.SMEM)


def call(kernel, outs, ins, scratch, megabytes, cost):
    flops, moved = cost
    return pl.pallas_call(
        kernel,
        out_shape=outs,
        in_specs=ins,
        out_specs=jax.tree.map(lambda _: VMEM, outs),
        scratch_shapes=scratch,
        compiler_params=pltpu.CompilerParams(vmem_limit_bytes=megabytes << 20),
        cost_estimate=pl.CostEstimate(flops=flops, bytes_accessed=moved, transcendentals=0),
    )


def shards(params, first_moment, second_moment, cameras, visible, send_plan, tile_lists, target):
    del visible
    cells = lax.axis_size("cells")
    views = lax.axis_size("views")
    plan = send_plan[0, 0]
    lists = tile_lists[0]
    tiles = lists.shape[0]
    rows_pix = tiles * cells // TILE_COLS * 16
    place = jnp.stack([lax.axis_index("cells"), jnp.int32(rows_pix)]).astype(I32)
    f32 = lambda *shape: jax.ShapeDtypeStruct(shape, F32)
    vmem = lambda *shape: pltpu.VMEM(shape, F32)

    wire = call(
        project_kernel,
        f32(192, LANES),
        [SMEM, VMEM, VMEM],
        [vmem(1024, LANES), vmem(144, LANES), pltpu.VMEM((16, LANES), I32)],
        16,
        (10_000_000, 600_000),
    )(cameras, params, plan)
    arrived = lax.all_to_all(wire.reshape(64, 1, 384), "cells", 0, 0, tiled=True)

    inverse, owner = call(
        prep_kernel,
        (jax.ShapeDtypeStruct((64, LANES), I32), f32(32, LANES)),
        [SMEM, SMEM, SMEM],
        [],
        8,
        (40_000_000, 50_000),
    )(cameras, plan, lists)
    owners = lax.all_gather(owner, "views", tiled=True)
    entries = lists.reshape(4, 8, 4, 16).transpose(0, 2, 3, 1).reshape(16, LANES)

    basis, moment = pixel_constants()
    back = call(
        render_kernel,
        f32(192, LANES),
        [SMEM, VMEM, VMEM, VMEM, VMEM, VMEM, VMEM],
        [
            vmem(144, LANES),
            vmem(512, LANES),
            vmem(512, 256),
            vmem(512, 384),
            vmem(512, 256),
            vmem(512, 256),
            pltpu.VMEM((4, 512, 256), BF16),
            vmem(512, LANES),
            vmem(144, LANES),
        ],
        32,
        (100_000_000, 300_000),
    )(place, arrived.reshape(192, LANES), entries, inverse, target[0], basis, moment)
    returned = lax.all_to_all(back.reshape(64, 1, 384), "cells", 0, 0, tiled=True)
    returned = returned.reshape(192, LANES)
    every = lax.all_to_all(
        jnp.broadcast_to(returned[None], (views, 192, LANES)), "views", 0, 0, tiled=True
    )
    shape = f32(*params.shape)
    return call(
        adam_kernel,
        (shape, shape, shape),
        [VMEM] * 5,
        [vmem(1024, LANES), vmem(144, LANES), vmem(16 * FEATS * 4, LANES)],
        24,
        (40_000_000, 3_500_000),
    )(every.reshape(192 * 4, LANES), owners, params, first_moment, second_moment)


def solution(mesh):
    in_specs = (
        P(None, "cells"),
        P(None, "cells"),
        P(None, "cells"),
        P("views", None),
        P("views", "cells"),
        P("views", "cells", None, None),
        P("views", "cells", None),
        P("views", None, "cells"),
    )
    out_specs = (P(None, "cells"), P(None, "cells"), P(None, "cells"))
    return jax.shard_map(shards, mesh=mesh, in_specs=in_specs, out_specs=out_specs, check_vma=False)
```

```python
import functools

import jax
import jax.numpy as jnp
import numpy as np
from jax import lax
from jax.experimental import pallas as pl
from jax.experimental.pallas import tpu as pltpu
from jax.sharding import PartitionSpec as P

TILE_COLS = 32
ADAM_STEP = 1000
ROWS = 59
FEATS = 9
LANES = 128
LOG2E = 1.4426950408889634
ABSENT = -10000.0

harmonic_zero = 0.28209479177387814
harmonic_one = 0.4886025119029199
harmonic_two = (
    1.0925484305920792,
    -1.0925484305920792,
    0.31539156525252005,
    -1.0925484305920792,
    0.5462742152960396,
)
harmonic_three = (
    -0.5900435899266435,
    2.890611442640554,
    -0.4570457994644658,
    0.3731763325901154,
    -0.4570457994644658,
    1.445305721320277,
    -0.5900435899266435,
)

F32 = jnp.float32
BF16 = jnp.bfloat16
I32 = jnp.int32


def harmonics(across, upward, onward):
    across_sq = across * across
    upward_sq = upward * upward
    onward_sq = onward * onward
    return [
        None,
        -harmonic_one * upward,
        harmonic_one * onward,
        -harmonic_one * across,
        harmonic_two[0] * across * upward,
        harmonic_two[1] * upward * onward,
        harmonic_two[2] * (2.0 * onward_sq - across_sq - upward_sq),
        harmonic_two[3] * across * onward,
        harmonic_two[4] * (across_sq - upward_sq),
        harmonic_three[0] * upward * (3.0 * across_sq - upward_sq),
        harmonic_three[1] * across * upward * onward,
        harmonic_three[2] * upward * (4.0 * onward_sq - across_sq - upward_sq),
        harmonic_three[3] * onward * (2.0 * onward_sq - 3.0 * across_sq - 3.0 * upward_sq),
        harmonic_three[4] * across * (4.0 * onward_sq - across_sq - upward_sq),
        harmonic_three[5] * onward * (across_sq - upward_sq),
        harmonic_three[6] * across * (across_sq - 3.0 * upward_sq),
    ]


def rotation(roll, pitch, yaw):
    cr, sr = jnp.cos(roll), jnp.sin(roll)
    cp, sp = jnp.cos(pitch), jnp.sin(pitch)
    cy, sy = jnp.cos(yaw), jnp.sin(yaw)
    return [
        cy * cp,
        cy * sp * sr - sy * cr,
        cy * sp * cr + sy * sr,
        sy * cp,
        sy * sp * sr + cy * cr,
        sy * sp * cr - cy * sr,
        -sp,
        cp * sr,
        cp * cr,
    ]


def shape_basis(rows):
    scales = [jnp.exp(rows[3 + k]) for k in range(3)]
    qw, qx, qy, qz = rows[6], rows[7], rows[8], rows[9]
    norm = 1.0 / jnp.sqrt(qw * qw + qx * qx + qy * qy + qz * qz)
    qw, qx, qy, qz = qw * norm, qx * norm, qy * norm, qz * norm
    spin = [
        [1.0 - 2.0 * (qy * qy + qz * qz), 2.0 * (qx * qy - qw * qz), 2.0 * (qx * qz + qw * qy)],
        [2.0 * (qx * qy + qw * qz), 1.0 - 2.0 * (qx * qx + qz * qz), 2.0 * (qy * qz - qw * qx)],
        [2.0 * (qx * qz - qw * qy), 2.0 * (qy * qz + qw * qx), 1.0 - 2.0 * (qx * qx + qy * qy)],
    ]
    return [[spin[m][k] * scales[k] for k in range(3)] for m in range(3)]


def project_view(rows, basis, opacity, turn, centre):
    offset = [rows[k] - centre[k] for k in range(3)]
    seen = [
        turn[3 * m] * offset[0] + turn[3 * m + 1] * offset[1] + turn[3 * m + 2] * offset[2]
        for m in range(3)
    ]
    inv_depth = 1.0 / seen[2]
    col = seen[0] * inv_depth
    row = seen[1] * inv_depth
    cam = [
        [
            turn[3 * m] * basis[0][k] + turn[3 * m + 1] * basis[1][k] + turn[3 * m + 2] * basis[2][k]
            for k in range(3)
        ]
        for m in range(3)
    ]
    top = [(cam[0][k] - col * cam[2][k]) * inv_depth for k in range(3)]
    low = [(cam[1][k] - row * cam[2][k]) * inv_depth for k in range(3)]
    sa = top[0] * top[0] + top[1] * top[1] + top[2] * top[2]
    sb = top[0] * low[0] + top[1] * low[1] + top[2] * low[2]
    sc = low[0] * low[0] + low[1] * low[1] + low[2] * low[2]
    inv_det = 1.0 / (sa * sc - sb * sb)
    inv_dist = 1.0 / jnp.sqrt(
        offset[0] * offset[0] + offset[1] * offset[1] + offset[2] * offset[2]
    )
    harm = harmonics(offset[0] * inv_dist, offset[1] * inv_dist, offset[2] * inv_dist)
    colors = []
    for k in range(3):
        total = 0.5 + harmonic_zero * rows[11 + k]
        for j in range(1, 16):
            total = total + harm[j] * rows[11 + 3 * j + k]
        colors.append(total)
    return [col, row, sc * inv_det, -sb * inv_det, sa * inv_det, opacity, *colors]


def logistic(x):
    return 1.0 / (1.0 + jnp.exp(-x))


def block_transpose(four):
    lane = lax.broadcasted_iota(I32, (8, LANES), 1)
    low = lane < 64
    even = (lane & 32) == 0
    a, b, c, d = four
    a, c = jnp.where(low, a, pltpu.roll(c, 64, 1)), jnp.where(low, pltpu.roll(a, 64, 1), c)
    b, d = jnp.where(low, b, pltpu.roll(d, 64, 1)), jnp.where(low, pltpu.roll(b, 64, 1), d)
    a, b = jnp.where(even, a, pltpu.roll(b, 32, 1)), jnp.where(even, pltpu.roll(a, 96, 1), b)
    c, d = jnp.where(even, c, pltpu.roll(d, 32, 1)), jnp.where(even, pltpu.roll(c, 96, 1), d)
    return [a, b, c, d]


def wire_to_table(wire_ref, at, table_ref):
    for j in range(3):
        for h in range(2):
            four = [
                wire_ref[pl.ds(at + 3 * (32 * h + 8 * q) + j, 8, stride=3), :] for q in range(4)
            ]
            parts = block_transpose(four)
            for i in range(4):
                f = 4 * j + i
                if f < FEATS:
                    table_ref[16 * f + 8 * h : 16 * f + 8 * h + 8, :] = parts[i]


def table_to_wire(table, wire_ref):
    zero = jnp.zeros((8, LANES), F32)
    for j in range(3):
        for h in range(2):
            four = [table[4 * j + i][h] if 4 * j + i < FEATS else zero for i in range(4)]
            parts = block_transpose(four)
            for q in range(4):
                wire_ref[pl.ds(3 * (32 * h + 8 * q) + j, 8, stride=3), :] = parts[q]


def lookup(table_ref, feats, row, lane):
    found = [jnp.zeros((8, LANES), F32) for _ in range(feats)]
    for k in range(16):
        here = row == k
        for f in range(feats):
            source = jnp.broadcast_to(table_ref[16 * f + k : 16 * f + k + 1, :], (8, LANES))
            found[f] = jnp.where(here, jnp.take_along_axis(source, lane, axis=1, mode="promise_in_bounds"), found[f])
    return found


def to_dense(natural_ref, scratch_ref):
    for k in range(16):
        for a in range(8):
            high = min(8, ROWS - 8 * a)
            scratch_ref[64 * k + 8 * a : 64 * k + 8 * a + high, :] = natural_ref[
                8 * a : 8 * a + high, LANES * k : LANES * k + LANES
            ]


def dense_rows(scratch_ref):
    return [
        jnp.concatenate(
            [scratch_ref[pl.ds(512 * h + f, 8, stride=64), :] for h in range(2)], axis=0
        )
        for f in range(ROWS)
    ]


def project_kernel(camera_ref, params_ref, plan_ref, wire_ref, scratch_ref, table_ref, idx_ref):
    to_dense(params_ref, scratch_ref)
    rows = dense_rows(scratch_ref)
    angle = [jnp.full((8, LANES), camera_ref[0, k], F32) for k in range(3)]
    turn = [jnp.concatenate([t, t], axis=0) for t in rotation(*angle)]
    centre = [camera_ref[0, 3 + k] for k in range(3)]
    feats = project_view(rows, shape_basis(rows), logistic(rows[10]), turn, centre)
    for f in range(FEATS):
        table_ref[16 * f : 16 * f + 16, :] = feats[f]
    plan = jnp.maximum(plan_ref[...], 0).T
    for h in range(2):
        for q in range(4):
            idx_ref[8 * h : 8 * h + 8, 32 * q : 32 * q + 32] = plan[
                32 * h + 8 * q : 32 * h + 8 * q + 8, :
            ]
    out = [[None, None] for _ in range(FEATS)]
    for h in range(2):
        idx = idx_ref[8 * h : 8 * h + 8, :]
        found = lookup(table_ref, FEATS, idx >> 7, idx & 127)
        for f in range(FEATS):
            out[f][h] = found[f]
    table_to_wire(out, wire_ref)


def slots_kernel(lists_ref, inverse_ref):
    row = lax.broadcasted_iota(I32, (16, LANES), 0)
    lane = lax.broadcasted_iota(I32, (16, LANES), 1)
    device = 32 * (row >> 3) + 8 * (lane >> 5) + (row & 7)
    slot = 32 * device + (lane & 31)
    none = jnp.full((16, LANES), -1, I32)

    def tile_step(i, kept):
        s = i >> 2
        u = i & 3
        kept = list(kept)
        for jj in range(16):
            for t in range(4):
                e = lists_ref[t, 64 * s + 16 * u + jj]
                kept[t] = jnp.where(slot == e, LANES * u + 8 * jj + s, kept[t])
        return tuple(kept)

    kept = lax.fori_loop(0, 32, tile_step, (none,) * 4)
    for t in range(4):
        inverse_ref[16 * t : 16 * t + 16, :] = kept[t]


def owner_kernel(camera_ref, plan_ref, code_ref, view_ref):
    row = lax.broadcasted_iota(I32, (16, LANES), 0)
    lane = lax.broadcasted_iota(I32, (16, LANES), 1)
    gauss = row * LANES + lane

    def plan_step(d, kept):
        code = (8 * (d >> 5) + (d & 7)) * LANES + 32 * ((d >> 3) & 3)
        for c in range(32):
            kept = jnp.where(gauss == plan_ref[c, d], code + c, kept)
        return kept

    code_ref[...] = lax.fori_loop(0, 64, plan_step, jnp.full((16, LANES), -1, I32))
    angle = [jnp.full((8, LANES), camera_ref[0, k], F32) for k in range(3)]
    values = rotation(*angle) + [jnp.full((8, LANES), camera_ref[0, 3 + k], F32) for k in range(3)]
    lane = lax.broadcasted_iota(I32, (8, LANES), 1)
    view = jnp.zeros((8, LANES), F32)
    for k in range(12):
        view = jnp.where(lane == k, values[k], view)
    view_ref[...] = view


def pull_kernel(wire_ref, code_ref, view_ref, out_ref, table_ref):
    wire_to_table(wire_ref, 0, table_ref)
    for h in range(2):
        code = code_ref[8 * h : 8 * h + 8, :]
        found = lookup(table_ref, FEATS, code >> 7, code & 127)
        for f in range(FEATS):
            out_ref[16 * f + 8 * h : 16 * f + 8 * h + 8, :] = found[f]
        out_ref[144 + 8 * h : 152 + 8 * h, :] = jnp.where(code >= 0, 1.0, 0.0)
    out_ref[160:168, :] = view_ref[...]


def split(x, parts):
    done = []
    for _ in range(parts - 1):
        high = x.astype(BF16).astype(F32)
        done.append(high)
        x = x - high
    done.append(x)
    return done


def sublane_shift(x, by, fill):
    s = lax.broadcasted_iota(I32, x.shape, 0)
    moved = pltpu.roll(x, by % 8, 0)
    return jnp.where((s >= by) if by > 0 else (s < 8 + by), moved, fill)


def render_kernel(
    device_rows,
    place_ref,
    wire_ref,
    lists_ref,
    inverse_ref,
    target_ref,
    basis_ref,
    moment_ref,
    out_ref,
    table_ref,
    lhs_ref,
    power_ref,
    color_ref,
    alpha_ref,
    trans_ref,
    split_ref,
    sums_ref,
    grads_ref,
):
    device = place_ref[0]
    rows_pix = device_rows
    wire_to_table(wire_ref, 0, table_ref)

    sub = lax.broadcasted_iota(I32, (8, LANES), 0)
    lane = lax.broadcasted_iota(I32, (8, LANES), 1)
    entry = []
    for h in range(2):
        e = jnp.zeros((8, LANES), I32)
        for w in range(4):
            at = slice(LANES * w, LANES * w + LANES)
            lists = jnp.where(
                sub < 4,
                jnp.broadcast_to(lists_ref[2 * h : 2 * h + 1, at], (8, LANES)),
                jnp.broadcast_to(lists_ref[2 * h + 1 : 2 * h + 2, at], (8, LANES)),
            )
            source = 64 * (lane & 1) + 16 * (sub & 3) + (lane >> 3)
            moved = jnp.take_along_axis(lists, source, axis=1, mode="promise_in_bounds")
            e = jnp.where((lane & 7) >> 1 == w, moved, e)
        entry.append(e)
    feats = [[None, None] for _ in range(FEATS)]
    for h in range(2):
        e = jnp.maximum(entry[h], 0)
        row = 8 * ((e >> 10) & 1) + ((e >> 5) & 7)
        lane = 32 * ((e >> 8) & 3) + (e & 31)
        found = lookup(table_ref, FEATS, row, lane)
        for f in range(FEATS):
            feats[f][h] = found[f]
    feats = [jnp.concatenate(two, axis=0) for two in feats]
    live = jnp.concatenate(entry, axis=0) >= 0
    col, scr, c0, c1, c2, opacity = feats[:6]

    block_cols = TILE_COLS // 4
    tile_col = (
        4 * (device % block_cols) + lax.broadcasted_iota(I32, (16, LANES), 0) // 4
    ).astype(F32)
    tile_row = (device // block_cols).astype(F32)
    half = TILE_COLS * 8.0
    ex = (16.0 * tile_col + 8.0 - half) - half * col
    ey = (16.0 * tile_row + 8.0 - rows_pix * 0.5) - half * scr
    factor = -0.5 * LOG2E / (half * half)
    a = factor * c0
    b = (2.0 * factor) * c1
    c = factor * c2
    bx = b * ex
    by = b * ey
    coeffs = [
        a,
        b,
        c,
        2.0 * a * ex + by,
        bx + 2.0 * c * ey,
        (a * ex + by) * ex + c * ey * ey + LOG2E * jnp.log(opacity),
    ]
    rest = [0.0, 0.0, 0.0, 0.0, 0.0, ABSENT]
    lines = []
    pieces = [split(jnp.where(live, x, r), 3) for x, r in zip(coeffs, rest)]
    for part in range(3):
        lines += [pieces[k][part] for k in range(6)]
    tints = [split(feats[6 + k], 3) for k in range(3)]
    for part in range(3):
        lines += [tints[k][part] for k in range(3)]
    lines += [jnp.zeros((16, LANES), F32)] * 5
    for k in range(32):
        for h in range(2):
            lhs_ref[pl.ds(256 * h + k, 8, stride=32), :] = lines[k][8 * h : 8 * h + 8, :]

    for t in range(4):
        for u in range(4):
            lhs = lhs_ref[32 * (4 * t + u) : 32 * (4 * t + u) + 32, :].T.astype(BF16)
            both = jnp.dot(lhs, basis_ref[...], preferred_element_type=F32)
            power_ref[128 * u : 128 * u + 128, :] = both[:, 0:256]
            color_ref[128 * u : 128 * u + 128, :] = both[:, 256:640]

        one = jnp.ones((8, LANES), F32)
        zero = jnp.zeros((8, LANES), F32)

        def forward(j, carry, t=t):
            at = pl.ds(pl.multiple_of(8 * j, 8), 8)
            tint = [color_ref[at, 128 * k : 128 * k + 128] for k in range(3)]
            new = []
            for p in range(2):
                trans, *image = carry[4 * p : 4 * p + 4]
                alpha = jnp.exp2(power_ref[at, 128 * p : 128 * p + 128])
                alpha_ref[at, 128 * p : 128 * p + 128] = alpha
                trans_ref[at, 128 * p : 128 * p + 128] = trans
                weight = alpha * trans
                new += [trans * (1.0 - alpha)]
                new += [image[k] + weight * tint[k] for k in range(3)]
            return tuple(new)

        carry = lax.fori_loop(0, 64, forward, (one, zero, zero, zero) * 2, unroll=8)

        before, behind, slopes = [], [], []
        for p in range(2):
            kept, *image = carry[4 * p : 4 * p + 4]
            lead = sublane_shift(kept, 1, 1.0)
            for by_ in (1, 2, 4):
                lead = lead * sublane_shift(lead, by_, 1.0)
            before.append(lead)
            slope = []
            for k in range(3):
                shown = jnp.sum(lead * image[k], axis=0, keepdims=True)
                goal = target_ref[k, :, 256 * t + 128 * p : 256 * t + 128 * p + 128]
                slope.append(2.0 * (shown - goal))
            slopes.append(slope)
            add = slope[0] * image[0] + slope[1] * image[1] + slope[2] * image[2]
            mul = kept
            for by_ in (1, 2, 4):
                add = add + mul * sublane_shift(add, -by_, 0.0)
                mul = mul * sublane_shift(mul, -by_, 1.0)
            behind.append(sublane_shift(add, -1, 0.0))

        slope = [jnp.concatenate([slopes[0][k], slopes[1][k]], axis=1) for k in range(3)]
        sliced = [split(slope[k], 3) for k in range(3)]
        pad = jnp.zeros((1, 256), F32)
        rhs = []
        for part in range(3):
            rhs += [pad] * 18 + [sliced[k][part] for _ in range(3) for k in range(3)] + [pad] * 5
        rhs = jnp.concatenate(rhs, axis=0).astype(BF16)
        for u in range(4):
            lhs = lhs_ref[32 * (4 * t + u) : 32 * (4 * t + u) + 32, :].T.astype(BF16)
            lhs = jnp.concatenate([lhs, lhs, lhs], axis=1)
            power_ref[128 * u : 128 * u + 128, :] = jnp.dot(lhs, rhs, preferred_element_type=F32)

        def backward(i, carry):
            carry = list(carry)
            at = pl.multiple_of(16 * (31 - i), 16)
            for p in range(2):
                rest = carry[p]
                pair = [None, None]
                for o in (1, 0):
                    here = pl.ds(at + 8 * o, 8)
                    alpha = alpha_ref[here, 128 * p : 128 * p + 128]
                    trans = trans_ref[here, 128 * p : 128 * p + 128] * before[p]
                    gap = power_ref[here, 128 * p : 128 * p + 128] - rest
                    step = alpha * gap
                    rest = rest + step
                    pair[o] = (trans * step, trans * alpha)
                carry[p] = rest
                for n in range(2):
                    value = jnp.concatenate([pair[0][n], pair[1][n]], axis=0)
                    high = value.astype(BF16)
                    split_ref[2 * n, pl.ds(at, 16), 128 * p : 128 * p + 128] = high
                    split_ref[2 * n + 1, pl.ds(at, 16), 128 * p : 128 * p + 128] = (
                        value - high.astype(F32)
                    ).astype(BF16)
            return tuple(carry)

        lax.fori_loop(0, 32, backward, tuple(behind), unroll=4)

        across = (((1,), (1,)), ((), ()))
        nine = jnp.concatenate(
            [sliced[k][part] for part in range(3) for k in range(3)] + [pad] * 7, axis=0
        ).astype(BF16)
        moments = lax.dot_general(
            moment_ref[...], split_ref[0], across, preferred_element_type=F32
        ) + lax.dot_general(moment_ref[...], split_ref[1], across, preferred_element_type=F32)
        shades = lax.dot_general(
            nine, split_ref[2], across, preferred_element_type=F32
        ) + lax.dot_general(nine, split_ref[3], across, preferred_element_type=F32)
        for u in range(4):
            sums_ref[32 * (4 * t + u) : 32 * (4 * t + u) + 16, :] = moments[
                :, 128 * u : 128 * u + 128
            ]
            sums_ref[32 * (4 * t + u) + 16 : 32 * (4 * t + u) + 32, :] = shades[
                :, 128 * u : 128 * u + 128
            ]

    def summed(k):
        return jnp.concatenate(
            [sums_ref[pl.ds(256 * h + k, 8, stride=32), :] for h in range(2)], axis=0
        )

    mxx, mxy, myy, mx, my, m0 = [summed(k) for k in range(6)]
    sx = ex * m0 + mx
    sy = ey * m0 + my
    sxx = ex * (ex * m0 + 2.0 * mx) + mxx
    sxy = ex * (ey * m0 + my) + ey * mx + mxy
    syy = ey * (ey * m0 + 2.0 * my) + myy
    unit = 1.0 / half
    grads = [
        (c0 * sx + c1 * sy) * unit,
        (c1 * sx + c2 * sy) * unit,
        (-0.5 * unit * unit) * sxx,
        (-unit * unit) * sxy,
        (-0.5 * unit * unit) * syy,
        m0 / opacity,
    ]
    for k in range(3):
        grads.append(summed(16 + k) + summed(19 + k) + summed(22 + k))
    for f in range(FEATS):
        grads_ref[16 * f : 16 * f + 16, :] = grads[f]

    out = [[None, None] for _ in range(FEATS)]
    for h in range(2):
        total = [jnp.zeros((8, LANES), F32) for _ in range(FEATS)]
        for t in range(4):
            code = inverse_ref[16 * t + 8 * h : 16 * t + 8 * h + 8, :]
            row = code >> 7
            lane = code & 127
            found = [jnp.zeros((8, LANES), F32) for _ in range(FEATS)]
            for u in range(4):
                here = row == u
                for f in range(FEATS):
                    at = 16 * f + 4 * t + u
                    source = jnp.broadcast_to(grads_ref[at : at + 1, :], (8, LANES))
                    found[f] = jnp.where(
                        here, jnp.take_along_axis(source, lane, axis=1, mode="promise_in_bounds"), found[f]
                    )
            total = [x + y for x, y in zip(total, found)]
        for f in range(FEATS):
            out[f][h] = total[f]
    table_to_wire(out, out_ref)


def adam_kernel(
    place_ref,
    own_ref,
    one_ref,
    two_ref,
    three_ref,
    params_ref,
    first_ref,
    second_ref,
    new_params_ref,
    new_first_ref,
    new_second_ref,
    scratch_ref,
    pulled_ref,
):
    for k, ref in enumerate((own_ref, one_ref, two_ref, three_ref)):
        at = pl.multiple_of(168 * ((place_ref[0] - k) & 3), 8)
        pulled_ref[pl.ds(at, 168), :] = ref[...]
    to_dense(params_ref, scratch_ref)
    rows = dense_rows(scratch_ref)
    seen = jnp.zeros((16, LANES), F32)
    cotangents = []
    cams = []
    for v in range(4):
        at = 168 * v
        cotangents.append(
            [pulled_ref[at + 16 * f : at + 16 * f + 16, :] for f in range(FEATS)]
        )
        seen = seen + pulled_ref[at + 144 : at + 160, :]
        cams.append(
            [
                jnp.broadcast_to(pulled_ref[at + 160 : at + 161, k : k + 1], (16, LANES))
                for k in range(12)
            ]
        )

    def all_views(values):
        basis = shape_basis(values)
        opacity = logistic(values[10])
        return [project_view(values, basis, opacity, cam[:9], cam[9:]) for cam in cams]

    _, pull = jax.vjp(all_views, rows)
    gradient = pull(cotangents)[0]
    for f in range(ROWS):
        for h in range(2):
            scratch_ref[pl.ds(512 * h + f, 8, stride=64), :] = gradient[f][8 * h : 8 * h + 8, :]
    bias_one = 1.0 - 0.9**ADAM_STEP
    bias_two = 1.0 - 0.999**ADAM_STEP
    for a in range(8):
        high = min(8, ROWS - 8 * a)
        row = lax.broadcasted_iota(I32, (high, LANES), 0) + 8 * a
        rate = jnp.where(
            row < 6,
            0.01,
            jnp.where(row < 10, 0.005, jnp.where(row < 11, 0.05, jnp.where(row < 14, 0.0025, 0.000125))),
        ).astype(F32) * (1.0 / bias_one)
        for k in range(16):
            at = (slice(8 * a, 8 * a + high), slice(LANES * k, LANES * k + LANES))
            grad = scratch_ref[64 * k + 8 * a : 64 * k + 8 * a + high, :]
            here = jnp.broadcast_to(seen[k : k + 1, :], (high, LANES)) > 0.0
            p, m, s = params_ref[at], first_ref[at], second_ref[at]
            m_new = 0.9 * m + 0.1 * grad
            s_new = 0.999 * s + 0.001 * grad * grad
            stride = rate * m_new / (jnp.sqrt(s_new * (1.0 / bias_two)) + 1e-08)
            new_params_ref[at] = jnp.where(here, p - stride, p)
            new_first_ref[at] = jnp.where(here, m_new, m)
            new_second_ref[at] = jnp.where(here, s_new, s)


def pixel_constants():
    pixel = np.arange(256)
    x = pixel % 16 - 7.5
    y = pixel // 16 - 7.5
    six = np.stack([x * x, x * y, y * y, x, y, np.ones(256)])
    basis = np.zeros((32, 640), np.float32)
    for part in range(3):
        basis[6 * part : 6 * part + 6, :256] = six
        for k in range(3):
            basis[18 + 3 * part + k, 256 + 128 * k : 384 + 128 * k] = 1.0
    moment = np.zeros((16, 256), np.float32)
    moment[:6] = six
    return jnp.asarray(basis, BF16), jnp.asarray(moment, BF16)


VMEM = pl.BlockSpec(memory_space=pltpu.VMEM)
SMEM = pl.BlockSpec(memory_space=pltpu.SMEM)


def call(kernel, outs, ins, scratch, megabytes, cost):
    flops, moved = cost
    return pl.pallas_call(
        kernel,
        out_shape=outs,
        in_specs=ins,
        out_specs=jax.tree.map(lambda _: VMEM, outs),
        scratch_shapes=scratch,
        compiler_params=pltpu.CompilerParams(vmem_limit_bytes=megabytes << 20),
        cost_estimate=pl.CostEstimate(flops=flops, bytes_accessed=moved, transcendentals=0),
    )


def shards(params, first_moment, second_moment, cameras, visible, send_plan, tile_lists, target):
    del visible
    cells = lax.axis_size("cells")
    views = lax.axis_size("views")
    plan = send_plan[0, 0].T
    lists = tile_lists[0]
    tiles = lists.shape[0]
    rows_pix = tiles * cells // TILE_COLS * 16
    f32 = lambda *shape: jax.ShapeDtypeStruct(shape, F32)
    i32 = lambda *shape: jax.ShapeDtypeStruct(shape, I32)
    vmem = lambda *shape: pltpu.VMEM(shape, F32)

    wire = call(
        project_kernel,
        f32(192, LANES),
        [SMEM, VMEM, VMEM],
        [vmem(1024, LANES), vmem(144, LANES), pltpu.VMEM((16, LANES), I32)],
        60,
        (10_000_000, 600_000),
    )(cameras, params, plan)
    arrived = lax.all_to_all(wire.reshape(64, 1, 384), "cells", 0, 0, tiled=True)

    inverse = call(slots_kernel, i32(64, LANES), [SMEM], [], 8, (20_000_000, 50_000))(lists)

    basis, moment = pixel_constants()
    back = call(
        functools.partial(render_kernel, float(rows_pix)),
        f32(192, LANES),
        [SMEM, VMEM, VMEM, VMEM, VMEM, VMEM, VMEM],
        [
            vmem(144, LANES),
            vmem(512, LANES),
            vmem(512, 256),
            vmem(512, 384),
            vmem(512, 256),
            vmem(512, 256),
            pltpu.VMEM((4, 512, 256), BF16),
            vmem(512, LANES),
            vmem(144, LANES),
        ],
        32,
        (100_000_000, 300_000),
    )(
        lax.axis_index("cells").astype(I32).reshape(1),
        arrived.reshape(192, LANES),
        lists,
        inverse,
        jnp.swapaxes(target, 0, 1),
        basis,
        moment,
    )
    returned = lax.all_to_all(back.reshape(64, 1, 384), "cells", 0, 0, tiled=True)

    code, view = call(
        owner_kernel, (i32(16, LANES), f32(8, LANES)), [SMEM, SMEM], [], 8, (20_000_000, 50_000)
    )(cameras, plan)
    own = call(
        pull_kernel, f32(168, LANES), [VMEM, VMEM, VMEM], [vmem(144, LANES)], 8, (1_000_000, 200_000)
    )(returned.reshape(192, LANES), code, view)
    others = [
        lax.ppermute(own, "views", [(i, (i + k) % views) for i in range(views)]) for k in (1, 2, 3)
    ]
    shape = f32(*params.shape)
    return call(
        adam_kernel,
        (shape, shape, shape),
        [SMEM] + [VMEM] * 7,
        [vmem(1024, LANES), vmem(168 * 4, LANES)],
        24,
        (40_000_000, 3_500_000),
    )(
        lax.axis_index("views").astype(I32).reshape(1),
        own,
        *others,
        params,
        first_moment,
        second_moment,
    )


def solution(mesh):
    in_specs = (
        P(None, "cells"),
        P(None, "cells"),
        P(None, "cells"),
        P("views", None),
        P("views", "cells"),
        P("views", "cells", None, None),
        P("views", "cells", None),
        P("views", None, "cells"),
    )
    out_specs = (P(None, "cells"), P(None, "cells"), P(None, "cells"))
    return jax.shard_map(shards, mesh=mesh, in_specs=in_specs, out_specs=out_specs, check_vma=False)
```

```python
import functools

import jax
import jax.numpy as jnp
import numpy as np
from jax import lax
from jax.experimental import pallas as pl
from jax.experimental.pallas import tpu as pltpu
from jax.sharding import PartitionSpec as P

TILE_COLS = 32
ADAM_STEP = 1000
ROWS = 59
FEATS = 9
LANES = 128
LOG2E = 1.4426950408889634
ABSENT = -10000.0
KEYS = 48

harmonic_zero = 0.28209479177387814
harmonic_one = 0.4886025119029199
harmonic_two = (
    1.0925484305920792,
    -1.0925484305920792,
    0.31539156525252005,
    -1.0925484305920792,
    0.5462742152960396,
)
harmonic_three = (
    -0.5900435899266435,
    2.890611442640554,
    -0.4570457994644658,
    0.3731763325901154,
    -0.4570457994644658,
    1.445305721320277,
    -0.5900435899266435,
)

F32 = jnp.float32
BF16 = jnp.bfloat16
I32 = jnp.int32


def harmonics(across, upward, onward):
    across_sq = across * across
    upward_sq = upward * upward
    onward_sq = onward * onward
    return [
        None,
        -harmonic_one * upward,
        harmonic_one * onward,
        -harmonic_one * across,
        harmonic_two[0] * across * upward,
        harmonic_two[1] * upward * onward,
        harmonic_two[2] * (2.0 * onward_sq - across_sq - upward_sq),
        harmonic_two[3] * across * onward,
        harmonic_two[4] * (across_sq - upward_sq),
        harmonic_three[0] * upward * (3.0 * across_sq - upward_sq),
        harmonic_three[1] * across * upward * onward,
        harmonic_three[2] * upward * (4.0 * onward_sq - across_sq - upward_sq),
        harmonic_three[3] * onward * (2.0 * onward_sq - 3.0 * across_sq - 3.0 * upward_sq),
        harmonic_three[4] * across * (4.0 * onward_sq - across_sq - upward_sq),
        harmonic_three[5] * onward * (across_sq - upward_sq),
        harmonic_three[6] * across * (across_sq - 3.0 * upward_sq),
    ]


def rotation(roll, pitch, yaw):
    cr, sr = jnp.cos(roll), jnp.sin(roll)
    cp, sp = jnp.cos(pitch), jnp.sin(pitch)
    cy, sy = jnp.cos(yaw), jnp.sin(yaw)
    return [
        cy * cp,
        cy * sp * sr - sy * cr,
        cy * sp * cr + sy * sr,
        sy * cp,
        sy * sp * sr + cy * cr,
        sy * sp * cr - cy * sr,
        -sp,
        cp * sr,
        cp * cr,
    ]


def shape_basis(rows):
    scales = [jnp.exp(rows[3 + k]) for k in range(3)]
    qw, qx, qy, qz = rows[6], rows[7], rows[8], rows[9]
    norm = 1.0 / jnp.sqrt(qw * qw + qx * qx + qy * qy + qz * qz)
    qw, qx, qy, qz = qw * norm, qx * norm, qy * norm, qz * norm
    spin = [
        [1.0 - 2.0 * (qy * qy + qz * qz), 2.0 * (qx * qy - qw * qz), 2.0 * (qx * qz + qw * qy)],
        [2.0 * (qx * qy + qw * qz), 1.0 - 2.0 * (qx * qx + qz * qz), 2.0 * (qy * qz - qw * qx)],
        [2.0 * (qx * qz - qw * qy), 2.0 * (qy * qz + qw * qx), 1.0 - 2.0 * (qx * qx + qy * qy)],
    ]
    return [[spin[m][k] * scales[k] for k in range(3)] for m in range(3)]


def project_view(rows, basis, opacity, turn, centre):
    offset = [rows[k] - centre[k] for k in range(3)]
    seen = [
        turn[3 * m] * offset[0] + turn[3 * m + 1] * offset[1] + turn[3 * m + 2] * offset[2]
        for m in range(3)
    ]
    inv_depth = 1.0 / seen[2]
    col = seen[0] * inv_depth
    row = seen[1] * inv_depth
    cam = [
        [
            turn[3 * m] * basis[0][k] + turn[3 * m + 1] * basis[1][k] + turn[3 * m + 2] * basis[2][k]
            for k in range(3)
        ]
        for m in range(3)
    ]
    top = [(cam[0][k] - col * cam[2][k]) * inv_depth for k in range(3)]
    low = [(cam[1][k] - row * cam[2][k]) * inv_depth for k in range(3)]
    sa = top[0] * top[0] + top[1] * top[1] + top[2] * top[2]
    sb = top[0] * low[0] + top[1] * low[1] + top[2] * low[2]
    sc = low[0] * low[0] + low[1] * low[1] + low[2] * low[2]
    inv_det = 1.0 / (sa * sc - sb * sb)
    inv_dist = 1.0 / jnp.sqrt(
        offset[0] * offset[0] + offset[1] * offset[1] + offset[2] * offset[2]
    )
    harm = harmonics(offset[0] * inv_dist, offset[1] * inv_dist, offset[2] * inv_dist)
    colors = []
    for k in range(3):
        total = 0.5 + harmonic_zero * rows[11 + k]
        for j in range(1, 16):
            total = total + harm[j] * rows[11 + 3 * j + k]
        colors.append(total)
    return [col, row, sc * inv_det, -sb * inv_det, sa * inv_det, opacity, *colors]


def logistic(x):
    return 1.0 / (1.0 + jnp.exp(-x))


def block_transpose(four):
    lane = lax.broadcasted_iota(I32, (8, LANES), 1)
    low = lane < 64
    even = (lane & 32) == 0
    a, b, c, d = four
    a, c = jnp.where(low, a, pltpu.roll(c, 64, 1)), jnp.where(low, pltpu.roll(a, 64, 1), c)
    b, d = jnp.where(low, b, pltpu.roll(d, 64, 1)), jnp.where(low, pltpu.roll(b, 64, 1), d)
    a, b = jnp.where(even, a, pltpu.roll(b, 32, 1)), jnp.where(even, pltpu.roll(a, 96, 1), b)
    c, d = jnp.where(even, c, pltpu.roll(d, 32, 1)), jnp.where(even, pltpu.roll(c, 96, 1), d)
    return [a, b, c, d]


def wire_to_table(wire_ref, at, table_ref):
    for j in range(3):
        for h in range(2):
            four = [
                wire_ref[pl.ds(at + 3 * (32 * h + 8 * q) + j, 8, stride=3), :] for q in range(4)
            ]
            parts = block_transpose(four)
            for i in range(4):
                f = 4 * j + i
                if f < FEATS:
                    table_ref[16 * f + 8 * h : 16 * f + 8 * h + 8, :] = parts[i]


def table_to_wire(table, wire_ref):
    zero = jnp.zeros((8, LANES), F32)
    for j in range(3):
        for h in range(2):
            four = [table[4 * j + i][h] if 4 * j + i < FEATS else zero for i in range(4)]
            parts = block_transpose(four)
            for q in range(4):
                wire_ref[pl.ds(3 * (32 * h + 8 * q) + j, 8, stride=3), :] = parts[q]


def lookup(table_ref, feats, row, lane):
    found = [jnp.zeros((8, LANES), F32) for _ in range(feats)]
    for k in range(16):
        here = row == k
        for f in range(feats):
            source = jnp.broadcast_to(table_ref[16 * f + k : 16 * f + k + 1, :], (8, LANES))
            found[f] = jnp.where(here, jnp.take_along_axis(source, lane, axis=1, mode="promise_in_bounds"), found[f])
    return found


def to_dense(natural_ref, scratch_ref):
    for k in range(16):
        for a in range(8):
            high = min(8, ROWS - 8 * a)
            scratch_ref[64 * k + 8 * a : 64 * k + 8 * a + high, :] = natural_ref[
                8 * a : 8 * a + high, LANES * k : LANES * k + LANES
            ]


def dense_rows(scratch_ref):
    return [
        jnp.concatenate(
            [scratch_ref[pl.ds(512 * h + f, 8, stride=64), :] for h in range(2)], axis=0
        )
        for f in range(ROWS)
    ]


def project_kernel(camera_ref, params_ref, plan_ref, wire_ref, scratch_ref, table_ref, idx_ref):
    to_dense(params_ref, scratch_ref)
    rows = dense_rows(scratch_ref)
    angle = [jnp.full((8, LANES), camera_ref[0, k], F32) for k in range(3)]
    turn = [jnp.concatenate([t, t], axis=0) for t in rotation(*angle)]
    centre = [camera_ref[0, 3 + k] for k in range(3)]
    feats = project_view(rows, shape_basis(rows), logistic(rows[10]), turn, centre)
    for f in range(FEATS):
        table_ref[16 * f : 16 * f + 16, :] = feats[f]
    plan = jnp.maximum(plan_ref[...], 0).T
    for h in range(2):
        for q in range(4):
            idx_ref[8 * h : 8 * h + 8, 32 * q : 32 * q + 32] = plan[
                32 * h + 8 * q : 32 * h + 8 * q + 8, :
            ]
    out = [[None, None] for _ in range(FEATS)]
    for h in range(2):
        idx = idx_ref[8 * h : 8 * h + 8, :]
        found = lookup(table_ref, FEATS, idx >> 7, idx & 127)
        for f in range(FEATS):
            out[f][h] = found[f]
    table_to_wire(out, wire_ref)


def slots_kernel(lists_ref, inverse_ref):
    row = lax.broadcasted_iota(I32, (16, LANES), 0)
    lane = lax.broadcasted_iota(I32, (16, LANES), 1)
    device = 32 * (row >> 3) + 8 * (lane >> 5) + (row & 7)
    slot = 32 * device + (lane & 31)
    none = jnp.full((16, LANES), -1, I32)

    def tile_step(i, kept):
        s = i >> 2
        u = i & 3
        kept = list(kept)
        for jj in range(16):
            for t in range(4):
                e = lists_ref[t, 64 * s + 16 * u + jj]
                kept[t] = jnp.where(slot == e, LANES * u + 8 * jj + s, kept[t])
        return tuple(kept)

    kept = lax.fori_loop(0, 32, tile_step, (none,) * 4)
    for t in range(4):
        inverse_ref[16 * t : 16 * t + 16, :] = kept[t]


def owner_kernel(camera_ref, plan_ref, code_ref, view_ref):
    row = lax.broadcasted_iota(I32, (16, LANES), 0)
    lane = lax.broadcasted_iota(I32, (16, LANES), 1)
    gauss = row * LANES + lane

    def plan_step(d, kept):
        code = (8 * (d >> 5) + (d & 7)) * LANES + 32 * ((d >> 3) & 3)
        for c in range(32):
            kept = jnp.where(gauss == plan_ref[c, d], code + c, kept)
        return kept

    code_ref[...] = lax.fori_loop(0, 64, plan_step, jnp.full((16, LANES), -1, I32))
    angle = [jnp.full((8, LANES), camera_ref[0, k], F32) for k in range(3)]
    values = rotation(*angle) + [jnp.full((8, LANES), camera_ref[0, 3 + k], F32) for k in range(3)]
    lane = lax.broadcasted_iota(I32, (8, LANES), 1)
    view = jnp.zeros((8, LANES), F32)
    for k in range(12):
        view = jnp.where(lane == k, values[k], view)
    view_ref[...] = view


def pull_kernel(wire_ref, code_ref, view_ref, out_ref, table_ref):
    wire_to_table(wire_ref, 0, table_ref)
    for h in range(2):
        code = code_ref[8 * h : 8 * h + 8, :]
        found = lookup(table_ref, FEATS, code >> 7, code & 127)
        for f in range(FEATS):
            out_ref[16 * f + 8 * h : 16 * f + 8 * h + 8, :] = found[f]
        out_ref[144 + 8 * h : 152 + 8 * h, :] = jnp.where(code >= 0, 1.0, 0.0)
    out_ref[160:168, :] = view_ref[...]


def split(x, parts):
    done = []
    for _ in range(parts - 1):
        high = x.astype(BF16).astype(F32)
        done.append(high)
        x = x - high
    done.append(x)
    return done


def sublane_shift(x, by, fill):
    s = lax.broadcasted_iota(I32, x.shape, 0)
    moved = pltpu.roll(x, by % 8, 0)
    return jnp.where((s >= by) if by > 0 else (s < 8 + by), moved, fill)


def render_kernel(
    device_rows,
    place_ref,
    wire_ref,
    lists_ref,
    inverse_ref,
    target_ref,
    basis_ref,
    moment_ref,
    out_ref,
    table_ref,
    lhs_ref,
    power_ref,
    left_ref,
    alpha_ref,
    weight_ref,
    slope_ref,
    shade_ref,
    part_ref,
    sums_ref,
    grads_ref,
):
    device = place_ref[0]
    rows_pix = device_rows
    wire_to_table(wire_ref, 0, table_ref)

    sub = lax.broadcasted_iota(I32, (8, LANES), 0)
    lane = lax.broadcasted_iota(I32, (8, LANES), 1)
    entry = []
    for h in range(2):
        e = jnp.zeros((8, LANES), I32)
        for w in range(4):
            at = slice(LANES * w, LANES * w + LANES)
            lists = jnp.where(
                sub < 4,
                jnp.broadcast_to(lists_ref[2 * h : 2 * h + 1, at], (8, LANES)),
                jnp.broadcast_to(lists_ref[2 * h + 1 : 2 * h + 2, at], (8, LANES)),
            )
            source = 64 * (lane & 1) + 16 * (sub & 3) + (lane >> 3)
            moved = jnp.take_along_axis(lists, source, axis=1, mode="promise_in_bounds")
            e = jnp.where((lane & 7) >> 1 == w, moved, e)
        entry.append(e)
    feats = [[None, None] for _ in range(FEATS)]
    for h in range(2):
        e = jnp.maximum(entry[h], 0)
        row = 8 * ((e >> 10) & 1) + ((e >> 5) & 7)
        lane = 32 * ((e >> 8) & 3) + (e & 31)
        found = lookup(table_ref, FEATS, row, lane)
        for f in range(FEATS):
            feats[f][h] = found[f]
    feats = [jnp.concatenate(two, axis=0) for two in feats]
    live = jnp.concatenate(entry, axis=0) >= 0
    col, scr, c0, c1, c2, opacity = feats[:6]

    block_cols = TILE_COLS // 4
    tile_col = (
        4 * (device % block_cols) + lax.broadcasted_iota(I32, (16, LANES), 0) // 4
    ).astype(F32)
    tile_row = (device // block_cols).astype(F32)
    screen = TILE_COLS * 8.0
    ex = (16.0 * tile_col + 8.0 - screen) - screen * col
    ey = (16.0 * tile_row + 8.0 - rows_pix * 0.5) - screen * scr
    factor = -0.5 * LOG2E / (screen * screen)
    a = factor * c0
    b = (2.0 * factor) * c1
    c = factor * c2
    bx = b * ex
    by = b * ey
    coeffs = [
        a,
        b,
        c,
        2.0 * a * ex + by,
        bx + 2.0 * c * ey,
        (a * ex + by) * ex + c * ey * ey + LOG2E * jnp.log(opacity),
    ]
    rest = [0.0, 0.0, 0.0, 0.0, 0.0, ABSENT]
    lines = []
    pieces = [split(jnp.where(live, x, r), 3) for x, r in zip(coeffs, rest)]
    for part in range(3):
        lines += [pieces[k][part] for k in range(6)]
    tints = [split(feats[6 + k], 3) for k in range(3)]
    tints = [tints[k][part] for part in range(3) for k in range(3)]
    lines += tints * 3 + feats[6:9]
    for k in range(KEYS):
        for h in range(2):
            lhs_ref[pl.ds(8 * KEYS * h + k, 8, stride=KEYS), :] = lines[k][8 * h : 8 * h + 8, :]

    one = jnp.ones((8, LANES), F32)
    zero = jnp.zeros((8, LANES), F32)
    spans = [(t, p) for t in range(4) for p in range(2)]

    def place(t, j):
        start = 512 * (j // 16) + 128 * t + 8 * (j % 16)
        return slice(start, start + 8)

    def chunk(t, u):
        return slice(512 * u + 128 * t, 512 * u + 128 * t + 128)

    def half(p):
        return slice(LANES * p, LANES * p + LANES)

    trans = {tp: one for tp in spans}
    image = {tp: [zero] * 3 for tp in spans}
    before, behind, rights, shades = {}, {}, {}, {}
    pad = jnp.zeros((1, 256), F32)
    for u in range(4):
        columns = []
        for t in range(4):
            lines = lhs_ref[KEYS * (4 * t + u) : KEYS * (4 * t + u) + KEYS, :].T
            columns.append(lines)
            left_ref[chunk(t, u), :] = lines.astype(BF16)
        power_ref[512 * u : 512 * u + 512, :] = jnp.dot(
            left_ref[512 * u : 512 * u + 512, :], basis_ref[...], preferred_element_type=F32
        )
        for j in range(16 * u, 16 * u + 16):
            for t in range(4):
                here = place(t, j)
                at = 8 * (j % 16)
                tint = [
                    jnp.broadcast_to(columns[t][at : at + 8, 45 + k : 46 + k], (8, LANES))
                    for k in range(3)
                ]
                for p in range(2):
                    alpha = jnp.exp2(power_ref[here, half(p)])
                    alpha_ref[here, half(p)] = alpha
                    weight = alpha * trans[t, p]
                    weight_ref[here, half(p)] = weight
                    trans[t, p] = trans[t, p] - weight
                    image[t, p] = [image[t, p][k] + weight * tint[k] for k in range(3)]

    for t in range(4):
        slopes = []
        for p in range(2):
            kept = trans[t, p]
            lead = sublane_shift(kept, 1, 1.0)
            for by_ in (1, 2, 4):
                lead = lead * sublane_shift(lead, by_, 1.0)
            before[t, p] = lead
            slope = []
            for k in range(3):
                shown = jnp.sum(lead * image[t, p][k], axis=0, keepdims=True)
                goal = target_ref[k, :, 256 * t + 128 * p : 256 * t + 128 * p + 128]
                slope.append(2.0 * (shown - goal))
            slopes.append(slope)
            add = sum(slope[k] * image[t, p][k] for k in range(3))
            mul = kept
            for by_ in (1, 2, 4):
                add = add + mul * sublane_shift(add, -by_, 0.0)
                mul = mul * sublane_shift(mul, -by_, 1.0)
            behind[t, p] = sublane_shift(add, -1, 0.0)
        parts = [
            split(jnp.concatenate([slopes[0][k], slopes[1][k]], axis=1), 3) for k in range(3)
        ]
        rows = [pad] * 18
        for part in range(3):
            rows += [parts[k][part] for _ in range(3) for k in range(3)]
        rights[t] = (jnp.concatenate(rows + [pad] * 3, axis=0).astype(BF16))
        nine = [parts[k][part] for part in range(3) for k in range(3)]
        shades[t] = (jnp.concatenate([pad] * 16 + nine + [pad] * 7, axis=0).T.astype(BF16))

    for t in range(4):
        left = jnp.concatenate([left_ref[chunk(t, u), :] for u in range(4)], axis=0)
        rest = jnp.dot(left, rights[t], preferred_element_type=F32)
        for u in range(4):
            power_ref[chunk(t, u), :] = rest[128 * u : 128 * u + 128, :]
    for u in (3, 2, 1, 0):
        for i in range(8 * u + 7, 8 * u - 1, -1):
            for t, p in spans:
                pair = [None, None]
                rest = behind[t, p]
                for o in (1, 0):
                    here = place(t, 2 * i + o)
                    weight = weight_ref[here, half(p)] * before[t, p]
                    gap = power_ref[here, half(p)] - rest
                    rest = rest + alpha_ref[here, half(p)] * gap
                    pair[o] = (weight * gap, weight)
                behind[t, p] = rest
                first = place(t, 2 * i).start
                for n, ref in enumerate((slope_ref, shade_ref)):
                    value = jnp.concatenate([pair[0][n], pair[1][n]], axis=0)
                    high = value.astype(BF16)
                    ref[first : first + 16, half(p)] = high
                    ref[first : first + 16, half(2 + p)] = (value - high.astype(F32)).astype(BF16)
        part_ref[512 * u : 512 * u + 512, :] = jnp.dot(
            slope_ref[512 * u : 512 * u + 512, :], moment_ref[...], preferred_element_type=F32
        )
    for t in range(4):
        weights = jnp.concatenate([shade_ref[chunk(t, u), :] for u in range(4)], axis=0)
        shaded = jnp.dot(
            weights, jnp.concatenate([shades[t]] * 2, axis=0), preferred_element_type=F32
        )
        for u in range(4):
            total = part_ref[chunk(t, u), :] + shaded[128 * u : 128 * u + 128, :]
            sums_ref[32 * (4 * t + u) : 32 * (4 * t + u) + 32, :] = total.T

    def summed(k):
        return jnp.concatenate(
            [sums_ref[pl.ds(256 * h + k, 8, stride=32), :] for h in range(2)], axis=0
        )

    mxx, mxy, myy, mx, my, m0 = [summed(k) for k in range(6)]
    sx = ex * m0 + mx
    sy = ey * m0 + my
    sxx = ex * (ex * m0 + 2.0 * mx) + mxx
    sxy = ex * (ey * m0 + my) + ey * mx + mxy
    syy = ey * (ey * m0 + 2.0 * my) + myy
    unit = 1.0 / screen
    grads = [
        (c0 * sx + c1 * sy) * unit,
        (c1 * sx + c2 * sy) * unit,
        (-0.5 * unit * unit) * sxx,
        (-unit * unit) * sxy,
        (-0.5 * unit * unit) * syy,
        m0 / opacity,
    ]
    for k in range(3):
        grads.append(summed(16 + k) + summed(19 + k) + summed(22 + k))
    for f in range(FEATS):
        grads_ref[16 * f : 16 * f + 16, :] = grads[f]

    out = [[None, None] for _ in range(FEATS)]
    for h in range(2):
        total = [jnp.zeros((8, LANES), F32) for _ in range(FEATS)]
        for t in range(4):
            code = inverse_ref[16 * t + 8 * h : 16 * t + 8 * h + 8, :]
            row = code >> 7
            lane = code & 127
            found = [jnp.zeros((8, LANES), F32) for _ in range(FEATS)]
            for u in range(4):
                here = row == u
                for f in range(FEATS):
                    at = 16 * f + 4 * t + u
                    source = jnp.broadcast_to(grads_ref[at : at + 1, :], (8, LANES))
                    found[f] = jnp.where(
                        here, jnp.take_along_axis(source, lane, axis=1, mode="promise_in_bounds"), found[f]
                    )
            total = [x + y for x, y in zip(total, found)]
        for f in range(FEATS):
            out[f][h] = total[f]
    table_to_wire(out, out_ref)


def adam_kernel(
    place_ref,
    own_ref,
    one_ref,
    two_ref,
    three_ref,
    params_ref,
    first_ref,
    second_ref,
    new_params_ref,
    new_first_ref,
    new_second_ref,
    scratch_ref,
    pulled_ref,
):
    for k, ref in enumerate((own_ref, one_ref, two_ref, three_ref)):
        at = pl.multiple_of(168 * ((place_ref[0] - k) & 3), 8)
        pulled_ref[pl.ds(at, 168), :] = ref[...]
    to_dense(params_ref, scratch_ref)
    rows = dense_rows(scratch_ref)
    seen = jnp.zeros((16, LANES), F32)
    cotangents = []
    cams = []
    for v in range(4):
        at = 168 * v
        cotangents.append(
            [pulled_ref[at + 16 * f : at + 16 * f + 16, :] for f in range(FEATS)]
        )
        seen = seen + pulled_ref[at + 144 : at + 160, :]
        cams.append(
            [
                jnp.broadcast_to(pulled_ref[at + 160 : at + 161, k : k + 1], (16, LANES))
                for k in range(12)
            ]
        )

    def all_views(values):
        basis = shape_basis(values)
        opacity = logistic(values[10])
        return [project_view(values, basis, opacity, cam[:9], cam[9:]) for cam in cams]

    _, pull = jax.vjp(all_views, rows)
    gradient = pull(cotangents)[0]
    for f in range(ROWS):
        for h in range(2):
            scratch_ref[pl.ds(512 * h + f, 8, stride=64), :] = gradient[f][8 * h : 8 * h + 8, :]
    bias_one = 1.0 - 0.9**ADAM_STEP
    bias_two = 1.0 - 0.999**ADAM_STEP
    for a in range(8):
        high = min(8, ROWS - 8 * a)
        row = lax.broadcasted_iota(I32, (high, LANES), 0) + 8 * a
        rate = jnp.where(
            row < 6,
            0.01,
            jnp.where(row < 10, 0.005, jnp.where(row < 11, 0.05, jnp.where(row < 14, 0.0025, 0.000125))),
        ).astype(F32) * (1.0 / bias_one)
        for k in range(16):
            at = (slice(8 * a, 8 * a + high), slice(LANES * k, LANES * k + LANES))
            grad = scratch_ref[64 * k + 8 * a : 64 * k + 8 * a + high, :]
            here = jnp.broadcast_to(seen[k : k + 1, :], (high, LANES)) > 0.0
            p, m, s = params_ref[at], first_ref[at], second_ref[at]
            m_new = 0.9 * m + 0.1 * grad
            s_new = 0.999 * s + 0.001 * grad * grad
            stride = rate * m_new / (jnp.sqrt(s_new * (1.0 / bias_two)) + 1e-08)
            new_params_ref[at] = jnp.where(here, p - stride, p)
            new_first_ref[at] = jnp.where(here, m_new, m)
            new_second_ref[at] = jnp.where(here, s_new, s)


def pixel_constants():
    pixel = np.arange(256)
    x = pixel % 16 - 7.5
    y = pixel // 16 - 7.5
    six = np.stack([x * x, x * y, y * y, x, y, np.ones(256)])
    basis = np.zeros((KEYS, 256), np.float32)
    for part in range(3):
        basis[6 * part : 6 * part + 6] = six
    moment = np.zeros((512, 32), np.float32)
    moment[:256, :6] = six.T
    moment[256:, :6] = six.T
    return jnp.asarray(basis, BF16), jnp.asarray(moment, BF16)


VMEM = pl.BlockSpec(memory_space=pltpu.VMEM)
SMEM = pl.BlockSpec(memory_space=pltpu.SMEM)


def call(kernel, outs, ins, scratch, megabytes, cost):
    flops, moved = cost
    return pl.pallas_call(
        kernel,
        out_shape=outs,
        in_specs=ins,
        out_specs=jax.tree.map(lambda _: VMEM, outs),
        scratch_shapes=scratch,
        compiler_params=pltpu.CompilerParams(vmem_limit_bytes=megabytes << 20),
        cost_estimate=pl.CostEstimate(flops=flops, bytes_accessed=moved, transcendentals=0),
    )


def render(rows_pix):
    vmem = lambda *shape: pltpu.VMEM(shape, F32)
    return call(
        functools.partial(render_kernel, float(rows_pix)),
        jax.ShapeDtypeStruct((192, LANES), F32),
        [SMEM, VMEM, VMEM, VMEM, VMEM, VMEM, VMEM],
        [
            vmem(144, LANES),
            vmem(16 * KEYS, LANES),
            vmem(2048, 256),
            pltpu.VMEM((2048, KEYS), BF16),
            vmem(2048, 256),
            vmem(2048, 256),
            pltpu.VMEM((2048, 512), BF16),
            pltpu.VMEM((2048, 512), BF16),
            vmem(2048, 32),
            vmem(512, LANES),
            vmem(144, LANES),
        ],
        32,
        (100_000_000, 300_000),
    )


def shards(params, first_moment, second_moment, cameras, visible, send_plan, tile_lists, target):
    del visible
    cells = lax.axis_size("cells")
    views = lax.axis_size("views")
    plan = send_plan[0, 0].T
    lists = tile_lists[0]
    tiles = lists.shape[0]
    rows_pix = tiles * cells // TILE_COLS * 16
    f32 = lambda *shape: jax.ShapeDtypeStruct(shape, F32)
    i32 = lambda *shape: jax.ShapeDtypeStruct(shape, I32)
    vmem = lambda *shape: pltpu.VMEM(shape, F32)

    wire = call(
        project_kernel,
        f32(192, LANES),
        [SMEM, VMEM, VMEM],
        [vmem(1024, LANES), vmem(144, LANES), pltpu.VMEM((16, LANES), I32)],
        60,
        (10_000_000, 600_000),
    )(cameras, params, plan)
    arrived = lax.all_to_all(wire.reshape(64, 1, 384), "cells", 0, 0, tiled=True)

    inverse = call(slots_kernel, i32(64, LANES), [SMEM], [], 8, (20_000_000, 50_000))(lists)

    basis, moment = pixel_constants()
    back = render(rows_pix)(
        lax.axis_index("cells").astype(I32).reshape(1),
        arrived.reshape(192, LANES),
        lists,
        inverse,
        jnp.swapaxes(target, 0, 1),
        basis,
        moment,
    )
    returned = lax.all_to_all(back.reshape(64, 1, 384), "cells", 0, 0, tiled=True)

    code, view = call(
        owner_kernel, (i32(16, LANES), f32(8, LANES)), [SMEM, SMEM], [], 8, (20_000_000, 50_000)
    )(cameras, plan)
    own = call(
        pull_kernel, f32(168, LANES), [VMEM, VMEM, VMEM], [vmem(144, LANES)], 8, (1_000_000, 200_000)
    )(returned.reshape(192, LANES), code, view)
    others = [
        lax.ppermute(own, "views", [(i, (i + k) % views) for i in range(views)]) for k in (1, 2, 3)
    ]
    shape = f32(*params.shape)
    return call(
        adam_kernel,
        (shape, shape, shape),
        [SMEM] + [VMEM] * 7,
        [vmem(1024, LANES), vmem(168 * 4, LANES)],
        24,
        (40_000_000, 3_500_000),
    )(
        lax.axis_index("views").astype(I32).reshape(1),
        own,
        *others,
        params,
        first_moment,
        second_moment,
    )


def solution(mesh):
    in_specs = (
        P(None, "cells"),
        P(None, "cells"),
        P(None, "cells"),
        P("views", None),
        P("views", "cells"),
        P("views", "cells", None, None),
        P("views", "cells", None),
        P("views", None, "cells"),
    )
    out_specs = (P(None, "cells"), P(None, "cells"), P(None, "cells"))
    return jax.shard_map(shards, mesh=mesh, in_specs=in_specs, out_specs=out_specs, check_vma=False)
```

```python
import functools

import jax
import jax.numpy as jnp
import numpy as np
from jax import lax
from jax.experimental import pallas as pl
from jax.experimental.pallas import tpu as pltpu
from jax.sharding import PartitionSpec as P

TILE_COLS = 32
ADAM_STEP = 1000
ROWS = 59
FEATS = 9
LANES = 128
LOG2E = 1.4426950408889634
ABSENT = -10000.0
KEYS = 48

harmonic_zero = 0.28209479177387814
harmonic_one = 0.4886025119029199
harmonic_two = (
    1.0925484305920792,
    -1.0925484305920792,
    0.31539156525252005,
    -1.0925484305920792,
    0.5462742152960396,
)
harmonic_three = (
    -0.5900435899266435,
    2.890611442640554,
    -0.4570457994644658,
    0.3731763325901154,
    -0.4570457994644658,
    1.445305721320277,
    -0.5900435899266435,
)

F32 = jnp.float32
BF16 = jnp.bfloat16
I32 = jnp.int32


def harmonics(across, upward, onward):
    across_sq = across * across
    upward_sq = upward * upward
    onward_sq = onward * onward
    return [
        None,
        -harmonic_one * upward,
        harmonic_one * onward,
        -harmonic_one * across,
        harmonic_two[0] * across * upward,
        harmonic_two[1] * upward * onward,
        harmonic_two[2] * (2.0 * onward_sq - across_sq - upward_sq),
        harmonic_two[3] * across * onward,
        harmonic_two[4] * (across_sq - upward_sq),
        harmonic_three[0] * upward * (3.0 * across_sq - upward_sq),
        harmonic_three[1] * across * upward * onward,
        harmonic_three[2] * upward * (4.0 * onward_sq - across_sq - upward_sq),
        harmonic_three[3] * onward * (2.0 * onward_sq - 3.0 * across_sq - 3.0 * upward_sq),
        harmonic_three[4] * across * (4.0 * onward_sq - across_sq - upward_sq),
        harmonic_three[5] * onward * (across_sq - upward_sq),
        harmonic_three[6] * across * (across_sq - 3.0 * upward_sq),
    ]


def rotation(roll, pitch, yaw):
    cr, sr = jnp.cos(roll), jnp.sin(roll)
    cp, sp = jnp.cos(pitch), jnp.sin(pitch)
    cy, sy = jnp.cos(yaw), jnp.sin(yaw)
    return [
        cy * cp,
        cy * sp * sr - sy * cr,
        cy * sp * cr + sy * sr,
        sy * cp,
        sy * sp * sr + cy * cr,
        sy * sp * cr - cy * sr,
        -sp,
        cp * sr,
        cp * cr,
    ]


def shape_basis(rows):
    scales = [jnp.exp(rows[3 + k]) for k in range(3)]
    qw, qx, qy, qz = rows[6], rows[7], rows[8], rows[9]
    norm = 1.0 / jnp.sqrt(qw * qw + qx * qx + qy * qy + qz * qz)
    qw, qx, qy, qz = qw * norm, qx * norm, qy * norm, qz * norm
    spin = [
        [1.0 - 2.0 * (qy * qy + qz * qz), 2.0 * (qx * qy - qw * qz), 2.0 * (qx * qz + qw * qy)],
        [2.0 * (qx * qy + qw * qz), 1.0 - 2.0 * (qx * qx + qz * qz), 2.0 * (qy * qz - qw * qx)],
        [2.0 * (qx * qz - qw * qy), 2.0 * (qy * qz + qw * qx), 1.0 - 2.0 * (qx * qx + qy * qy)],
    ]
    return [[spin[m][k] * scales[k] for k in range(3)] for m in range(3)]


def project_view(rows, basis, turn, centre):
    offset = [rows[k] - centre[k] for k in range(3)]
    seen = [
        turn[3 * m] * offset[0] + turn[3 * m + 1] * offset[1] + turn[3 * m + 2] * offset[2]
        for m in range(3)
    ]
    inv_depth = 1.0 / seen[2]
    col = seen[0] * inv_depth
    row = seen[1] * inv_depth
    cam = [
        [
            turn[3 * m] * basis[0][k] + turn[3 * m + 1] * basis[1][k] + turn[3 * m + 2] * basis[2][k]
            for k in range(3)
        ]
        for m in range(3)
    ]
    top = [(cam[0][k] - col * cam[2][k]) * inv_depth for k in range(3)]
    low = [(cam[1][k] - row * cam[2][k]) * inv_depth for k in range(3)]
    sa = top[0] * top[0] + top[1] * top[1] + top[2] * top[2]
    sb = top[0] * low[0] + top[1] * low[1] + top[2] * low[2]
    sc = low[0] * low[0] + low[1] * low[1] + low[2] * low[2]
    inv_det = 1.0 / (sa * sc - sb * sb)
    return [col, row, sc * inv_det, -sb * inv_det, sa * inv_det]


def color_view(rows, centre):
    offset = [rows[k] - centre[k] for k in range(3)]
    inv_dist = 1.0 / jnp.sqrt(
        offset[0] * offset[0] + offset[1] * offset[1] + offset[2] * offset[2]
    )
    harm = harmonics(offset[0] * inv_dist, offset[1] * inv_dist, offset[2] * inv_dist)
    colors = []
    for k in range(3):
        total = 0.5 + harmonic_zero * rows[11 + k]
        for j in range(1, 16):
            total = total + harm[j] * rows[11 + 3 * j + k]
        colors.append(total)
    return colors


def logistic(x):
    return 1.0 / (1.0 + jnp.exp(-x))


def block_transpose(four):
    lane = lax.broadcasted_iota(I32, (8, LANES), 1)
    low = lane < 64
    even = (lane & 32) == 0
    a, b, c, d = four
    a, c = jnp.where(low, a, pltpu.roll(c, 64, 1)), jnp.where(low, pltpu.roll(a, 64, 1), c)
    b, d = jnp.where(low, b, pltpu.roll(d, 64, 1)), jnp.where(low, pltpu.roll(b, 64, 1), d)
    a, b = jnp.where(even, a, pltpu.roll(b, 32, 1)), jnp.where(even, pltpu.roll(a, 96, 1), b)
    c, d = jnp.where(even, c, pltpu.roll(d, 32, 1)), jnp.where(even, pltpu.roll(c, 96, 1), d)
    return [a, b, c, d]


def wire_to_table(wire_ref, at, table_ref):
    for j in range(3):
        for h in range(2):
            four = [
                wire_ref[pl.ds(at + 3 * (32 * h + 8 * q) + j, 8, stride=3), :] for q in range(4)
            ]
            parts = block_transpose(four)
            for i in range(4):
                f = 4 * j + i
                if f < FEATS:
                    table_ref[16 * f + 8 * h : 16 * f + 8 * h + 8, :] = parts[i]


def table_to_wire(table, wire_ref):
    zero = jnp.zeros((8, LANES), F32)
    for j in range(3):
        for h in range(2):
            four = [table[4 * j + i][h] if 4 * j + i < FEATS else zero for i in range(4)]
            parts = block_transpose(four)
            for q in range(4):
                wire_ref[pl.ds(3 * (32 * h + 8 * q) + j, 8, stride=3), :] = parts[q]


def lookup(table_ref, feats, row, lane):
    found = [jnp.zeros((8, LANES), F32) for _ in range(feats)]
    for k in range(16):
        here = row == k
        for f in range(feats):
            source = jnp.broadcast_to(table_ref[16 * f + k : 16 * f + k + 1, :], (8, LANES))
            found[f] = jnp.where(here, jnp.take_along_axis(source, lane, axis=1, mode="promise_in_bounds"), found[f])
    return found


def to_dense(natural_ref, scratch_ref):
    for k in range(16):
        for a in range(8):
            high = min(8, ROWS - 8 * a)
            scratch_ref[64 * k + 8 * a : 64 * k + 8 * a + high, :] = natural_ref[
                8 * a : 8 * a + high, LANES * k : LANES * k + LANES
            ]


def dense_rows(scratch_ref):
    return [
        jnp.concatenate(
            [scratch_ref[pl.ds(512 * h + f, 8, stride=64), :] for h in range(2)], axis=0
        )
        for f in range(ROWS)
    ]


def project_kernel(camera_ref, params_ref, plan_ref, wire_ref, scratch_ref, table_ref, idx_ref):
    to_dense(params_ref, scratch_ref)
    rows = dense_rows(scratch_ref)
    angle = [jnp.full((8, LANES), camera_ref[0, k], F32) for k in range(3)]
    turn = [jnp.concatenate([t, t], axis=0) for t in rotation(*angle)]
    centre = [camera_ref[0, 3 + k] for k in range(3)]
    feats = project_view(rows, shape_basis(rows), turn, centre) + [logistic(rows[10])]
    feats += color_view(rows, centre)
    for f in range(FEATS):
        table_ref[16 * f : 16 * f + 16, :] = feats[f]
    plan = jnp.maximum(plan_ref[...], 0).T
    for h in range(2):
        for q in range(4):
            idx_ref[8 * h : 8 * h + 8, 32 * q : 32 * q + 32] = plan[
                32 * h + 8 * q : 32 * h + 8 * q + 8, :
            ]
    out = [[None, None] for _ in range(FEATS)]
    for h in range(2):
        idx = idx_ref[8 * h : 8 * h + 8, :]
        found = lookup(table_ref, FEATS, idx >> 7, idx & 127)
        for f in range(FEATS):
            out[f][h] = found[f]
    table_to_wire(out, wire_ref)


def slots_kernel(lists_ref, inverse_ref):
    row = lax.broadcasted_iota(I32, (16, LANES), 0)
    lane = lax.broadcasted_iota(I32, (16, LANES), 1)
    device = 32 * (row >> 3) + 8 * (lane >> 5) + (row & 7)
    slot = 32 * device + (lane & 31)
    none = jnp.full((16, LANES), -1, I32)

    def tile_step(i, kept):
        s = i >> 2
        u = i & 3
        kept = list(kept)
        for jj in range(16):
            for t in range(4):
                e = lists_ref[t, 64 * s + 16 * u + jj]
                kept[t] = jnp.where(slot == e, LANES * u + 8 * jj + s, kept[t])
        return tuple(kept)

    kept = lax.fori_loop(0, 32, tile_step, (none,) * 4)
    for t in range(4):
        inverse_ref[16 * t : 16 * t + 16, :] = kept[t]


def owner_kernel(camera_ref, plan_ref, code_ref, view_ref):
    row = lax.broadcasted_iota(I32, (16, LANES), 0)
    lane = lax.broadcasted_iota(I32, (16, LANES), 1)
    gauss = row * LANES + lane

    def plan_step(d, kept):
        code = (8 * (d >> 5) + (d & 7)) * LANES + 32 * ((d >> 3) & 3)
        for c in range(32):
            kept = jnp.where(gauss == plan_ref[c, d], code + c, kept)
        return kept

    code_ref[...] = lax.fori_loop(0, 64, plan_step, jnp.full((16, LANES), -1, I32))
    angle = [jnp.full((8, LANES), camera_ref[0, k], F32) for k in range(3)]
    values = rotation(*angle) + [jnp.full((8, LANES), camera_ref[0, 3 + k], F32) for k in range(3)]
    lane = lax.broadcasted_iota(I32, (8, LANES), 1)
    view = jnp.zeros((8, LANES), F32)
    for k in range(12):
        view = jnp.where(lane == k, values[k], view)
    view_ref[...] = view


def pull_kernel(wire_ref, code_ref, view_ref, out_ref, table_ref):
    wire_to_table(wire_ref, 0, table_ref)
    for h in range(2):
        code = code_ref[8 * h : 8 * h + 8, :]
        found = lookup(table_ref, FEATS, code >> 7, code & 127)
        for f in range(FEATS):
            out_ref[16 * f + 8 * h : 16 * f + 8 * h + 8, :] = found[f]
        out_ref[144 + 8 * h : 152 + 8 * h, :] = jnp.where(code >= 0, 1.0, 0.0)
    out_ref[160:168, :] = view_ref[...]


def split(x, parts):
    done = []
    for _ in range(parts - 1):
        high = x.astype(BF16).astype(F32)
        done.append(high)
        x = x - high
    done.append(x)
    return done


def sublane_shift(x, by, fill):
    s = lax.broadcasted_iota(I32, x.shape, 0)
    moved = pltpu.roll(x, by % 8, 0)
    return jnp.where((s >= by) if by > 0 else (s < 8 + by), moved, fill)


def render_kernel(
    device_rows,
    place_ref,
    wire_ref,
    lists_ref,
    inverse_ref,
    target_ref,
    basis_ref,
    moment_ref,
    out_ref,
    table_ref,
    lhs_ref,
    power_ref,
    left_ref,
    color_ref,
    alpha_ref,
    weight_ref,
    slope_ref,
    shade_ref,
    part_ref,
    sums_ref,
    grads_ref,
):
    device = place_ref[0]
    rows_pix = device_rows
    wire_to_table(wire_ref, 0, table_ref)

    sub = lax.broadcasted_iota(I32, (8, LANES), 0)
    lane = lax.broadcasted_iota(I32, (8, LANES), 1)
    entry = []
    for h in range(2):
        e = jnp.zeros((8, LANES), I32)
        for w in range(4):
            at = slice(LANES * w, LANES * w + LANES)
            lists = jnp.where(
                sub < 4,
                jnp.broadcast_to(lists_ref[2 * h : 2 * h + 1, at], (8, LANES)),
                jnp.broadcast_to(lists_ref[2 * h + 1 : 2 * h + 2, at], (8, LANES)),
            )
            source = 64 * (lane & 1) + 16 * (sub & 3) + (lane >> 3)
            moved = jnp.take_along_axis(lists, source, axis=1, mode="promise_in_bounds")
            e = jnp.where((lane & 7) >> 1 == w, moved, e)
        entry.append(e)
    feats = [[None, None] for _ in range(FEATS)]
    for h in range(2):
        e = jnp.maximum(entry[h], 0)
        row = 8 * ((e >> 10) & 1) + ((e >> 5) & 7)
        lane = 32 * ((e >> 8) & 3) + (e & 31)
        found = lookup(table_ref, FEATS, row, lane)
        for f in range(FEATS):
            feats[f][h] = found[f]
    feats = [jnp.concatenate(two, axis=0) for two in feats]
    live = jnp.concatenate(entry, axis=0) >= 0
    col, scr, c0, c1, c2, opacity = feats[:6]

    block_cols = TILE_COLS // 4
    tile_col = (
        4 * (device % block_cols) + lax.broadcasted_iota(I32, (16, LANES), 0) // 4
    ).astype(F32)
    tile_row = (device // block_cols).astype(F32)
    screen = TILE_COLS * 8.0
    ex = (16.0 * tile_col + 8.0 - screen) - screen * col
    ey = (16.0 * tile_row + 8.0 - rows_pix * 0.5) - screen * scr
    factor = -0.5 * LOG2E / (screen * screen)
    a = factor * c0
    b = (2.0 * factor) * c1
    c = factor * c2
    bx = b * ex
    by = b * ey
    coeffs = [
        a,
        b,
        c,
        2.0 * a * ex + by,
        bx + 2.0 * c * ey,
        (a * ex + by) * ex + c * ey * ey + LOG2E * jnp.log(opacity),
    ]
    rest = [0.0, 0.0, 0.0, 0.0, 0.0, ABSENT]
    lines = []
    pieces = [split(jnp.where(live, x, r), 3) for x, r in zip(coeffs, rest)]
    for part in range(3):
        lines += [pieces[k][part] for k in range(6)]
    tints = [split(feats[6 + k], 3) for k in range(3)]
    tints = [tints[k][part] for part in range(3) for k in range(3)]
    lines += tints * 3 + [feats[6]] + [jnp.zeros((16, LANES), F32)] * 2
    for k in range(KEYS):
        for h in range(2):
            lhs_ref[pl.ds(8 * KEYS * h + k, 8, stride=KEYS), :] = lines[k][8 * h : 8 * h + 8, :]

    one = jnp.ones((8, LANES), F32)
    zero = jnp.zeros((8, LANES), F32)
    spans = [(t, p) for t in range(4) for p in range(2)]

    def place(t, j):
        start = 512 * (j // 16) + 128 * t + 8 * (j % 16)
        return slice(start, start + 8)

    def chunk(t, u):
        return slice(512 * u + 128 * t, 512 * u + 128 * t + 128)

    def half(p):
        return slice(LANES * p, LANES * p + LANES)

    trans = {tp: one for tp in spans}
    image = {tp: [zero] * 3 for tp in spans}
    before, behind, rights, shades = {}, {}, {}, {}
    pad = jnp.zeros((1, 256), F32)
    for u in range(4):
        columns = []
        for t in range(4):
            lines = lhs_ref[KEYS * (4 * t + u) : KEYS * (4 * t + u) + KEYS, :].T
            columns.append(lines)
            left_ref[chunk(t, u), :] = lines.astype(BF16)
        both = jnp.dot(
            left_ref[512 * u : 512 * u + 512, :], basis_ref[...], preferred_element_type=F32
        )
        power_ref[512 * u : 512 * u + 512, :] = both[:, 0:256]
        color_ref[512 * u : 512 * u + 512, :] = both[:, 256:512]
        for j in range(16 * u, 16 * u + 16):
            for t in range(4):
                here = place(t, j)
                at = 8 * (j % 16)
                tint = [jnp.broadcast_to(columns[t][at : at + 8, 45:46], (8, LANES))]
                tint += [color_ref[here, half(k)] for k in range(2)]
                for p in range(2):
                    alpha = jnp.exp2(power_ref[here, half(p)])
                    alpha_ref[here, half(p)] = alpha
                    weight = alpha * trans[t, p]
                    weight_ref[here, half(p)] = weight
                    trans[t, p] = trans[t, p] - weight
                    image[t, p] = [image[t, p][k] + weight * tint[k] for k in range(3)]

    for t in range(4):
        slopes = []
        for p in range(2):
            kept = trans[t, p]
            lead = sublane_shift(kept, 1, 1.0)
            for by_ in (1, 2, 4):
                lead = lead * sublane_shift(lead, by_, 1.0)
            before[t, p] = lead
            slope = []
            for k in range(3):
                shown = jnp.sum(lead * image[t, p][k], axis=0, keepdims=True)
                goal = target_ref[k, :, 256 * t + 128 * p : 256 * t + 128 * p + 128]
                slope.append(2.0 * (shown - goal))
            slopes.append(slope)
            add = sum(slope[k] * image[t, p][k] for k in range(3))
            mul = kept
            for by_ in (1, 2, 4):
                add = add + mul * sublane_shift(add, -by_, 0.0)
                mul = mul * sublane_shift(mul, -by_, 1.0)
            behind[t, p] = sublane_shift(add, -1, 0.0)
        parts = [
            split(jnp.concatenate([slopes[0][k], slopes[1][k]], axis=1), 3) for k in range(3)
        ]
        rows = [pad] * 18
        for part in range(3):
            rows += [parts[k][part] for _ in range(3) for k in range(3)]
        rights[t] = (jnp.concatenate(rows + [pad] * 3, axis=0).astype(BF16))
        nine = [parts[k][part] for part in range(3) for k in range(3)]
        shades[t] = (jnp.concatenate([pad] * 16 + nine + [pad] * 7, axis=0).T.astype(BF16))

    for t in range(4):
        left = jnp.concatenate([left_ref[chunk(t, u), :] for u in range(4)], axis=0)
        rest = jnp.dot(left, rights[t], preferred_element_type=F32)
        for u in range(4):
            power_ref[chunk(t, u), :] = rest[128 * u : 128 * u + 128, :]
    for u in (3, 2, 1, 0):
        for i in range(8 * u + 7, 8 * u - 1, -1):
            for t, p in spans:
                pair = [None, None]
                rest = behind[t, p]
                for o in (1, 0):
                    here = place(t, 2 * i + o)
                    weight = weight_ref[here, half(p)] * before[t, p]
                    gap = power_ref[here, half(p)] - rest
                    rest = rest + alpha_ref[here, half(p)] * gap
                    pair[o] = (weight * gap, weight)
                behind[t, p] = rest
                first = place(t, 2 * i).start
                for n, ref in enumerate((slope_ref, shade_ref)):
                    value = jnp.concatenate([pair[0][n], pair[1][n]], axis=0)
                    high = value.astype(BF16)
                    ref[first : first + 16, half(p)] = high
                    ref[first : first + 16, half(2 + p)] = (value - high.astype(F32)).astype(BF16)
        part_ref[512 * u : 512 * u + 512, :] = jnp.dot(
            slope_ref[512 * u : 512 * u + 512, :], moment_ref[...], preferred_element_type=F32
        )
    for t in range(4):
        weights = jnp.concatenate([shade_ref[chunk(t, u), :] for u in range(4)], axis=0)
        shaded = jnp.dot(
            weights, jnp.concatenate([shades[t]] * 2, axis=0), preferred_element_type=F32
        )
        for u in range(4):
            total = part_ref[chunk(t, u), :] + shaded[128 * u : 128 * u + 128, :]
            sums_ref[32 * (4 * t + u) : 32 * (4 * t + u) + 32, :] = total.T

    def summed(k):
        return jnp.concatenate(
            [sums_ref[pl.ds(256 * h + k, 8, stride=32), :] for h in range(2)], axis=0
        )

    mxx, mxy, myy, mx, my, m0 = [summed(k) for k in range(6)]
    sx = ex * m0 + mx
    sy = ey * m0 + my
    sxx = ex * (ex * m0 + 2.0 * mx) + mxx
    sxy = ex * (ey * m0 + my) + ey * mx + mxy
    syy = ey * (ey * m0 + 2.0 * my) + myy
    unit = 1.0 / screen
    grads = [
        (c0 * sx + c1 * sy) * unit,
        (c1 * sx + c2 * sy) * unit,
        (-0.5 * unit * unit) * sxx,
        (-unit * unit) * sxy,
        (-0.5 * unit * unit) * syy,
        m0 / opacity,
    ]
    for k in range(3):
        grads.append(summed(16 + k) + summed(19 + k) + summed(22 + k))
    for f in range(FEATS):
        grads_ref[16 * f : 16 * f + 16, :] = grads[f]

    out = [[None, None] for _ in range(FEATS)]
    for h in range(2):
        total = [jnp.zeros((8, LANES), F32) for _ in range(FEATS)]
        for t in range(4):
            code = inverse_ref[16 * t + 8 * h : 16 * t + 8 * h + 8, :]
            row = code >> 7
            lane = code & 127
            found = [jnp.zeros((8, LANES), F32) for _ in range(FEATS)]
            for u in range(4):
                here = row == u
                for f in range(FEATS):
                    at = 16 * f + 4 * t + u
                    source = jnp.broadcast_to(grads_ref[at : at + 1, :], (8, LANES))
                    found[f] = jnp.where(
                        here, jnp.take_along_axis(source, lane, axis=1, mode="promise_in_bounds"), found[f]
                    )
            total = [x + y for x, y in zip(total, found)]
        for f in range(FEATS):
            out[f][h] = total[f]
    table_to_wire(out, out_ref)


def adam_kernel(
    place_ref,
    own_ref,
    one_ref,
    two_ref,
    three_ref,
    params_ref,
    first_ref,
    second_ref,
    new_params_ref,
    new_first_ref,
    new_second_ref,
    scratch_ref,
    pulled_ref,
    local_ref,
    sems,
):
    for k, ref in enumerate((own_ref, one_ref, two_ref, three_ref)):
        at = pl.multiple_of(168 * ((place_ref[0] - k) & 3), 8)
        pulled_ref[pl.ds(at, 168), :] = ref[...]
    to_dense(params_ref, scratch_ref)
    rows = dense_rows(scratch_ref)
    seen = jnp.zeros((16, LANES), F32)
    cotangents = []
    cams = []
    for v in range(4):
        at = 168 * v
        cotangents.append(
            [pulled_ref[at + 16 * f : at + 16 * f + 16, :] for f in range(FEATS)]
        )
        seen = seen + pulled_ref[at + 144 : at + 160, :]
        cams.append(
            [
                jnp.broadcast_to(pulled_ref[at + 160 : at + 161, k : k + 1], (16, LANES))
                for k in range(12)
            ]
        )

    def leave(n):
        at = (slice(16, ROWS) if n == 0 else slice(0, 16), slice(None))
        return [
            pltpu.make_async_copy(local_ref.at[(m, *at)], ref.at[at], sems.at[n, m])
            for m, ref in enumerate((new_params_ref, new_first_ref, new_second_ref))
        ]

    def keep(f, value):
        for h in range(2):
            scratch_ref[pl.ds(512 * h + f, 8, stride=64), :] = value[8 * h : 8 * h + 8, :]

    def update(a):
        high = min(8, ROWS - 8 * a)
        row = lax.broadcasted_iota(I32, (high, LANES), 0) + 8 * a
        rate = jnp.where(
            row < 6,
            0.01,
            jnp.where(row < 10, 0.005, jnp.where(row < 11, 0.05, jnp.where(row < 14, 0.0025, 0.000125))),
        ).astype(F32) * (1.0 / bias_one)
        for k in range(16):
            at = (slice(8 * a, 8 * a + high), slice(LANES * k, LANES * k + LANES))
            grad = scratch_ref[64 * k + 8 * a : 64 * k + 8 * a + high, :]
            here = jnp.broadcast_to(seen[k : k + 1, :], (high, LANES)) > 0.0
            p, m, s = params_ref[at], first_ref[at], second_ref[at]
            m_new = 0.9 * m + 0.1 * grad
            s_new = 0.999 * s + 0.001 * grad * grad
            stride = rate * m_new / (jnp.sqrt(s_new * (1.0 / bias_two)) + 1e-08)
            local_ref[(0, *at)] = jnp.where(here, p - stride, p)
            local_ref[(1, *at)] = jnp.where(here, m_new, m)
            local_ref[(2, *at)] = jnp.where(here, s_new, s)

    bias_one = 1.0 - 0.9**ADAM_STEP
    bias_two = 1.0 - 0.999**ADAM_STEP

    def colors(means, coefficients):
        values = means + [None] * 8 + coefficients
        return [color_view(values, cam[9:]) for cam in cams]

    def geometry(values):
        basis = shape_basis(values)
        opacity = logistic(values[10])
        return [project_view(values, basis, cam[:9], cam[9:]) + [opacity] for cam in cams]

    _, pull = jax.vjp(colors, rows[:3], rows[11:])
    aimed, tinted = pull([cot[6:] for cot in cotangents])
    for k in range(48):
        keep(11 + k, tinted[k])
    for a in range(2, 8):
        update(a)
    for copy in leave(0):
        copy.start()
    _, pull = jax.vjp(geometry, rows[:11])
    shaped = pull([cot[:6] for cot in cotangents])[0]
    for k in range(11):
        keep(k, shaped[k] + aimed[k] if k < 3 else shaped[k])
    for a in range(2):
        update(a)
    for copy in leave(1):
        copy.start()
    for n in range(2):
        for copy in leave(n):
            copy.wait()


def pixel_constants():
    pixel = np.arange(256)
    x = pixel % 16 - 7.5
    y = pixel // 16 - 7.5
    six = np.stack([x * x, x * y, y * y, x, y, np.ones(256)])
    basis = np.zeros((KEYS, 512), np.float32)
    for part in range(3):
        basis[6 * part : 6 * part + 6, :256] = six
        for k in range(2):
            basis[19 + 3 * part + k, 256 + 128 * k : 384 + 128 * k] = 1.0
    moment = np.zeros((512, 32), np.float32)
    moment[:256, :6] = six.T
    moment[256:, :6] = six.T
    return jnp.asarray(basis, BF16), jnp.asarray(moment, BF16)


VMEM = pl.BlockSpec(memory_space=pltpu.VMEM)
SMEM = pl.BlockSpec(memory_space=pltpu.SMEM)
ANY = pl.BlockSpec(memory_space=pl.ANY)


def call(kernel, outs, ins, scratch, megabytes, cost, space=VMEM):
    flops, moved = cost
    return pl.pallas_call(
        kernel,
        out_shape=outs,
        in_specs=ins,
        out_specs=jax.tree.map(lambda _: space, outs),
        scratch_shapes=scratch,
        compiler_params=pltpu.CompilerParams(vmem_limit_bytes=megabytes << 20),
        cost_estimate=pl.CostEstimate(flops=flops, bytes_accessed=moved, transcendentals=0),
    )


def render(rows_pix):
    vmem = lambda *shape: pltpu.VMEM(shape, F32)
    return call(
        functools.partial(render_kernel, float(rows_pix)),
        jax.ShapeDtypeStruct((192, LANES), F32),
        [SMEM, VMEM, VMEM, VMEM, VMEM, VMEM, VMEM],
        [
            vmem(144, LANES),
            vmem(16 * KEYS, LANES),
            vmem(2048, 256),
            pltpu.VMEM((2048, KEYS), BF16),
            vmem(2048, 256),
            vmem(2048, 256),
            vmem(2048, 256),
            pltpu.VMEM((2048, 512), BF16),
            pltpu.VMEM((2048, 512), BF16),
            vmem(2048, 32),
            vmem(512, LANES),
            vmem(144, LANES),
        ],
        32,
        (100_000_000, 300_000),
    )


def shards(params, first_moment, second_moment, cameras, visible, send_plan, tile_lists, target):
    del visible
    cells = lax.axis_size("cells")
    views = lax.axis_size("views")
    plan = send_plan[0, 0].T
    lists = tile_lists[0]
    tiles = lists.shape[0]
    rows_pix = tiles * cells // TILE_COLS * 16
    f32 = lambda *shape: jax.ShapeDtypeStruct(shape, F32)
    i32 = lambda *shape: jax.ShapeDtypeStruct(shape, I32)
    vmem = lambda *shape: pltpu.VMEM(shape, F32)

    wire = call(
        project_kernel,
        f32(192, LANES),
        [SMEM, VMEM, VMEM],
        [vmem(1024, LANES), vmem(144, LANES), pltpu.VMEM((16, LANES), I32)],
        60,
        (10_000_000, 600_000),
    )(cameras, params, plan)
    arrived = lax.all_to_all(wire.reshape(64, 1, 384), "cells", 0, 0, tiled=True)

    inverse = call(slots_kernel, i32(64, LANES), [SMEM], [], 8, (20_000_000, 50_000))(lists)

    basis, moment = pixel_constants()
    back = render(rows_pix)(
        lax.axis_index("cells").astype(I32).reshape(1),
        arrived.reshape(192, LANES),
        lists,
        inverse,
        jnp.swapaxes(target, 0, 1),
        basis,
        moment,
    )
    returned = lax.all_to_all(back.reshape(64, 1, 384), "cells", 0, 0, tiled=True)

    code, view = call(
        owner_kernel, (i32(16, LANES), f32(8, LANES)), [SMEM, SMEM], [], 8, (20_000_000, 50_000)
    )(cameras, plan)
    own = call(
        pull_kernel, f32(168, LANES), [VMEM, VMEM, VMEM], [vmem(144, LANES)], 8, (1_000_000, 200_000)
    )(returned.reshape(192, LANES), code, view)
    others = [
        lax.ppermute(own, "views", [(i, (i + k) % views) for i in range(views)]) for k in (1, 2, 3)
    ]
    shape = f32(*params.shape)
    return call(
        adam_kernel,
        (shape, shape, shape),
        [SMEM] + [VMEM] * 7,
        [
            vmem(1024, LANES),
            vmem(168 * 4, LANES),
            vmem(3, ROWS, 2048),
            pltpu.SemaphoreType.DMA((2, 3)),
        ],
        24,
        (40_000_000, 3_500_000),
        ANY,
    )(
        lax.axis_index("views").astype(I32).reshape(1),
        own,
        *others,
        params,
        first_moment,
        second_moment,
    )


def solution(mesh):
    in_specs = (
        P(None, "cells"),
        P(None, "cells"),
        P(None, "cells"),
        P("views", None),
        P("views", "cells"),
        P("views", "cells", None, None),
        P("views", "cells", None),
        P("views", None, "cells"),
    )
    out_specs = (P(None, "cells"), P(None, "cells"), P(None, "cells"))
    return jax.shard_map(shards, mesh=mesh, in_specs=in_specs, out_specs=out_specs, check_vma=False)
```

```python
import functools

import jax
import jax.numpy as jnp
import numpy as np
from jax import lax
from jax.experimental import pallas as pl
from jax.experimental.pallas import tpu as pltpu
from jax.sharding import PartitionSpec as P

TILE_COLS = 32
ADAM_STEP = 1000
ROWS = 59
FEATS = 9
LANES = 128
LOG2E = 1.4426950408889634
ABSENT = -10000.0
KEYS = 48

harmonic_zero = 0.28209479177387814
harmonic_one = 0.4886025119029199
harmonic_two = (
    1.0925484305920792,
    -1.0925484305920792,
    0.31539156525252005,
    -1.0925484305920792,
    0.5462742152960396,
)
harmonic_three = (
    -0.5900435899266435,
    2.890611442640554,
    -0.4570457994644658,
    0.3731763325901154,
    -0.4570457994644658,
    1.445305721320277,
    -0.5900435899266435,
)

F32 = jnp.float32
BF16 = jnp.bfloat16
I32 = jnp.int32


def harmonics(across, upward, onward):
    across_sq = across * across
    upward_sq = upward * upward
    onward_sq = onward * onward
    return [
        None,
        -harmonic_one * upward,
        harmonic_one * onward,
        -harmonic_one * across,
        harmonic_two[0] * across * upward,
        harmonic_two[1] * upward * onward,
        harmonic_two[2] * (2.0 * onward_sq - across_sq - upward_sq),
        harmonic_two[3] * across * onward,
        harmonic_two[4] * (across_sq - upward_sq),
        harmonic_three[0] * upward * (3.0 * across_sq - upward_sq),
        harmonic_three[1] * across * upward * onward,
        harmonic_three[2] * upward * (4.0 * onward_sq - across_sq - upward_sq),
        harmonic_three[3] * onward * (2.0 * onward_sq - 3.0 * across_sq - 3.0 * upward_sq),
        harmonic_three[4] * across * (4.0 * onward_sq - across_sq - upward_sq),
        harmonic_three[5] * onward * (across_sq - upward_sq),
        harmonic_three[6] * across * (across_sq - 3.0 * upward_sq),
    ]


def rotation(roll, pitch, yaw):
    cr, sr = jnp.cos(roll), jnp.sin(roll)
    cp, sp = jnp.cos(pitch), jnp.sin(pitch)
    cy, sy = jnp.cos(yaw), jnp.sin(yaw)
    return [
        cy * cp,
        cy * sp * sr - sy * cr,
        cy * sp * cr + sy * sr,
        sy * cp,
        sy * sp * sr + cy * cr,
        sy * sp * cr - cy * sr,
        -sp,
        cp * sr,
        cp * cr,
    ]


def shape_basis(rows):
    scales = [jnp.exp(rows[3 + k]) for k in range(3)]
    qw, qx, qy, qz = rows[6], rows[7], rows[8], rows[9]
    norm = 1.0 / jnp.sqrt(qw * qw + qx * qx + qy * qy + qz * qz)
    qw, qx, qy, qz = qw * norm, qx * norm, qy * norm, qz * norm
    spin = [
        [1.0 - 2.0 * (qy * qy + qz * qz), 2.0 * (qx * qy - qw * qz), 2.0 * (qx * qz + qw * qy)],
        [2.0 * (qx * qy + qw * qz), 1.0 - 2.0 * (qx * qx + qz * qz), 2.0 * (qy * qz - qw * qx)],
        [2.0 * (qx * qz - qw * qy), 2.0 * (qy * qz + qw * qx), 1.0 - 2.0 * (qx * qx + qy * qy)],
    ]
    return [[spin[m][k] * scales[k] for k in range(3)] for m in range(3)]


def project_view(rows, basis, turn, centre):
    offset = [rows[k] - centre[k] for k in range(3)]
    seen = [
        turn[3 * m] * offset[0] + turn[3 * m + 1] * offset[1] + turn[3 * m + 2] * offset[2]
        for m in range(3)
    ]
    inv_depth = 1.0 / seen[2]
    col = seen[0] * inv_depth
    row = seen[1] * inv_depth
    cam = [
        [
            turn[3 * m] * basis[0][k] + turn[3 * m + 1] * basis[1][k] + turn[3 * m + 2] * basis[2][k]
            for k in range(3)
        ]
        for m in range(3)
    ]
    top = [(cam[0][k] - col * cam[2][k]) * inv_depth for k in range(3)]
    low = [(cam[1][k] - row * cam[2][k]) * inv_depth for k in range(3)]
    sa = top[0] * top[0] + top[1] * top[1] + top[2] * top[2]
    sb = top[0] * low[0] + top[1] * low[1] + top[2] * low[2]
    sc = low[0] * low[0] + low[1] * low[1] + low[2] * low[2]
    inv_det = 1.0 / (sa * sc - sb * sb)
    return [col, row, sc * inv_det, -sb * inv_det, sa * inv_det]


def color_view(rows, centre):
    offset = [rows[k] - centre[k] for k in range(3)]
    inv_dist = 1.0 / jnp.sqrt(
        offset[0] * offset[0] + offset[1] * offset[1] + offset[2] * offset[2]
    )
    harm = harmonics(offset[0] * inv_dist, offset[1] * inv_dist, offset[2] * inv_dist)
    colors = []
    for k in range(3):
        total = 0.5 + harmonic_zero * rows[11 + k]
        for j in range(1, 16):
            total = total + harm[j] * rows[11 + 3 * j + k]
        colors.append(total)
    return colors


def logistic(x):
    return 1.0 / (1.0 + jnp.exp(-x))


def block_transpose(four):
    lane = lax.broadcasted_iota(I32, (8, LANES), 1)
    low = lane < 64
    even = (lane & 32) == 0
    a, b, c, d = four
    a, c = jnp.where(low, a, pltpu.roll(c, 64, 1)), jnp.where(low, pltpu.roll(a, 64, 1), c)
    b, d = jnp.where(low, b, pltpu.roll(d, 64, 1)), jnp.where(low, pltpu.roll(b, 64, 1), d)
    a, b = jnp.where(even, a, pltpu.roll(b, 32, 1)), jnp.where(even, pltpu.roll(a, 96, 1), b)
    c, d = jnp.where(even, c, pltpu.roll(d, 32, 1)), jnp.where(even, pltpu.roll(c, 96, 1), d)
    return [a, b, c, d]


def wire_to_table(wire_ref, at, table_ref):
    for j in range(3):
        for h in range(2):
            four = [
                wire_ref[pl.ds(at + 3 * (32 * h + 8 * q) + j, 8, stride=3), :] for q in range(4)
            ]
            parts = block_transpose(four)
            for i in range(4):
                f = 4 * j + i
                if f < FEATS:
                    table_ref[16 * f + 8 * h : 16 * f + 8 * h + 8, :] = parts[i]


def table_to_wire(table, wire_ref):
    zero = jnp.zeros((8, LANES), F32)
    for j in range(3):
        for h in range(2):
            four = [table[4 * j + i][h] if 4 * j + i < FEATS else zero for i in range(4)]
            parts = block_transpose(four)
            for q in range(4):
                wire_ref[pl.ds(3 * (32 * h + 8 * q) + j, 8, stride=3), :] = parts[q]


def lookup(table_ref, feats, row, lane):
    found = []
    bits = [(row >> n) & 1 == 1 for n in range(4)]
    for f in range(feats):
        level = []
        for k in range(16):
            source = jnp.broadcast_to(table_ref[16 * f + k : 16 * f + k + 1, :], (8, LANES))
            level.append(jnp.take_along_axis(source, lane, axis=1, mode="promise_in_bounds"))
        for n in range(4):
            level = [jnp.where(bits[n], level[2 * i + 1], level[2 * i]) for i in range(len(level) // 2)]
        found.append(level[0])
    return found


def to_dense(natural_ref, scratch_ref):
    for k in range(16):
        for a in range(8):
            high = min(8, ROWS - 8 * a)
            scratch_ref[64 * k + 8 * a : 64 * k + 8 * a + high, :] = natural_ref[
                8 * a : 8 * a + high, LANES * k : LANES * k + LANES
            ]


def dense_rows(scratch_ref):
    return [
        jnp.concatenate(
            [scratch_ref[pl.ds(512 * h + f, 8, stride=64), :] for h in range(2)], axis=0
        )
        for f in range(ROWS)
    ]


def project_kernel(camera_ref, params_ref, plan_ref, wire_ref, scratch_ref, table_ref, idx_ref):
    to_dense(params_ref, scratch_ref)
    rows = dense_rows(scratch_ref)
    angle = [jnp.full((8, LANES), camera_ref[0, k], F32) for k in range(3)]
    turn = [jnp.concatenate([t, t], axis=0) for t in rotation(*angle)]
    centre = [camera_ref[0, 3 + k] for k in range(3)]
    feats = project_view(rows, shape_basis(rows), turn, centre) + [logistic(rows[10])]
    feats += color_view(rows, centre)
    for f in range(FEATS):
        table_ref[16 * f : 16 * f + 16, :] = feats[f]
    plan = jnp.maximum(plan_ref[...], 0).T
    for h in range(2):
        for q in range(4):
            idx_ref[8 * h : 8 * h + 8, 32 * q : 32 * q + 32] = plan[
                32 * h + 8 * q : 32 * h + 8 * q + 8, :
            ]
    out = [[None, None] for _ in range(FEATS)]
    for h in range(2):
        idx = idx_ref[8 * h : 8 * h + 8, :]
        found = lookup(table_ref, FEATS, idx >> 7, idx & 127)
        for f in range(FEATS):
            out[f][h] = found[f]
    table_to_wire(out, wire_ref)


def slots_kernel(lists_ref, inverse_ref):
    row = lax.broadcasted_iota(I32, (16, LANES), 0)
    lane = lax.broadcasted_iota(I32, (16, LANES), 1)
    device = 32 * (row >> 3) + 8 * (lane >> 5) + (row & 7)
    slot = 32 * device + (lane & 31)
    none = jnp.full((16, LANES), -1, I32)

    def tile_step(i, kept):
        s = i >> 2
        u = i & 3
        kept = list(kept)
        for jj in range(16):
            for t in range(4):
                e = lists_ref[t, 64 * s + 16 * u + jj]
                kept[t] = jnp.where(slot == e, LANES * u + 8 * jj + s, kept[t])
        return tuple(kept)

    kept = lax.fori_loop(0, 32, tile_step, (none,) * 4)
    for t in range(4):
        inverse_ref[16 * t : 16 * t + 16, :] = kept[t]


def owner_kernel(camera_ref, plan_ref, code_ref, view_ref):
    row = lax.broadcasted_iota(I32, (16, LANES), 0)
    lane = lax.broadcasted_iota(I32, (16, LANES), 1)
    gauss = row * LANES + lane

    def plan_step(d, kept):
        code = (8 * (d >> 5) + (d & 7)) * LANES + 32 * ((d >> 3) & 3)
        for c in range(32):
            kept = jnp.where(gauss == plan_ref[c, d], code + c, kept)
        return kept

    code_ref[...] = lax.fori_loop(0, 64, plan_step, jnp.full((16, LANES), -1, I32))
    angle = [jnp.full((8, LANES), camera_ref[0, k], F32) for k in range(3)]
    values = rotation(*angle) + [jnp.full((8, LANES), camera_ref[0, 3 + k], F32) for k in range(3)]
    lane = lax.broadcasted_iota(I32, (8, LANES), 1)
    view = jnp.zeros((8, LANES), F32)
    for k in range(12):
        view = jnp.where(lane == k, values[k], view)
    view_ref[...] = view


def pull_kernel(wire_ref, code_ref, view_ref, out_ref, table_ref):
    wire_to_table(wire_ref, 0, table_ref)
    for h in range(2):
        code = code_ref[8 * h : 8 * h + 8, :]
        found = lookup(table_ref, FEATS, code >> 7, code & 127)
        for f in range(FEATS):
            out_ref[16 * f + 8 * h : 16 * f + 8 * h + 8, :] = jnp.where(code >= 0, found[f], 0.0)
        out_ref[144 + 8 * h : 152 + 8 * h, :] = jnp.where(code >= 0, 1.0, 0.0)
    out_ref[160:168, :] = view_ref[...]


def split(x, parts):
    done = []
    for _ in range(parts - 1):
        high = x.astype(BF16).astype(F32)
        done.append(high)
        x = x - high
    done.append(x)
    return done


def sublane_shift(x, by, fill):
    s = lax.broadcasted_iota(I32, x.shape, 0)
    moved = pltpu.roll(x, by % 8, 0)
    return jnp.where((s >= by) if by > 0 else (s < 8 + by), moved, fill)


def render_kernel(
    device_rows,
    place_ref,
    wire_ref,
    lists_ref,
    inverse_ref,
    target_ref,
    basis_ref,
    moment_ref,
    out_ref,
    table_ref,
    lhs_ref,
    power_ref,
    left_ref,
    color_ref,
    alpha_ref,
    weight_ref,
    slope_ref,
    shade_ref,
    part_ref,
    sums_ref,
    grads_ref,
):
    device = place_ref[0]
    rows_pix = device_rows
    wire_to_table(wire_ref, 0, table_ref)

    sub = lax.broadcasted_iota(I32, (8, LANES), 0)
    lane = lax.broadcasted_iota(I32, (8, LANES), 1)
    entry = []
    for h in range(2):
        e = jnp.zeros((8, LANES), I32)
        for w in range(4):
            at = slice(LANES * w, LANES * w + LANES)
            lists = jnp.where(
                sub < 4,
                jnp.broadcast_to(lists_ref[2 * h : 2 * h + 1, at], (8, LANES)),
                jnp.broadcast_to(lists_ref[2 * h + 1 : 2 * h + 2, at], (8, LANES)),
            )
            source = 64 * (lane & 1) + 16 * (sub & 3) + (lane >> 3)
            moved = jnp.take_along_axis(lists, source, axis=1, mode="promise_in_bounds")
            e = jnp.where((lane & 7) >> 1 == w, moved, e)
        entry.append(e)
    feats = [[None, None] for _ in range(FEATS)]
    for h in range(2):
        e = jnp.maximum(entry[h], 0)
        row = 8 * ((e >> 10) & 1) + ((e >> 5) & 7)
        lane = 32 * ((e >> 8) & 3) + (e & 31)
        found = lookup(table_ref, FEATS, row, lane)
        for f in range(FEATS):
            feats[f][h] = found[f]
    feats = [jnp.concatenate(two, axis=0) for two in feats]
    live = jnp.concatenate(entry, axis=0) >= 0
    col, scr, c0, c1, c2, opacity = feats[:6]

    block_cols = TILE_COLS // 4
    tile_col = (
        4 * (device % block_cols) + lax.broadcasted_iota(I32, (16, LANES), 0) // 4
    ).astype(F32)
    tile_row = (device // block_cols).astype(F32)
    screen = TILE_COLS * 8.0
    ex = (16.0 * tile_col + 8.0 - screen) - screen * col
    ey = (16.0 * tile_row + 8.0 - rows_pix * 0.5) - screen * scr
    factor = -0.5 * LOG2E / (screen * screen)
    a = factor * c0
    b = (2.0 * factor) * c1
    c = factor * c2
    bx = b * ex
    by = b * ey
    coeffs = [
        a,
        b,
        c,
        2.0 * a * ex + by,
        bx + 2.0 * c * ey,
        (a * ex + by) * ex + c * ey * ey + LOG2E * jnp.log(opacity),
    ]
    rest = [0.0, 0.0, 0.0, 0.0, 0.0, ABSENT]
    lines = []
    pieces = [split(jnp.where(live, x, r), 3) for x, r in zip(coeffs, rest)]
    for part in range(3):
        lines += [pieces[k][part] for k in range(6)]
    tints = [split(feats[6 + k], 3) for k in range(3)]
    tints = [tints[k][part] for part in range(3) for k in range(3)]
    lines += tints * 3 + [feats[6]] + [jnp.zeros((16, LANES), F32)] * 2
    for k in range(KEYS):
        for h in range(2):
            lhs_ref[pl.ds(8 * KEYS * h + k, 8, stride=KEYS), :] = lines[k][8 * h : 8 * h + 8, :]

    one = jnp.ones((8, LANES), F32)
    zero = jnp.zeros((8, LANES), F32)
    spans = [(t, p) for t in range(4) for p in range(2)]

    def place(t, j):
        start = 512 * (j // 16) + 128 * t + 8 * (j % 16)
        return slice(start, start + 8)

    def chunk(t, u):
        return slice(512 * u + 128 * t, 512 * u + 128 * t + 128)

    def half(p):
        return slice(LANES * p, LANES * p + LANES)

    trans = {tp: one for tp in spans}
    image = {tp: [zero] * 3 for tp in spans}
    before, behind, rights, shades = {}, {}, {}, {}
    pad = jnp.zeros((1, 256), F32)
    for u in range(4):
        columns = []
        for t in range(4):
            lines = lhs_ref[KEYS * (4 * t + u) : KEYS * (4 * t + u) + KEYS, :].T
            columns.append(lines)
            left_ref[chunk(t, u), :] = lines.astype(BF16)
        both = jnp.dot(
            left_ref[512 * u : 512 * u + 512, :], basis_ref[...], preferred_element_type=F32
        )
        power_ref[512 * u : 512 * u + 512, :] = both[:, 0:256]
        color_ref[512 * u : 512 * u + 512, :] = both[:, 256:512]
        for j in range(16 * u, 16 * u + 16):
            for t in range(4):
                here = place(t, j)
                at = 8 * (j % 16)
                tint = [jnp.broadcast_to(columns[t][at : at + 8, 45:46], (8, LANES))]
                tint += [color_ref[here, half(k)] for k in range(2)]
                for p in range(2):
                    alpha = jnp.exp2(power_ref[here, half(p)])
                    alpha_ref[here, half(p)] = alpha
                    weight = alpha * trans[t, p]
                    weight_ref[here, half(p)] = weight
                    trans[t, p] = trans[t, p] - weight
                    image[t, p] = [image[t, p][k] + weight * tint[k] for k in range(3)]

    for t in range(4):
        slopes = []
        for p in range(2):
            kept = trans[t, p]
            lead = sublane_shift(kept, 1, 1.0)
            for by_ in (1, 2, 4):
                lead = lead * sublane_shift(lead, by_, 1.0)
            before[t, p] = lead
            slope = []
            for k in range(3):
                shown = jnp.sum(lead * image[t, p][k], axis=0, keepdims=True)
                goal = target_ref[k, :, 256 * t + 128 * p : 256 * t + 128 * p + 128]
                slope.append(2.0 * (shown - goal))
            slopes.append(slope)
            add = sum(slope[k] * image[t, p][k] for k in range(3))
            mul = kept
            for by_ in (1, 2, 4):
                add = add + mul * sublane_shift(add, -by_, 0.0)
                mul = mul * sublane_shift(mul, -by_, 1.0)
            behind[t, p] = sublane_shift(add, -1, 0.0)
        parts = [
            split(jnp.concatenate([slopes[0][k], slopes[1][k]], axis=1), 3) for k in range(3)
        ]
        rows = [pad] * 18
        for part in range(3):
            rows += [parts[k][part] for _ in range(3) for k in range(3)]
        rights[t] = (jnp.concatenate(rows + [pad] * 3, axis=0).astype(BF16))
        nine = [parts[k][part] for part in range(3) for k in range(3)]
        shades[t] = (jnp.concatenate([pad] * 16 + nine + [pad] * 7, axis=0).T.astype(BF16))

    for t in range(4):
        left = jnp.concatenate([left_ref[chunk(t, u), :] for u in range(4)], axis=0)
        rest = jnp.dot(left, rights[t], preferred_element_type=F32)
        for u in range(4):
            power_ref[chunk(t, u), :] = rest[128 * u : 128 * u + 128, :]
    for u in (3, 2, 1, 0):
        for i in range(8 * u + 7, 8 * u - 1, -1):
            for t, p in spans:
                pair = [None, None]
                rest = behind[t, p]
                for o in (1, 0):
                    here = place(t, 2 * i + o)
                    weight = weight_ref[here, half(p)] * before[t, p]
                    gap = power_ref[here, half(p)] - rest
                    rest = rest + alpha_ref[here, half(p)] * gap
                    pair[o] = (weight * gap, weight)
                behind[t, p] = rest
                first = place(t, 2 * i).start
                for n, ref in enumerate((slope_ref, shade_ref)):
                    value = jnp.concatenate([pair[0][n], pair[1][n]], axis=0)
                    high = value.astype(BF16)
                    ref[first : first + 16, half(p)] = high
                    ref[first : first + 16, half(2 + p)] = (value - high.astype(F32)).astype(BF16)
        part_ref[512 * u : 512 * u + 512, :] = jnp.dot(
            slope_ref[512 * u : 512 * u + 512, :], moment_ref[...], preferred_element_type=F32
        )
    for t in range(4):
        weights = jnp.concatenate([shade_ref[chunk(t, u), :] for u in range(4)], axis=0)
        shaded = jnp.dot(
            weights, jnp.concatenate([shades[t]] * 2, axis=0), preferred_element_type=F32
        )
        for u in range(4):
            total = part_ref[chunk(t, u), :] + shaded[128 * u : 128 * u + 128, :]
            sums_ref[32 * (4 * t + u) : 32 * (4 * t + u) + 32, :] = total.T

    def summed(k):
        return jnp.concatenate(
            [sums_ref[pl.ds(256 * h + k, 8, stride=32), :] for h in range(2)], axis=0
        )

    mxx, mxy, myy, mx, my, m0 = [summed(k) for k in range(6)]
    sx = ex * m0 + mx
    sy = ey * m0 + my
    sxx = ex * (ex * m0 + 2.0 * mx) + mxx
    sxy = ex * (ey * m0 + my) + ey * mx + mxy
    syy = ey * (ey * m0 + 2.0 * my) + myy
    unit = 1.0 / screen
    grads = [
        (c0 * sx + c1 * sy) * unit,
        (c1 * sx + c2 * sy) * unit,
        (-0.5 * unit * unit) * sxx,
        (-unit * unit) * sxy,
        (-0.5 * unit * unit) * syy,
        m0 / opacity,
    ]
    for k in range(3):
        grads.append(summed(16 + k) + summed(19 + k) + summed(22 + k))
    for f in range(FEATS):
        grads_ref[16 * f : 16 * f + 16, :] = grads[f]

    out = [[None, None] for _ in range(FEATS)]
    for h in range(2):
        total = [jnp.zeros((8, LANES), F32) for _ in range(FEATS)]
        for t in range(4):
            code = inverse_ref[16 * t + 8 * h : 16 * t + 8 * h + 8, :]
            row = code >> 7
            lane = code & 127
            found = [jnp.zeros((8, LANES), F32) for _ in range(FEATS)]
            for u in range(4):
                here = row == u
                for f in range(FEATS):
                    at = 16 * f + 4 * t + u
                    source = jnp.broadcast_to(grads_ref[at : at + 1, :], (8, LANES))
                    found[f] = jnp.where(
                        here, jnp.take_along_axis(source, lane, axis=1, mode="promise_in_bounds"), found[f]
                    )
            total = [x + y for x, y in zip(total, found)]
        for f in range(FEATS):
            out[f][h] = total[f]
    table_to_wire(out, out_ref)


def adam_kernel(
    place_ref,
    own_ref,
    one_ref,
    two_ref,
    three_ref,
    params_ref,
    first_ref,
    second_ref,
    new_params_ref,
    new_first_ref,
    new_second_ref,
    scratch_ref,
    pulled_ref,
    local_ref,
    sems,
):
    for k, ref in enumerate((own_ref, one_ref, two_ref, three_ref)):
        at = pl.multiple_of(168 * ((place_ref[0] - k) & 3), 8)
        pulled_ref[pl.ds(at, 168), :] = ref[...]
    to_dense(params_ref, scratch_ref)
    rows = dense_rows(scratch_ref)
    seen = jnp.zeros((16, LANES), F32)
    cotangents = []
    cams = []
    for v in range(4):
        at = 168 * v
        cotangents.append(
            [pulled_ref[at + 16 * f : at + 16 * f + 16, :] for f in range(FEATS)]
        )
        seen = seen + pulled_ref[at + 144 : at + 160, :]
        cams.append(
            [
                jnp.broadcast_to(pulled_ref[at + 160 : at + 161, k : k + 1], (16, LANES))
                for k in range(12)
            ]
        )

    def leave(n):
        at = (slice(16, ROWS) if n == 0 else slice(0, 16), slice(None))
        return [
            pltpu.make_async_copy(local_ref.at[(m, *at)], ref.at[at], sems.at[n, m])
            for m, ref in enumerate((new_params_ref, new_first_ref, new_second_ref))
        ]

    def keep(f, value):
        for h in range(2):
            scratch_ref[pl.ds(512 * h + f, 8, stride=64), :] = value[8 * h : 8 * h + 8, :]

    def update(a):
        high = min(8, ROWS - 8 * a)
        row = lax.broadcasted_iota(I32, (high, LANES), 0) + 8 * a
        rate = jnp.where(
            row < 6,
            0.01,
            jnp.where(row < 10, 0.005, jnp.where(row < 11, 0.05, jnp.where(row < 14, 0.0025, 0.000125))),
        ).astype(F32) * (1.0 / bias_one)
        for k in range(16):
            at = (slice(8 * a, 8 * a + high), slice(LANES * k, LANES * k + LANES))
            grad = scratch_ref[64 * k + 8 * a : 64 * k + 8 * a + high, :]
            here = jnp.broadcast_to(seen[k : k + 1, :], (high, LANES)) > 0.0
            p, m, s = params_ref[at], first_ref[at], second_ref[at]
            m_new = 0.9 * m + 0.1 * grad
            s_new = 0.999 * s + 0.001 * grad * grad
            stride = rate * m_new / (jnp.sqrt(s_new * (1.0 / bias_two)) + 1e-08)
            local_ref[(0, *at)] = jnp.where(here, p - stride, p)
            local_ref[(1, *at)] = jnp.where(here, m_new, m)
            local_ref[(2, *at)] = jnp.where(here, s_new, s)

    bias_one = 1.0 - 0.9**ADAM_STEP
    bias_two = 1.0 - 0.999**ADAM_STEP

    def colors(means, coefficients):
        values = means + [None] * 8 + coefficients
        return [color_view(values, cam[9:]) for cam in cams]

    def geometry(values):
        basis = shape_basis(values)
        opacity = logistic(values[10])
        return [project_view(values, basis, cam[:9], cam[9:]) + [opacity] for cam in cams]

    _, pull = jax.vjp(colors, rows[:3], rows[11:])
    aimed, tinted = pull([cot[6:] for cot in cotangents])
    for k in range(48):
        keep(11 + k, tinted[k])
    for a in range(2, 8):
        update(a)
    for copy in leave(0):
        copy.start()
    _, pull = jax.vjp(geometry, rows[:11])
    shaped = pull([cot[:6] for cot in cotangents])[0]
    for k in range(11):
        keep(k, shaped[k] + aimed[k] if k < 3 else shaped[k])
    for a in range(2):
        update(a)
    for copy in leave(1):
        copy.start()
    for n in range(2):
        for copy in leave(n):
            copy.wait()


def pixel_constants():
    pixel = np.arange(256)
    x = pixel % 16 - 7.5
    y = pixel // 16 - 7.5
    six = np.stack([x * x, x * y, y * y, x, y, np.ones(256)])
    basis = np.zeros((KEYS, 512), np.float32)
    for part in range(3):
        basis[6 * part : 6 * part + 6, :256] = six
        for k in range(2):
            basis[19 + 3 * part + k, 256 + 128 * k : 384 + 128 * k] = 1.0
    moment = np.zeros((512, 32), np.float32)
    moment[:256, :6] = six.T
    moment[256:, :6] = six.T
    return jnp.asarray(basis, BF16), jnp.asarray(moment, BF16)


VMEM = pl.BlockSpec(memory_space=pltpu.VMEM)
SMEM = pl.BlockSpec(memory_space=pltpu.SMEM)
ANY = pl.BlockSpec(memory_space=pl.ANY)


def call(kernel, outs, ins, scratch, megabytes, cost, space=VMEM):
    flops, moved = cost
    return pl.pallas_call(
        kernel,
        out_shape=outs,
        in_specs=ins,
        out_specs=jax.tree.map(lambda _: space, outs),
        scratch_shapes=scratch,
        compiler_params=pltpu.CompilerParams(vmem_limit_bytes=megabytes << 20),
        cost_estimate=pl.CostEstimate(flops=flops, bytes_accessed=moved, transcendentals=0),
    )


def render(rows_pix):
    vmem = lambda *shape: pltpu.VMEM(shape, F32)
    return call(
        functools.partial(render_kernel, float(rows_pix)),
        jax.ShapeDtypeStruct((192, LANES), F32),
        [SMEM, VMEM, VMEM, VMEM, VMEM, VMEM, VMEM],
        [
            vmem(144, LANES),
            vmem(16 * KEYS, LANES),
            vmem(2048, 256),
            pltpu.VMEM((2048, KEYS), BF16),
            vmem(2048, 256),
            vmem(2048, 256),
            vmem(2048, 256),
            pltpu.VMEM((2048, 512), BF16),
            pltpu.VMEM((2048, 512), BF16),
            vmem(2048, 32),
            vmem(512, LANES),
            vmem(144, LANES),
        ],
        32,
        (100_000_000, 300_000),
    )


def shards(params, first_moment, second_moment, cameras, visible, send_plan, tile_lists, target):
    del visible
    cells = lax.axis_size("cells")
    views = lax.axis_size("views")
    plan = send_plan[0, 0].T
    lists = tile_lists[0]
    tiles = lists.shape[0]
    rows_pix = tiles * cells // TILE_COLS * 16
    f32 = lambda *shape: jax.ShapeDtypeStruct(shape, F32)
    i32 = lambda *shape: jax.ShapeDtypeStruct(shape, I32)
    vmem = lambda *shape: pltpu.VMEM(shape, F32)

    wire = call(
        project_kernel,
        f32(192, LANES),
        [SMEM, VMEM, VMEM],
        [vmem(1024, LANES), vmem(144, LANES), pltpu.VMEM((16, LANES), I32)],
        60,
        (10_000_000, 600_000),
    )(cameras, params, plan)
    arrived = lax.all_to_all(wire.reshape(64, 1, 384), "cells", 0, 0, tiled=True)

    inverse = call(slots_kernel, i32(64, LANES), [SMEM], [], 8, (20_000_000, 50_000))(lists)

    basis, moment = pixel_constants()
    back = render(rows_pix)(
        lax.axis_index("cells").astype(I32).reshape(1),
        arrived.reshape(192, LANES),
        lists,
        inverse,
        jnp.swapaxes(target, 0, 1),
        basis,
        moment,
    )
    returned = lax.all_to_all(back.reshape(64, 1, 384), "cells", 0, 0, tiled=True)

    code, view = call(
        owner_kernel, (i32(16, LANES), f32(8, LANES)), [SMEM, SMEM], [], 8, (20_000_000, 50_000)
    )(cameras, plan)
    own = call(
        pull_kernel, f32(168, LANES), [VMEM, VMEM, VMEM], [vmem(144, LANES)], 8, (1_000_000, 200_000)
    )(returned.reshape(192, LANES), code, view)
    others = [
        lax.ppermute(own, "views", [(i, (i + k) % views) for i in range(views)]) for k in (1, 2, 3)
    ]
    shape = f32(*params.shape)
    return call(
        adam_kernel,
        (shape, shape, shape),
        [SMEM] + [VMEM] * 7,
        [
            vmem(1024, LANES),
            vmem(168 * 4, LANES),
            vmem(3, ROWS, 2048),
            pltpu.SemaphoreType.DMA((2, 3)),
        ],
        24,
        (40_000_000, 3_500_000),
        ANY,
    )(
        lax.axis_index("views").astype(I32).reshape(1),
        own,
        *others,
        params,
        first_moment,
        second_moment,
    )


def solution(mesh):
    in_specs = (
        P(None, "cells"),
        P(None, "cells"),
        P(None, "cells"),
        P("views", None),
        P("views", "cells"),
        P("views", "cells", None, None),
        P("views", "cells", None),
        P("views", None, "cells"),
    )
    out_specs = (P(None, "cells"), P(None, "cells"), P(None, "cells"))
    return jax.shard_map(shards, mesh=mesh, in_specs=in_specs, out_specs=out_specs, check_vma=False)
```

```python
import functools

import jax
import jax.numpy as jnp
import numpy as np
from jax import lax
from jax.experimental import pallas as pl
from jax.experimental.pallas import tpu as pltpu
from jax.sharding import PartitionSpec as P

TILE_COLS = 32
ADAM_STEP = 1000
ROWS = 59
FEATS = 9
LANES = 128
LOG2E = 1.4426950408889634
ABSENT = -10000.0
KEYS = 48

harmonic_zero = 0.28209479177387814
harmonic_one = 0.4886025119029199
harmonic_two = (
    1.0925484305920792,
    -1.0925484305920792,
    0.31539156525252005,
    -1.0925484305920792,
    0.5462742152960396,
)
harmonic_three = (
    -0.5900435899266435,
    2.890611442640554,
    -0.4570457994644658,
    0.3731763325901154,
    -0.4570457994644658,
    1.445305721320277,
    -0.5900435899266435,
)

F32 = jnp.float32
BF16 = jnp.bfloat16
I32 = jnp.int32


def harmonics(across, upward, onward):
    across_sq = across * across
    upward_sq = upward * upward
    onward_sq = onward * onward
    return [
        None,
        -harmonic_one * upward,
        harmonic_one * onward,
        -harmonic_one * across,
        harmonic_two[0] * across * upward,
        harmonic_two[1] * upward * onward,
        harmonic_two[2] * (2.0 * onward_sq - across_sq - upward_sq),
        harmonic_two[3] * across * onward,
        harmonic_two[4] * (across_sq - upward_sq),
        harmonic_three[0] * upward * (3.0 * across_sq - upward_sq),
        harmonic_three[1] * across * upward * onward,
        harmonic_three[2] * upward * (4.0 * onward_sq - across_sq - upward_sq),
        harmonic_three[3] * onward * (2.0 * onward_sq - 3.0 * across_sq - 3.0 * upward_sq),
        harmonic_three[4] * across * (4.0 * onward_sq - across_sq - upward_sq),
        harmonic_three[5] * onward * (across_sq - upward_sq),
        harmonic_three[6] * across * (across_sq - 3.0 * upward_sq),
    ]


def rotation(roll, pitch, yaw):
    cr, sr = jnp.cos(roll), jnp.sin(roll)
    cp, sp = jnp.cos(pitch), jnp.sin(pitch)
    cy, sy = jnp.cos(yaw), jnp.sin(yaw)
    return [
        cy * cp,
        cy * sp * sr - sy * cr,
        cy * sp * cr + sy * sr,
        sy * cp,
        sy * sp * sr + cy * cr,
        sy * sp * cr - cy * sr,
        -sp,
        cp * sr,
        cp * cr,
    ]


def shape_basis(rows):
    scales = [jnp.exp(rows[3 + k]) for k in range(3)]
    qw, qx, qy, qz = rows[6], rows[7], rows[8], rows[9]
    norm = 1.0 / jnp.sqrt(qw * qw + qx * qx + qy * qy + qz * qz)
    qw, qx, qy, qz = qw * norm, qx * norm, qy * norm, qz * norm
    spin = [
        [1.0 - 2.0 * (qy * qy + qz * qz), 2.0 * (qx * qy - qw * qz), 2.0 * (qx * qz + qw * qy)],
        [2.0 * (qx * qy + qw * qz), 1.0 - 2.0 * (qx * qx + qz * qz), 2.0 * (qy * qz - qw * qx)],
        [2.0 * (qx * qz - qw * qy), 2.0 * (qy * qz + qw * qx), 1.0 - 2.0 * (qx * qx + qy * qy)],
    ]
    return [[spin[m][k] * scales[k] for k in range(3)] for m in range(3)]


def project_view(rows, basis, turn, centre):
    offset = [rows[k] - centre[k] for k in range(3)]
    seen = [
        turn[3 * m] * offset[0] + turn[3 * m + 1] * offset[1] + turn[3 * m + 2] * offset[2]
        for m in range(3)
    ]
    inv_depth = 1.0 / seen[2]
    col = seen[0] * inv_depth
    row = seen[1] * inv_depth
    cam = [
        [
            turn[3 * m] * basis[0][k] + turn[3 * m + 1] * basis[1][k] + turn[3 * m + 2] * basis[2][k]
            for k in range(3)
        ]
        for m in range(3)
    ]
    top = [(cam[0][k] - col * cam[2][k]) * inv_depth for k in range(3)]
    low = [(cam[1][k] - row * cam[2][k]) * inv_depth for k in range(3)]
    sa = top[0] * top[0] + top[1] * top[1] + top[2] * top[2]
    sb = top[0] * low[0] + top[1] * low[1] + top[2] * low[2]
    sc = low[0] * low[0] + low[1] * low[1] + low[2] * low[2]
    inv_det = 1.0 / (sa * sc - sb * sb)
    return [col, row, sc * inv_det, -sb * inv_det, sa * inv_det]


def color_view(rows, centre):
    offset = [rows[k] - centre[k] for k in range(3)]
    inv_dist = 1.0 / jnp.sqrt(
        offset[0] * offset[0] + offset[1] * offset[1] + offset[2] * offset[2]
    )
    harm = harmonics(offset[0] * inv_dist, offset[1] * inv_dist, offset[2] * inv_dist)
    colors = []
    for k in range(3):
        total = 0.5 + harmonic_zero * rows[11 + k]
        for j in range(1, 16):
            total = total + harm[j] * rows[11 + 3 * j + k]
        colors.append(total)
    return colors


def logistic(x):
    return 1.0 / (1.0 + jnp.exp(-x))


def block_transpose(four):
    lane = lax.broadcasted_iota(I32, (8, LANES), 1)
    low = lane < 64
    even = (lane & 32) == 0
    a, b, c, d = four
    a, c = jnp.where(low, a, pltpu.roll(c, 64, 1)), jnp.where(low, pltpu.roll(a, 64, 1), c)
    b, d = jnp.where(low, b, pltpu.roll(d, 64, 1)), jnp.where(low, pltpu.roll(b, 64, 1), d)
    a, b = jnp.where(even, a, pltpu.roll(b, 32, 1)), jnp.where(even, pltpu.roll(a, 96, 1), b)
    c, d = jnp.where(even, c, pltpu.roll(d, 32, 1)), jnp.where(even, pltpu.roll(c, 96, 1), d)
    return [a, b, c, d]


def wire_to_table(wire_ref, at, table_ref):
    for j in range(3):
        for h in range(2):
            four = [
                wire_ref[pl.ds(at + 3 * (32 * h + 8 * q) + j, 8, stride=3), :] for q in range(4)
            ]
            parts = block_transpose(four)
            for i in range(4):
                f = 4 * j + i
                if f < FEATS:
                    table_ref[16 * f + 8 * h : 16 * f + 8 * h + 8, :] = parts[i]


def table_to_wire(table, wire_ref):
    zero = jnp.zeros((8, LANES), F32)
    for j in range(3):
        for h in range(2):
            four = [table[4 * j + i][h] if 4 * j + i < FEATS else zero for i in range(4)]
            parts = block_transpose(four)
            for q in range(4):
                wire_ref[pl.ds(3 * (32 * h + 8 * q) + j, 8, stride=3), :] = parts[q]


def lookup(table_ref, feats, row, lane):
    found = []
    bits = [(row >> n) & 1 == 1 for n in range(4)]
    for f in range(feats):
        level = []
        for k in range(16):
            source = jnp.broadcast_to(table_ref[16 * f + k : 16 * f + k + 1, :], (8, LANES))
            level.append(jnp.take_along_axis(source, lane, axis=1, mode="promise_in_bounds"))
        for n in range(4):
            level = [jnp.where(bits[n], level[2 * i + 1], level[2 * i]) for i in range(len(level) // 2)]
        found.append(level[0])
    return found


def to_dense(natural_ref, scratch_ref):
    for k in range(16):
        for a in range(8):
            high = min(8, ROWS - 8 * a)
            scratch_ref[64 * k + 8 * a : 64 * k + 8 * a + high, :] = natural_ref[
                8 * a : 8 * a + high, LANES * k : LANES * k + LANES
            ]


def dense_rows(scratch_ref):
    return [
        jnp.concatenate(
            [scratch_ref[pl.ds(512 * h + f, 8, stride=64), :] for h in range(2)], axis=0
        )
        for f in range(ROWS)
    ]


def project_kernel(camera_ref, params_ref, plan_ref, wire_ref, scratch_ref, table_ref, idx_ref):
    to_dense(params_ref, scratch_ref)
    rows = dense_rows(scratch_ref)
    angle = [jnp.full((8, LANES), camera_ref[0, k], F32) for k in range(3)]
    turn = [jnp.concatenate([t, t], axis=0) for t in rotation(*angle)]
    centre = [camera_ref[0, 3 + k] for k in range(3)]
    feats = project_view(rows, shape_basis(rows), turn, centre) + [logistic(rows[10])]
    feats += color_view(rows, centre)
    for f in range(FEATS):
        table_ref[16 * f : 16 * f + 16, :] = feats[f]
    plan = jnp.maximum(plan_ref[...], 0).T
    for h in range(2):
        for q in range(4):
            idx_ref[8 * h : 8 * h + 8, 32 * q : 32 * q + 32] = plan[
                32 * h + 8 * q : 32 * h + 8 * q + 8, :
            ]
    out = [[None, None] for _ in range(FEATS)]
    for h in range(2):
        idx = idx_ref[8 * h : 8 * h + 8, :]
        found = lookup(table_ref, FEATS, idx >> 7, idx & 127)
        for f in range(FEATS):
            out[f][h] = found[f]
    table_to_wire(out, wire_ref)


def slots_kernel(lists_ref, inverse_ref):
    row = lax.broadcasted_iota(I32, (16, LANES), 0)
    lane = lax.broadcasted_iota(I32, (16, LANES), 1)
    device = 32 * (row >> 3) + 8 * (lane >> 5) + (row & 7)
    slot = 32 * device + (lane & 31)
    none = jnp.full((16, LANES), -1, I32)

    def tile_step(i, kept):
        s = i >> 2
        u = i & 3
        kept = list(kept)
        for jj in range(16):
            for t in range(4):
                e = lists_ref[t, 64 * s + 16 * u + jj]
                kept[t] = jnp.where(slot == e, LANES * u + 8 * jj + s, kept[t])
        return tuple(kept)

    kept = lax.fori_loop(0, 32, tile_step, (none,) * 4)
    for t in range(4):
        inverse_ref[16 * t : 16 * t + 16, :] = kept[t]


def owner_kernel(camera_ref, plan_ref, code_ref, view_ref):
    row = lax.broadcasted_iota(I32, (16, LANES), 0)
    lane = lax.broadcasted_iota(I32, (16, LANES), 1)
    gauss = row * LANES + lane

    def plan_step(d, kept):
        code = (8 * (d >> 5) + (d & 7)) * LANES + 32 * ((d >> 3) & 3)
        for c in range(32):
            kept = jnp.where(gauss == plan_ref[c, d], code + c, kept)
        return kept

    code_ref[...] = lax.fori_loop(0, 64, plan_step, jnp.full((16, LANES), -1, I32))
    angle = [jnp.full((8, LANES), camera_ref[0, k], F32) for k in range(3)]
    values = rotation(*angle) + [jnp.full((8, LANES), camera_ref[0, 3 + k], F32) for k in range(3)]
    lane = lax.broadcasted_iota(I32, (8, LANES), 1)
    view = jnp.zeros((8, LANES), F32)
    for k in range(12):
        view = jnp.where(lane == k, values[k], view)
    view_ref[...] = view


def pull_kernel(wire_ref, code_ref, view_ref, out_ref, table_ref):
    wire_to_table(wire_ref, 0, table_ref)
    for h in range(2):
        code = code_ref[8 * h : 8 * h + 8, :]
        found = lookup(table_ref, FEATS, code >> 7, code & 127)
        for f in range(FEATS):
            out_ref[16 * f + 8 * h : 16 * f + 8 * h + 8, :] = jnp.where(code >= 0, found[f], 0.0)
        out_ref[144 + 8 * h : 152 + 8 * h, :] = jnp.where(code >= 0, 1.0, 0.0)
    out_ref[160:168, :] = view_ref[...]


def split(x, parts):
    done = []
    for _ in range(parts - 1):
        high = x.astype(BF16).astype(F32)
        done.append(high)
        x = x - high
    done.append(x)
    return done


def sublane_shift(x, by, fill):
    s = lax.broadcasted_iota(I32, x.shape, 0)
    moved = pltpu.roll(x, by % 8, 0)
    return jnp.where((s >= by) if by > 0 else (s < 8 + by), moved, fill)


def render_kernel(
    device_rows,
    place_ref,
    wire_ref,
    lists_ref,
    inverse_ref,
    target_ref,
    basis_ref,
    moment_ref,
    out_ref,
    table_ref,
    lhs_ref,
    power_ref,
    left_ref,
    color_ref,
    alpha_ref,
    weight_ref,
    slope_ref,
    shade_ref,
    part_ref,
    sums_ref,
    grads_ref,
):
    device = place_ref[0]
    rows_pix = device_rows
    wire_to_table(wire_ref, 0, table_ref)

    sub = lax.broadcasted_iota(I32, (8, LANES), 0)
    lane = lax.broadcasted_iota(I32, (8, LANES), 1)
    entry = []
    for h in range(2):
        e = jnp.zeros((8, LANES), I32)
        for w in range(4):
            at = slice(LANES * w, LANES * w + LANES)
            lists = jnp.where(
                sub < 4,
                jnp.broadcast_to(lists_ref[2 * h : 2 * h + 1, at], (8, LANES)),
                jnp.broadcast_to(lists_ref[2 * h + 1 : 2 * h + 2, at], (8, LANES)),
            )
            source = 64 * (lane & 1) + 16 * (sub & 3) + (lane >> 3)
            moved = jnp.take_along_axis(lists, source, axis=1, mode="promise_in_bounds")
            e = jnp.where((lane & 7) >> 1 == w, moved, e)
        entry.append(e)
    feats = [[None, None] for _ in range(FEATS)]
    for h in range(2):
        e = jnp.maximum(entry[h], 0)
        row = 8 * ((e >> 10) & 1) + ((e >> 5) & 7)
        lane = 32 * ((e >> 8) & 3) + (e & 31)
        found = lookup(table_ref, FEATS, row, lane)
        for f in range(FEATS):
            feats[f][h] = found[f]
    feats = [jnp.concatenate(two, axis=0) for two in feats]
    live = jnp.concatenate(entry, axis=0) >= 0
    col, scr, c0, c1, c2, opacity = feats[:6]

    block_cols = TILE_COLS // 4
    tile_col = (
        4 * (device % block_cols) + lax.broadcasted_iota(I32, (16, LANES), 0) // 4
    ).astype(F32)
    tile_row = (device // block_cols).astype(F32)
    screen = TILE_COLS * 8.0
    ex = (16.0 * tile_col + 8.0 - screen) - screen * col
    ey = (16.0 * tile_row + 8.0 - rows_pix * 0.5) - screen * scr
    factor = -0.5 * LOG2E / (screen * screen)
    a = factor * c0
    b = (2.0 * factor) * c1
    c = factor * c2
    bx = b * ex
    by = b * ey
    coeffs = [
        a,
        b,
        c,
        2.0 * a * ex + by,
        bx + 2.0 * c * ey,
        (a * ex + by) * ex + c * ey * ey + LOG2E * jnp.log(opacity),
    ]
    rest = [0.0, 0.0, 0.0, 0.0, 0.0, ABSENT]
    lines = []
    pieces = [split(jnp.where(live, x, r), 3) for x, r in zip(coeffs, rest)]
    for part in range(3):
        lines += [pieces[k][part] for k in range(6)]
    tints = [split(feats[6 + k], 3) for k in range(3)]
    tints = [tints[k][part] for part in range(3) for k in range(3)]
    lines += tints * 3 + [feats[6]] + [jnp.zeros((16, LANES), F32)] * 2
    for k in range(KEYS):
        for h in range(2):
            lhs_ref[pl.ds(8 * KEYS * h + k, 8, stride=KEYS), :] = lines[k][8 * h : 8 * h + 8, :]

    one = jnp.ones((8, LANES), F32)
    zero = jnp.zeros((8, LANES), F32)
    spans = [(t, p) for t in range(4) for p in range(2)]

    def place(t, j):
        start = 512 * (j // 16) + 128 * t + 8 * (j % 16)
        return slice(start, start + 8)

    def chunk(t, u):
        return slice(512 * u + 128 * t, 512 * u + 128 * t + 128)

    def half(p):
        return slice(LANES * p, LANES * p + LANES)

    trans = {tp: one for tp in spans}
    image = {tp: [zero] * 3 for tp in spans}
    before, behind, rights, shades = {}, {}, {}, {}
    pad = jnp.zeros((1, 256), F32)
    for u in range(4):
        columns = []
        for t in range(4):
            lines = lhs_ref[KEYS * (4 * t + u) : KEYS * (4 * t + u) + KEYS, :].T
            columns.append(lines)
            left_ref[chunk(t, u), :] = lines.astype(BF16)
        both = jnp.dot(
            left_ref[512 * u : 512 * u + 512, :], basis_ref[...], preferred_element_type=F32
        )
        power_ref[512 * u : 512 * u + 512, :] = both[:, 0:256]
        color_ref[512 * u : 512 * u + 512, :] = both[:, 256:512]
        for j in range(16 * u, 16 * u + 16):
            for t in range(4):
                here = place(t, j)
                at = 8 * (j % 16)
                tint = [jnp.broadcast_to(columns[t][at : at + 8, 45:46], (8, LANES))]
                tint += [color_ref[here, half(k)] for k in range(2)]
                for p in range(2):
                    alpha = jnp.exp2(power_ref[here, half(p)])
                    alpha_ref[here, half(p)] = alpha
                    weight = alpha * trans[t, p]
                    weight_ref[here, half(p)] = weight
                    trans[t, p] = trans[t, p] - weight
                    image[t, p] = [image[t, p][k] + weight * tint[k] for k in range(3)]

    for t in range(4):
        slopes = []
        for p in range(2):
            kept = trans[t, p]
            lead = sublane_shift(kept, 1, 1.0)
            for by_ in (1, 2, 4):
                lead = lead * sublane_shift(lead, by_, 1.0)
            before[t, p] = lead
            slope = []
            for k in range(3):
                shown = jnp.sum(lead * image[t, p][k], axis=0, keepdims=True)
                goal = target_ref[k, :, 256 * t + 128 * p : 256 * t + 128 * p + 128]
                slope.append(2.0 * (shown - goal))
            slopes.append(slope)
            add = sum(slope[k] * image[t, p][k] for k in range(3))
            mul = kept
            for by_ in (1, 2, 4):
                add = add + mul * sublane_shift(add, -by_, 0.0)
                mul = mul * sublane_shift(mul, -by_, 1.0)
            behind[t, p] = sublane_shift(add, -1, 0.0)
        parts = [
            split(jnp.concatenate([slopes[0][k], slopes[1][k]], axis=1), 3) for k in range(3)
        ]
        rows = [pad] * 18
        for part in range(3):
            rows += [parts[k][part] for _ in range(3) for k in range(3)]
        rights[t] = (jnp.concatenate(rows + [pad] * 3, axis=0).astype(BF16))
        nine = [parts[k][part] for part in range(3) for k in range(3)]
        shades[t] = (jnp.concatenate([pad] * 16 + nine + [pad] * 7, axis=0).T.astype(BF16))

    for t in range(4):
        left = jnp.concatenate([left_ref[chunk(t, u), :] for u in range(4)], axis=0)
        rest = jnp.dot(left, rights[t], preferred_element_type=F32)
        for u in range(4):
            power_ref[chunk(t, u), :] = rest[128 * u : 128 * u + 128, :]
    for u in (3, 2, 1, 0):
        for i in range(8 * u + 7, 8 * u - 1, -1):
            for t, p in spans:
                pair = [None, None]
                rest = behind[t, p]
                for o in (1, 0):
                    here = place(t, 2 * i + o)
                    weight = weight_ref[here, half(p)] * before[t, p]
                    shade = power_ref[here, half(p)]
                    alpha = alpha_ref[here, half(p)]
                    gap = shade - rest
                    rest = (1.0 - alpha) * rest + alpha * shade
                    pair[o] = (weight * gap, weight)
                behind[t, p] = rest
                first = place(t, 2 * i).start
                for n, ref in enumerate((slope_ref, shade_ref)):
                    value = jnp.concatenate([pair[0][n], pair[1][n]], axis=0)
                    high = value.astype(BF16)
                    ref[first : first + 16, half(p)] = high
                    ref[first : first + 16, half(2 + p)] = (value - high.astype(F32)).astype(BF16)
        part_ref[512 * u : 512 * u + 512, :] = jnp.dot(
            slope_ref[512 * u : 512 * u + 512, :], moment_ref[...], preferred_element_type=F32
        )
    for t in range(4):
        weights = jnp.concatenate([shade_ref[chunk(t, u), :] for u in range(4)], axis=0)
        shaded = jnp.dot(
            weights, jnp.concatenate([shades[t]] * 2, axis=0), preferred_element_type=F32
        )
        for u in range(4):
            total = part_ref[chunk(t, u), :] + shaded[128 * u : 128 * u + 128, :]
            sums_ref[32 * (4 * t + u) : 32 * (4 * t + u) + 32, :] = total.T

    def summed(k):
        return jnp.concatenate(
            [sums_ref[pl.ds(256 * h + k, 8, stride=32), :] for h in range(2)], axis=0
        )

    mxx, mxy, myy, mx, my, m0 = [summed(k) for k in range(6)]
    sx = ex * m0 + mx
    sy = ey * m0 + my
    sxx = ex * (ex * m0 + 2.0 * mx) + mxx
    sxy = ex * (ey * m0 + my) + ey * mx + mxy
    syy = ey * (ey * m0 + 2.0 * my) + myy
    unit = 1.0 / screen
    grads = [
        (c0 * sx + c1 * sy) * unit,
        (c1 * sx + c2 * sy) * unit,
        (-0.5 * unit * unit) * sxx,
        (-unit * unit) * sxy,
        (-0.5 * unit * unit) * syy,
        m0 / opacity,
    ]
    for k in range(3):
        grads.append(summed(16 + k) + summed(19 + k) + summed(22 + k))
    for f in range(FEATS):
        grads_ref[16 * f : 16 * f + 16, :] = grads[f]

    out = [[None, None] for _ in range(FEATS)]
    for h in range(2):
        total = [jnp.zeros((8, LANES), F32) for _ in range(FEATS)]
        for t in range(4):
            code = inverse_ref[16 * t + 8 * h : 16 * t + 8 * h + 8, :]
            row = code >> 7
            lane = code & 127
            found = [jnp.zeros((8, LANES), F32) for _ in range(FEATS)]
            for u in range(4):
                here = row == u
                for f in range(FEATS):
                    at = 16 * f + 4 * t + u
                    source = grads_ref[pl.ds(at, 8, stride=0), :]
                    found[f] = jnp.where(
                        here, jnp.take_along_axis(source, lane, axis=1, mode="promise_in_bounds"), found[f]
                    )
            total = [x + y for x, y in zip(total, found)]
        for f in range(FEATS):
            out[f][h] = total[f]
    table_to_wire(out, out_ref)


def adam_kernel(
    place_ref,
    own_ref,
    one_ref,
    two_ref,
    three_ref,
    params_ref,
    first_ref,
    second_ref,
    new_params_ref,
    new_first_ref,
    new_second_ref,
    scratch_ref,
    pulled_ref,
    local_ref,
    sems,
):
    for k, ref in enumerate((own_ref, one_ref, two_ref, three_ref)):
        at = pl.multiple_of(168 * ((place_ref[0] - k) & 3), 8)
        pulled_ref[pl.ds(at, 168), :] = ref[...]
    to_dense(params_ref, scratch_ref)
    rows = dense_rows(scratch_ref)
    seen = jnp.zeros((16, LANES), F32)
    cotangents = []
    cams = []
    for v in range(4):
        at = 168 * v
        cotangents.append(
            [pulled_ref[at + 16 * f : at + 16 * f + 16, :] for f in range(FEATS)]
        )
        seen = seen + pulled_ref[at + 144 : at + 160, :]
        cams.append(
            [
                jnp.broadcast_to(pulled_ref[at + 160 : at + 161, k : k + 1], (16, LANES))
                for k in range(12)
            ]
        )

    def leave(n):
        at = (slice(16, ROWS) if n == 0 else slice(0, 16), slice(None))
        return [
            pltpu.make_async_copy(local_ref.at[(m, *at)], ref.at[at], sems.at[n, m])
            for m, ref in enumerate((new_params_ref, new_first_ref, new_second_ref))
        ]

    def keep(f, value):
        for h in range(2):
            scratch_ref[pl.ds(512 * h + f, 8, stride=64), :] = value[8 * h : 8 * h + 8, :]

    def update(a):
        high = min(8, ROWS - 8 * a)
        row = lax.broadcasted_iota(I32, (high, LANES), 0) + 8 * a
        rate = jnp.where(
            row < 6,
            0.01,
            jnp.where(row < 10, 0.005, jnp.where(row < 11, 0.05, jnp.where(row < 14, 0.0025, 0.000125))),
        ).astype(F32) * (1.0 / bias_one)
        for k in range(16):
            at = (slice(8 * a, 8 * a + high), slice(LANES * k, LANES * k + LANES))
            grad = scratch_ref[64 * k + 8 * a : 64 * k + 8 * a + high, :]
            here = jnp.broadcast_to(seen[k : k + 1, :], (high, LANES)) > 0.0
            p, m, s = params_ref[at], first_ref[at], second_ref[at]
            m_new = 0.9 * m + 0.1 * grad
            s_new = 0.999 * s + 0.001 * grad * grad
            stride = rate * m_new / (jnp.sqrt(s_new * (1.0 / bias_two)) + 1e-08)
            local_ref[(0, *at)] = jnp.where(here, p - stride, p)
            local_ref[(1, *at)] = jnp.where(here, m_new, m)
            local_ref[(2, *at)] = jnp.where(here, s_new, s)

    bias_one = 1.0 - 0.9**ADAM_STEP
    bias_two = 1.0 - 0.999**ADAM_STEP

    def colors(means, coefficients):
        values = means + [None] * 8 + coefficients
        return [color_view(values, cam[9:]) for cam in cams]

    def geometry(values):
        basis = shape_basis(values)
        opacity = logistic(values[10])
        return [project_view(values, basis, cam[:9], cam[9:]) + [opacity] for cam in cams]

    _, pull = jax.vjp(colors, rows[:3], rows[11:])
    aimed, tinted = pull([cot[6:] for cot in cotangents])
    for k in range(48):
        keep(11 + k, tinted[k])
    for a in range(2, 8):
        update(a)
    for copy in leave(0):
        copy.start()
    _, pull = jax.vjp(geometry, rows[:11])
    shaped = pull([cot[:6] for cot in cotangents])[0]
    for k in range(11):
        keep(k, shaped[k] + aimed[k] if k < 3 else shaped[k])
    for a in range(2):
        update(a)
    for copy in leave(1):
        copy.start()
    for n in range(2):
        for copy in leave(n):
            copy.wait()


def pixel_constants():
    pixel = np.arange(256)
    x = pixel % 16 - 7.5
    y = pixel // 16 - 7.5
    six = np.stack([x * x, x * y, y * y, x, y, np.ones(256)])
    basis = np.zeros((KEYS, 512), np.float32)
    for part in range(3):
        basis[6 * part : 6 * part + 6, :256] = six
        for k in range(2):
            basis[19 + 3 * part + k, 256 + 128 * k : 384 + 128 * k] = 1.0
    moment = np.zeros((512, 32), np.float32)
    moment[:256, :6] = six.T
    moment[256:, :6] = six.T
    return jnp.asarray(basis, BF16), jnp.asarray(moment, BF16)


VMEM = pl.BlockSpec(memory_space=pltpu.VMEM)
SMEM = pl.BlockSpec(memory_space=pltpu.SMEM)
ANY = pl.BlockSpec(memory_space=pl.ANY)


def call(kernel, outs, ins, scratch, megabytes, cost, space=VMEM):
    flops, moved = cost
    return pl.pallas_call(
        kernel,
        out_shape=outs,
        in_specs=ins,
        out_specs=jax.tree.map(lambda _: space, outs),
        scratch_shapes=scratch,
        compiler_params=pltpu.CompilerParams(vmem_limit_bytes=megabytes << 20),
        cost_estimate=pl.CostEstimate(flops=flops, bytes_accessed=moved, transcendentals=0),
    )


def render(rows_pix):
    vmem = lambda *shape: pltpu.VMEM(shape, F32)
    return call(
        functools.partial(render_kernel, float(rows_pix)),
        jax.ShapeDtypeStruct((192, LANES), F32),
        [SMEM, VMEM, VMEM, VMEM, VMEM, VMEM, VMEM],
        [
            vmem(144, LANES),
            vmem(16 * KEYS, LANES),
            vmem(2048, 256),
            pltpu.VMEM((2048, KEYS), BF16),
            vmem(2048, 256),
            vmem(2048, 256),
            vmem(2048, 256),
            pltpu.VMEM((2048, 512), BF16),
            pltpu.VMEM((2048, 512), BF16),
            vmem(2048, 32),
            vmem(512, LANES),
            vmem(144, LANES),
        ],
        32,
        (100_000_000, 300_000),
    )


def shards(params, first_moment, second_moment, cameras, visible, send_plan, tile_lists, target):
    del visible
    cells = lax.axis_size("cells")
    views = lax.axis_size("views")
    plan = send_plan[0, 0].T
    lists = tile_lists[0]
    tiles = lists.shape[0]
    rows_pix = tiles * cells // TILE_COLS * 16
    f32 = lambda *shape: jax.ShapeDtypeStruct(shape, F32)
    i32 = lambda *shape: jax.ShapeDtypeStruct(shape, I32)
    vmem = lambda *shape: pltpu.VMEM(shape, F32)

    wire = call(
        project_kernel,
        f32(192, LANES),
        [SMEM, VMEM, VMEM],
        [vmem(1024, LANES), vmem(144, LANES), pltpu.VMEM((16, LANES), I32)],
        60,
        (10_000_000, 600_000),
    )(cameras, params, plan)
    arrived = lax.all_to_all(wire.reshape(64, 1, 384), "cells", 0, 0, tiled=True)

    inverse = call(slots_kernel, i32(64, LANES), [SMEM], [], 8, (20_000_000, 50_000))(lists)

    basis, moment = pixel_constants()
    back = render(rows_pix)(
        lax.axis_index("cells").astype(I32).reshape(1),
        arrived.reshape(192, LANES),
        lists,
        inverse,
        jnp.swapaxes(target, 0, 1),
        basis,
        moment,
    )
    returned = lax.all_to_all(back.reshape(64, 1, 384), "cells", 0, 0, tiled=True)

    code, view = call(
        owner_kernel, (i32(16, LANES), f32(8, LANES)), [SMEM, SMEM], [], 8, (20_000_000, 50_000)
    )(cameras, plan)
    own = call(
        pull_kernel, f32(168, LANES), [VMEM, VMEM, VMEM], [vmem(144, LANES)], 8, (1_000_000, 200_000)
    )(returned.reshape(192, LANES), code, view)
    others = [
        lax.ppermute(own, "views", [(i, (i + k) % views) for i in range(views)]) for k in (1, 2, 3)
    ]
    shape = f32(*params.shape)
    return call(
        adam_kernel,
        (shape, shape, shape),
        [SMEM] + [VMEM] * 7,
        [
            vmem(1024, LANES),
            vmem(168 * 4, LANES),
            vmem(3, ROWS, 2048),
            pltpu.SemaphoreType.DMA((2, 3)),
        ],
        24,
        (40_000_000, 3_500_000),
        ANY,
    )(
        lax.axis_index("views").astype(I32).reshape(1),
        own,
        *others,
        params,
        first_moment,
        second_moment,
    )


def solution(mesh):
    in_specs = (
        P(None, "cells"),
        P(None, "cells"),
        P(None, "cells"),
        P("views", None),
        P("views", "cells"),
        P("views", "cells", None, None),
        P("views", "cells", None),
        P("views", None, "cells"),
    )
    out_specs = (P(None, "cells"), P(None, "cells"), P(None, "cells"))
    return jax.shard_map(shards, mesh=mesh, in_specs=in_specs, out_specs=out_specs, check_vma=False)
```
